32 devices in a mesh: replica: 8 (over z, core), fsdp: 4 (over y, x).
Axes of the slice: x: 2, y: 2, z: 4, core: 2. Of those that a mesh axis runs over, the one named last changes fastest.
Arguments:
- tokens: bfloat16 [2, 2048, 2048], P(None, ('replica', 'fsdp')), may hold values from -6 to 6
- cotangent: bfloat16 [2, 2048, 2048], P(None, ('replica', 'fsdp'))
- parents: int32 [2, 8, 13], P(None, 'replica'), may hold values from 0 to 11, as said below
- lengths: int32 [2, 8, 13], P(None, 'replica'), may hold values from 1 to 128, 256 in all within a row
- qkv_weight: bfloat16 [3, 2048, 2048], P(None, None, 'fsdp')
- out_weight: bfloat16 [2048, 2048], P('fsdp'), may hold values from -0.125 to 0.125
- gate_up_weight: bfloat16 [2, 2048, 8192], P(None, None, 'fsdp'), may hold values from -0.125 to 0.125
- down_weight: bfloat16 [8192, 2048], P('fsdp'), may hold values from -0.0625 to 0.0625
- qk_gain: float32 [2, 2048], P(None, 'fsdp'), may hold values from 1.1 to 1.9
- post_gain: float32 [2, 2048], replicated, may hold values from 0.5 to 1.5
Outputs:
- output: float32 [2, 2048, 2048], P(None, ('replica', 'fsdp'))
- input_grad: float32 [2, 2048, 2048], P(None, ('replica', 'fsdp'))
- qkv_grad: float32 [3, 2048, 2048], P(None, 'replica', 'fsdp')
- out_grad: float32 [2048, 2048], P('fsdp', 'replica')
- gate_up_grad: float32 [2, 2048, 8192], P(None, 'replica', 'fsdp')
- down_grad: float32 [8192, 2048], P('fsdp', 'replica')
- qk_gain_grad: float32 [2, 2048], P(None, 'fsdp')
- post_gain_grad: float32 [2, 2048], P(None, 'fsdp')
The draws below stay inside these ranges and needn't reach their ends.
Inputs may be any that keep to these rules, and one draw needn't show every extreme that they name: parents[..., 0] = 0 and parents[..., s] < s for every later segment s, so a tree's root is segment 0. The lengths of one tree add up to 256, and the largest is exactly 128.
All inputs are finite; a program needn't handle non-finite values.
Results may differ from the reference program's by a relative error of at most 0.02.
Values may be sent and summed in bfloat16 or wider, within the bound.
No kernel may reach another device: no remote copies, remote signals or barrier semaphores. Data moves between devices by JAX's collectives and lax.ppermute only.
A program may use at most 256 MiB of HBM per device.

```python
import math
import jax
import jax.numpy as jnp
import numpy as np
from jax import lax

D = 2048
H = 16
HD = 128
FF = 8192
MB = 2
SEGS = 13
GROUP_TOK = 256
TOKENS = 2048
N_REPLICA = 8


def draw_qkv_weight(key, part):
    base = jax.random.normal(key, (3, D, D), jnp.float32)
    column = jnp.arange(D, dtype=jnp.float32) / (D - 1)
    rising = jnp.where(jnp.arange(3)[:, None] < 2, (3.0 ** (0.55 * column))[None, :], 1.0)
    return (base * D ** (-0.5) * rising[:, None, :]).astype(jnp.bfloat16)


def draw_cotangent(key, part):
    first = jax.random.fold_in(key, 11)
    second = jax.random.fold_in(key, 12)
    row_place = jnp.arange(TOKENS, dtype=jnp.float32) / (TOKENS - 1)
    jitter = jnp.exp(jax.random.uniform(second, (MB, TOKENS, 1), jnp.float32, -0.4, 0.4))
    base = jax.random.normal(first, (MB, TOKENS, D), jnp.float32)
    return (base * 0.6 * (3.0 ** row_place)[None, :, None] * jitter).astype(jnp.bfloat16)


def draw_parents(key, part):
    random_bits = jax.random.randint(key, (MB, N_REPLICA, SEGS), 0, 1048576)
    labels = jnp.arange(SEGS, dtype=jnp.int32)
    return (random_bits % jnp.maximum(labels, 1)[None, None, :]).astype(jnp.int32)


def block_scale(own_key, extent, cuts, smallest, top_value):
    loudness = 1.0
    for dim, parts in cuts:
        steps = jax.random.uniform(jax.random.fold_in(jax.random.fold_in(own_key, 6), dim), (parts,), jnp.float32, smallest / len(cuts), top_value / len(cuts))
        loudness = loudness * jnp.repeat(jnp.exp(steps), extent[dim] // parts).reshape((-1,) + (1,) * (len(extent) - 1 - dim))
    return loudness


def profile(amount, total, bound, skew):
    portions = [(1 << 20) // math.isqrt(rank ** skew) + 1 for rank in range(2, amount + 1)]
    spare, holding = total - bound - (amount - 1), [1] * (amount - 1)
    while spare > 0:
        movable = [i for i in range(amount - 1) if holding[i] < bound]
        whole, left = sum([portions[i] for i in movable]), spare
        for i in movable:
            addition = min(bound - holding[i], max(1, left * portions[i] // whole), spare)
            holding[i] = holding[i] + addition
            spare = spare - addition
    return np.array([bound] + holding)


def uneven(key, amount, total, reach, lean):
    if amount == 2:
        one = jax.random.randint(key, (), max(1, total - reach), min(reach, total - 1) + 1)
        return jnp.stack([one, total - one])
    tallies = jnp.asarray(profile(amount, total, reach, lean), jnp.int32)
    pairs = (amount - 1) // 2
    source_of, sink = tallies[1:1 + 2 * pairs:2], tallies[2:2 + 2 * pairs:2]
    room = jnp.minimum(source_of - 1, reach - sink)
    passed = jax.random.randint(jax.random.fold_in(key, 1), (pairs,), 0, 1 << 20) % (room + 1)
    tallies = tallies.at[1:1 + 2 * pairs:2].set(source_of - passed).at[2:2 + 2 * pairs:2].set(sink + passed)
    return tallies[jax.random.permutation(jax.random.fold_in(key, 2), amount)]


def normal_values(own_key, dims, spread, reach, pieces=(), held_as=jnp.bfloat16):
    factor_of = block_scale(own_key, dims, pieces, -0.22, 0.18) if pieces else 1.0
    array = jax.random.normal(own_key, dims, jnp.float32) * spread * factor_of
    return jnp.minimum(jnp.maximum(array, -reach), reach).astype(held_as)


def setup_inputs(seed: int = 0) -> dict:
    splits = jax.random.split(jax.random.key(seed), 11)
    return {
        "tokens": normal_values(splits[0], (MB, TOKENS, D), 1.0, 6.0, ((1, 32),)),
        "cotangent": draw_cotangent(jax.random.fold_in(splits[10], 71), 0),
        "parents": draw_parents(jax.random.fold_in(splits[10], 71), 0),
        "lengths": jax.vmap(lambda own: uneven(own, SEGS, GROUP_TOK, GROUP_TOK // 2, 2))(jax.random.split(splits[3], MB * N_REPLICA)).reshape((MB, N_REPLICA, SEGS)).astype(jnp.int32),
        "qkv_weight": draw_qkv_weight(jax.random.fold_in(splits[10], 71), 0),
        "out_weight": normal_values(splits[5], (D, D), D ** -0.5, 0.125, ((0, 4),)),
        "gate_up_weight": normal_values(splits[6], (2, D, FF), D ** -0.5, 0.125, ((2, 4),)),
        "down_weight": normal_values(splits[7], (FF, D), FF ** -0.5, 0.0625, ((0, 4),)),
        "qk_gain": jnp.clip(1.1 + 0.79999995 * jax.random.uniform(splits[8], (2, D), jnp.float32) ** block_scale(splits[8], (2, D), ((1, 4),), -0.2, 0.2), 1.1, 1.9),
        "post_gain": jnp.clip(1.0 + 0.1 * jax.random.normal(splits[9], (2, D), jnp.float32), 0.5, 1.5),
    }


EPSILON = 1e-06
ROPE_BASE = 500000.0

@jax.custom_vjp
def low(v):
    return lax.optimization_barrier(v.astype(jnp.bfloat16)).astype(jnp.float32)

@jax.custom_vjp
def low_back(v):
    return v

def low_keep(v):
    return (low(v), None)

def low_pass(kept, grad):
    return (grad,)

def back_keep(v):
    return (v, None)

def back_low(kept, grad):
    return (low(grad),)
low.defvjp(low_keep, low_pass)
low_back.defvjp(back_keep, back_low)

def tree_layout(parent_row, length_row, group_rows):
    segments = parent_row.shape[0]
    ends = jnp.cumsum(length_row).astype(jnp.int32)
    starts = (ends - length_row).astype(jnp.int32)
    places = jnp.arange(group_rows, dtype=jnp.int32)
    labels = jnp.arange(segments, dtype=jnp.int32)
    segment_of = lax.optimization_barrier(jnp.sum((places[:, None] >= ends[None, :]).astype(jnp.int32), axis=1)).astype(jnp.int32)
    member = segment_of[:, None] == labels[None, :]
    walker = labels
    ancestry = walker[:, None] == labels[None, :]
    for depth_step in range(segments - 1):
        walker = lax.optimization_barrier(jnp.sum(jnp.where(walker[:, None] == labels[None, :], parent_row[None, :], 0), axis=1)).astype(jnp.int32)
        ancestry = ancestry | (walker[:, None] == labels[None, :])
    above = (lax.optimization_barrier(jnp.sum(jnp.where(ancestry, length_row[None, :], 0), axis=1)) - length_row).astype(jnp.int32)
    moved = lax.optimization_barrier(jnp.sum(jnp.where(member, (above - starts)[None, :], 0), axis=1)).astype(jnp.int32)
    position = (places + moved).astype(jnp.float32)
    return (segment_of, ancestry, position)

def rope_tables(position, head_dim):
    freq = ROPE_BASE ** (-jnp.arange(0, head_dim, 2, dtype=jnp.float32) / head_dim)
    angle = position[:, None] * freq[None, :]
    angle = jnp.concatenate([angle, angle], axis=1)
    return (jnp.cos(angle)[:, None, :], jnp.sin(angle)[:, None, :])

def rotate(field, cos_t, sin_t):
    half = field.shape[-1] // 2
    turned = jnp.concatenate([-field[..., half:], field[..., :half]], axis=-1)
    return field * cos_t + turned * sin_t

def rms_scale(field):
    return lax.rsqrt(lax.optimization_barrier(jnp.mean(field * field, axis=-1, keepdims=True)) + EPSILON)

def forward(tokens_f, qkv_w, out_w, gate_up_w, down_w, qk_g, post_g, cos_t, sin_t, allowed):
    highest = lax.Precision.HIGHEST
    group_rows = tokens_f.shape[0]
    projected = low_back(jnp.einsum('td,nde->tne', low(tokens_f), qkv_w, precision=highest))
    query_raw = projected[:, 0]
    key_raw = projected[:, 1]
    queries = low(rotate((query_raw * rms_scale(query_raw) * qk_g[0]).reshape(group_rows, H, HD), cos_t, sin_t))
    lookups = low(rotate((key_raw * rms_scale(key_raw) * qk_g[1]).reshape(group_rows, H, HD), cos_t, sin_t))
    contents = low(projected[:, 2].reshape(group_rows, H, HD))
    scores = low_back(jnp.einsum('qhd,khd->hqk', queries, lookups, precision=highest) * HD ** (-0.5))
    masked = jnp.where(allowed[None], scores, -1e+30)
    prob_rows = low(jax.nn.softmax(masked, axis=-1))
    context = low_back(low(jnp.einsum('hqk,khd->qhd', prob_rows, contents, precision=highest)))
    attn = low_back(jnp.dot(context.reshape(group_rows, D), out_w, precision=highest))
    hidden = tokens_f + attn * rms_scale(attn) * post_g[0]
    gate_up = low_back(jnp.einsum('td,ndf->tnf', low(hidden), gate_up_w, precision=highest))
    swiglu = low(jax.nn.silu(gate_up[:, 0]) * gate_up[:, 1])
    mlp = low_back(jnp.dot(swiglu, down_w, precision=highest))
    return hidden + mlp * rms_scale(mlp) * post_g[1]

def reference(tokens, cotangent, parents, lengths, qkv_weight, out_weight, gate_up_weight, down_weight, qk_gain, post_gain):
    packs = MB * N_REPLICA
    token_packs = tokens.reshape(packs, GROUP_TOK, D)
    grad_packs = cotangent.reshape(packs, GROUP_TOK, D)
    parent_packs = parents.reshape(packs, SEGS)
    length_packs = lengths.reshape(packs, SEGS)
    weights = (qkv_weight.astype(jnp.float32), out_weight.astype(jnp.float32), gate_up_weight.astype(jnp.float32), down_weight.astype(jnp.float32), qk_gain.astype(jnp.float32), post_gain.astype(jnp.float32))
    places = jnp.arange(GROUP_TOK, dtype=jnp.int32)

    def one_pack(running, items):
        token_rows, grad_rows, parent_row, length_row = items
        segment_of, ancestry, position = tree_layout(parent_row, length_row, GROUP_TOK)
        row_anc = ancestry[segment_of]
        allowed = row_anc[:, segment_of] & (places[None, :] <= places[:, None])
        cos_t, sin_t = rope_tables(position, HD)

        def layer(tokens_f, qkv_w, out_w, gate_up_w, down_w, qk_g, post_g):
            return forward(tokens_f, qkv_w, out_w, gate_up_w, down_w, qk_g, post_g, cos_t, sin_t, allowed)
        result, pull = jax.vjp(layer, token_rows.astype(jnp.float32), *weights)
        grads = pull(grad_rows.astype(jnp.float32))
        running = tuple((held + added for held, added in zip(running, grads[1:])))
        return (running, (result, grads[0]))
    start_sums = tuple((jnp.zeros(w.shape, jnp.float32) for w in weights))
    sums, (results, input_rows) = lax.scan(one_pack, start_sums, (token_packs, grad_packs, parent_packs, length_packs))
    output = results.reshape(MB, TOKENS, D)
    input_grad = input_rows.reshape(MB, TOKENS, D)
    return (output, input_grad, sums[0], sums[1], sums[2], sums[3], sums[4], sums[5])
```

```python
import jax
import jax.numpy as jnp
from jax import lax
from jax.sharding import PartitionSpec as P

HD = 128


EPSILON = 1e-06
ROPE_BASE = 500000.0


def exchange(value, axis, flip):
    size = lax.axis_size(axis)
    return lax.ppermute(value, axis, [(i, i ^ flip) for i in range(size)])


def gather_rows(rows):
    size = lax.axis_size("fsdp")
    return jnp.concatenate(
        [rows] + [exchange(rows, "fsdp", flip) for flip in range(1, size)], axis=0
    )


def scatter_rows(partial):
    size = lax.axis_size("fsdp")
    blocks = jnp.split(partial, size, axis=0)
    total = blocks[0].astype(jnp.float32)
    for flip in range(1, size):
        total = total + exchange(blocks[flip], "fsdp", flip).astype(jnp.float32)
    return total


def sum_small(value, axis):
    size = lax.axis_size(axis)
    flip = 1
    while flip < size:
        value = value + exchange(value, axis, flip)
        flip *= 2
    return value


def sum_row_values(value):
    size = lax.axis_size("fsdp")
    kinds, rows = value.shape
    total = value
    for flip in range(1, size):
        blocks = exchange(value, "fsdp", flip).reshape(kinds, size, rows // size)
        total = total + jnp.concatenate(
            [blocks[:, block ^ flip] for block in range(size)], axis=1
        )
    return total


def true_rows(tok_dev):
    size = lax.axis_size("fsdp")
    block = jnp.arange(size, dtype=jnp.int32) ^ lax.axis_index("fsdp")
    return (block[:, None] * tok_dev + jnp.arange(tok_dev, dtype=jnp.int32)[None, :]).reshape(-1)


def tree_layout(parent_row, length_row, places):
    segments = parent_row.shape[0]
    labels = jnp.arange(segments, dtype=jnp.int32)
    before = labels[:, None] >= labels[None, :]
    ends = jnp.sum(jnp.where(before, length_row[None, :], 0), axis=1)
    starts = ends - length_row
    segment_of = jnp.sum((places[:, None] >= ends[None, :]).astype(jnp.int32), axis=1)
    member = segment_of[:, None] == labels[None, :]
    reach = ((labels[:, None] == labels[None, :]) | (parent_row[:, None] == labels[None, :])).astype(
        jnp.float32
    )
    steps = 1
    while steps < segments - 1:
        reach = (jnp.dot(reach, reach) > 0.5).astype(jnp.float32)
        steps *= 2
    ancestry = reach > 0.5
    above = jnp.sum(jnp.where(ancestry, length_row[None, :], 0), axis=1) - length_row
    moved = jnp.sum(jnp.where(member, (above - starts)[None, :], 0), axis=1)
    position = (places + moved).astype(jnp.float32)
    member_f = member.astype(jnp.float32)
    near = jnp.dot(jnp.dot(member_f, reach), member_f.T) > 0.5
    visible = near & (places[None, :] <= places[:, None])
    return (visible, position)


def rope_tables(position, head_dim):
    freq = ROPE_BASE ** (-jnp.arange(0, head_dim, 2, dtype=jnp.float32) / head_dim)
    angle = position[:, None] * freq[None, :]
    angle = jnp.concatenate([angle, angle], axis=1)
    return (jnp.cos(angle)[:, None, :], jnp.sin(angle)[:, None, :])


def rotate(field, cos_t, sin_t):
    half = field.shape[-1] // 2
    turned = jnp.concatenate([-field[..., half:], field[..., :half]], axis=-1)
    return field * cos_t + turned * sin_t


def unrotate(grad_field, cos_t, sin_t):
    half = grad_field.shape[-1] // 2
    sined = grad_field * sin_t
    turned = jnp.concatenate([sined[..., half:], -sined[..., :half]], axis=-1)
    return grad_field * cos_t + turned


def block_scores(query_block, lookups, visible, score_scale):
    raw = (
        jnp.einsum("bhd,khd->hbk", query_block, lookups, preferred_element_type=jnp.float32)
        * score_scale
    )
    return jnp.where(visible[None], raw, -1e30)


def norm_back(field, inv_rms, gain, upstream, model_width, partner_sum):
    weighted = upstream * gain
    return inv_rms[:, None] * weighted - field * (inv_rms**3 * partner_sum / model_width)[:, None]


def micro_step(
    x_rows,
    grad_rows,
    parent_row,
    length_row,
    qkv_weight,
    out_weight,
    gate_up_weight,
    down_weight,
    qk_gain,
    post_gain,
):
    tok_dev, model_width = x_rows.shape
    group_rows = tok_dev * lax.axis_size("fsdp")
    local_width = qkv_weight.shape[2]
    local_heads = local_width // HD
    score_scale = HD ** (-0.5)
    x_full = gather_rows(x_rows)
    visible, position = tree_layout(parent_row, length_row, true_rows(tok_dev))
    cos_t, sin_t = rope_tables(position, HD)
    projected = jnp.einsum("td,nde->tne", x_full, qkv_weight, preferred_element_type=jnp.float32)
    query_raw = projected[:, 0]
    key_raw = projected[:, 1]
    squares = sum_row_values(
        jnp.stack([jnp.sum(query_raw * query_raw, axis=1), jnp.sum(key_raw * key_raw, axis=1)])
    )
    inv_rms = lax.rsqrt(squares / model_width + EPSILON)
    queries = rotate(
        (query_raw * inv_rms[0][:, None] * qk_gain[0]).reshape(group_rows, local_heads, HD),
        cos_t,
        sin_t,
    ).astype(jnp.bfloat16)
    lookups = rotate(
        (key_raw * inv_rms[1][:, None] * qk_gain[1]).reshape(group_rows, local_heads, HD),
        cos_t,
        sin_t,
    ).astype(jnp.bfloat16)
    contents = projected[:, 2].reshape(group_rows, local_heads, HD).astype(jnp.bfloat16)
    scores = block_scores(queries, lookups, visible, score_scale)
    row_max = jnp.max(scores, axis=2)
    raw_weights = jnp.exp(scores - row_max[:, :, None])
    row_total = jnp.sum(raw_weights, axis=2)
    prob_rows = (raw_weights / row_total[:, :, None]).astype(jnp.bfloat16)
    context_parts = jnp.einsum(
        "hbk,khd->bhd", prob_rows, contents, preferred_element_type=jnp.float32
    ).astype(jnp.bfloat16)
    total_parts = row_max + jnp.log(row_total)
    context = context_parts.reshape(group_rows, local_width)
    attn = scatter_rows(jnp.dot(context, out_weight, preferred_element_type=jnp.bfloat16))
    rms_attn = lax.rsqrt(jnp.mean(attn * attn, axis=1) + EPSILON)
    hidden = x_rows.astype(jnp.float32) + attn * rms_attn[:, None] * post_gain[0]
    hidden_full = gather_rows(hidden.astype(jnp.bfloat16))
    gate_up = jnp.einsum(
        "td,ndf->tnf", hidden_full, gate_up_weight, preferred_element_type=jnp.float32
    )
    gate_pre = gate_up[:, 0]
    up_pre = gate_up[:, 1]
    sigmoid_gate = jax.nn.sigmoid(gate_pre)
    silu_gate = gate_pre * sigmoid_gate
    swiglu = (silu_gate * up_pre).astype(jnp.bfloat16)
    mlp = scatter_rows(jnp.dot(swiglu, down_weight, preferred_element_type=jnp.bfloat16))
    rms_mlp = lax.rsqrt(jnp.mean(mlp * mlp, axis=1) + EPSILON)
    out_rows = hidden + mlp * rms_mlp[:, None] * post_gain[1]
    upstream = grad_rows.astype(jnp.float32)
    gain_mlp = jnp.sum(upstream * mlp * rms_mlp[:, None], axis=0)
    d_mlp = norm_back(
        mlp,
        rms_mlp,
        post_gain[1],
        upstream,
        model_width,
        jnp.sum(mlp * post_gain[1] * upstream, axis=1),
    ).astype(jnp.bfloat16)
    d_mlp_full = gather_rows(d_mlp)
    d_swiglu = jnp.einsum("td,fd->tf", d_mlp_full, down_weight, preferred_element_type=jnp.float32)
    d_gate = d_swiglu * up_pre * sigmoid_gate * (1.0 + gate_pre * (1.0 - sigmoid_gate))
    d_up = d_swiglu * silu_gate
    d_gate_up = jnp.stack([d_gate, d_up], axis=1).astype(jnp.bfloat16)
    d_hidden = upstream + scatter_rows(
        jnp.einsum("tnf,ndf->td", d_gate_up, gate_up_weight, preferred_element_type=jnp.bfloat16)
    )
    gain_attn = jnp.sum(d_hidden * attn * rms_attn[:, None], axis=0)
    d_attn = norm_back(
        attn,
        rms_attn,
        post_gain[0],
        d_hidden,
        model_width,
        jnp.sum(attn * post_gain[0] * d_hidden, axis=1),
    ).astype(jnp.bfloat16)
    d_attn_full = gather_rows(d_attn)
    d_context = jnp.einsum("td,cd->tc", d_attn_full, out_weight, preferred_element_type=jnp.float32)
    d_context_b = d_context.astype(jnp.bfloat16).reshape(group_rows, local_heads, HD)
    scores = block_scores(queries, lookups, visible, score_scale)
    prob_f = jnp.exp(scores - total_parts[:, :, None])
    prob_rows = prob_f.astype(jnp.bfloat16)
    d_prob = jnp.einsum("bhd,khd->hbk", d_context_b, contents, preferred_element_type=jnp.float32)
    row_delta = jnp.sum(d_prob * prob_f, axis=2)
    d_scores = (prob_f * (d_prob - row_delta[:, :, None])).astype(jnp.bfloat16)
    query_grads = (
        jnp.einsum("hbk,khd->bhd", d_scores, lookups, preferred_element_type=jnp.float32)
        * score_scale
    )
    key_grad = (
        jnp.einsum("hbk,bhd->khd", d_scores, queries, preferred_element_type=jnp.float32)
        * score_scale
    )
    value_grad = jnp.einsum(
        "hbk,bhd->khd", prob_rows, d_context_b, preferred_element_type=jnp.float32
    )
    query_norm_grad = unrotate(query_grads, cos_t, sin_t).reshape(group_rows, local_width)
    key_norm_grad = unrotate(key_grad, cos_t, sin_t).reshape(group_rows, local_width)
    gain_query = jnp.sum(query_norm_grad * query_raw * inv_rms[0][:, None], axis=0)
    gain_key = jnp.sum(key_norm_grad * key_raw * inv_rms[1][:, None], axis=0)
    feature_sums = sum_row_values(
        jnp.stack(
            [
                jnp.sum(query_raw * qk_gain[0] * query_norm_grad, axis=1),
                jnp.sum(key_raw * qk_gain[1] * key_norm_grad, axis=1),
            ]
        )
    )
    d_query_raw = norm_back(
        query_raw, inv_rms[0], qk_gain[0], query_norm_grad, model_width, feature_sums[0]
    )
    d_key_raw = norm_back(
        key_raw, inv_rms[1], qk_gain[1], key_norm_grad, model_width, feature_sums[1]
    )
    d_projected = jnp.stack(
        [d_query_raw, d_key_raw, value_grad.reshape(group_rows, local_width)], axis=1
    ).astype(jnp.bfloat16)
    input_rows = d_hidden + scatter_rows(
        jnp.einsum("tne,nde->td", d_projected, qkv_weight, preferred_element_type=jnp.bfloat16)
    )
    saved = (
        x_full,
        d_projected,
        context,
        d_attn_full,
        hidden_full,
        d_gate_up,
        swiglu,
        d_mlp_full,
    )
    return (
        out_rows,
        input_rows,
        saved,
        jnp.stack([gain_attn, gain_mlp]),
        jnp.stack([gain_query, gain_key]),
    )


def to_owners(grad, dim):
    return lax.psum_scatter(grad, "replica", scatter_dimension=dim, tiled=True).astype(jnp.float32)


def weight_grads(saved):
    merged = [jnp.concatenate(parts, axis=0) for parts in zip(*saved)]
    x_full, d_projected, context, d_attn, hidden, d_gate_up, swiglu, d_mlp = merged
    kind = jnp.bfloat16
    down = to_owners(jnp.einsum("tf,td->fd", swiglu, d_mlp, preferred_element_type=kind), 1)
    gate_up = to_owners(jnp.einsum("td,tnf->ndf", hidden, d_gate_up, preferred_element_type=kind), 1)
    out = to_owners(jnp.einsum("tc,td->cd", context, d_attn, preferred_element_type=kind), 1)
    qkv = to_owners(jnp.einsum("td,tne->nde", x_full, d_projected, preferred_element_type=kind), 1)
    return (qkv, out, gate_up, down)


def on_device(
    tokens,
    cotangent,
    parents,
    lengths,
    qkv_weight,
    out_weight,
    gate_up_weight,
    down_weight,
    qk_gain,
    post_gain,
):
    micro, tok_dev, model_width = tokens.shape
    local_width = qkv_weight.shape[2]
    outputs = []
    input_grads = []
    saved = []
    gains = []
    for micro_idx in range(micro):
        out_rows, input_rows, kept, gain_add, query_key_add = micro_step(
            tokens[micro_idx],
            cotangent[micro_idx],
            parents[micro_idx, 0],
            lengths[micro_idx, 0],
            qkv_weight,
            out_weight,
            gate_up_weight,
            down_weight,
            qk_gain,
            post_gain,
        )
        outputs.append(out_rows)
        input_grads.append(input_rows)
        saved.append(kept)
        gains.append((gain_add, query_key_add))
    grads = weight_grads(saved)
    gain_rows = sum(gain for gain, _ in gains)
    query_key_rows = sum(gain for _, gain in gains)
    size = lax.axis_size("fsdp")
    me = lax.axis_index("fsdp")
    split = gain_rows.reshape(2, size, local_width)
    post_rows = lax.dynamic_index_in_dim(split, me, 1, keepdims=False)
    for flip in range(1, size):
        sent = lax.dynamic_index_in_dim(split, me ^ flip, 1, keepdims=False)
        post_rows = post_rows + exchange(sent, "fsdp", flip)
    sums = sum_small(jnp.concatenate([query_key_rows, post_rows], axis=0), "replica")
    return (
        jnp.stack(outputs),
        jnp.stack(input_grads),
        grads[0],
        grads[1],
        grads[2],
        grads[3],
        sums[:2],
        sums[2:],
    )


def solution(mesh):
    in_specs = (
        P(None, ("replica", "fsdp"), None),
        P(None, ("replica", "fsdp"), None),
        P(None, "replica", None),
        P(None, "replica", None),
        P(None, None, "fsdp"),
        P("fsdp", None),
        P(None, None, "fsdp"),
        P("fsdp", None),
        P(None, "fsdp"),
        P(),
    )
    out_specs = (
        P(None, ("replica", "fsdp"), None),
        P(None, ("replica", "fsdp"), None),
        P(None, "replica", "fsdp"),
        P("fsdp", "replica"),
        P(None, "replica", "fsdp"),
        P("fsdp", "replica"),
        P(None, "fsdp"),
        P(None, "fsdp"),
    )
    return jax.shard_map(
        on_device, mesh=mesh, in_specs=in_specs, out_specs=out_specs, check_vma=False
    )
```

```python
import jax
import jax.numpy as jnp
from jax import lax
from jax.experimental import pallas as pl
from jax.experimental.pallas import tpu as pltpu
from jax.sharding import PartitionSpec as P

HD = 128


EPSILON = 1e-06
ROPE_BASE = 500000.0


def exchange(value, axis, flip):
    size = lax.axis_size(axis)
    return lax.ppermute(value, axis, [(i, i ^ flip) for i in range(size)])


def gather_rows(rows):
    size = lax.axis_size("fsdp")
    return jnp.concatenate(
        [rows] + [exchange(rows, "fsdp", flip) for flip in range(1, size)], axis=0
    )


def scatter_rows(partial):
    size = lax.axis_size("fsdp")
    blocks = jnp.split(partial, size, axis=0)
    total = blocks[0].astype(jnp.float32)
    for flip in range(1, size):
        total = total + exchange(blocks[flip], "fsdp", flip).astype(jnp.float32)
    return total


def sum_small(value, axis):
    size = lax.axis_size(axis)
    flip = 1
    while flip < size:
        value = value + exchange(value, axis, flip)
        flip *= 2
    return value


def sum_row_values(value):
    size = lax.axis_size("fsdp")
    kinds, rows = value.shape
    total = value
    for flip in range(1, size):
        blocks = exchange(value, "fsdp", flip).reshape(kinds, size, rows // size)
        total = total + jnp.concatenate(
            [blocks[:, block ^ flip] for block in range(size)], axis=1
        )
    return total


def true_rows(tok_dev):
    size = lax.axis_size("fsdp")
    block = jnp.arange(size, dtype=jnp.int32) ^ lax.axis_index("fsdp")
    return (block[:, None] * tok_dev + jnp.arange(tok_dev, dtype=jnp.int32)[None, :]).reshape(-1)


def tree_layout(parent_row, length_row, places):
    segments = parent_row.shape[0]
    labels = jnp.arange(segments, dtype=jnp.int32)
    before = labels[:, None] >= labels[None, :]
    ends = jnp.sum(jnp.where(before, length_row[None, :], 0), axis=1)
    starts = ends - length_row
    segment_of = jnp.sum((places[:, None] >= ends[None, :]).astype(jnp.int32), axis=1)
    member = segment_of[:, None] == labels[None, :]
    reach = ((labels[:, None] == labels[None, :]) | (parent_row[:, None] == labels[None, :])).astype(
        jnp.float32
    )
    steps = 1
    while steps < segments - 1:
        reach = (jnp.dot(reach, reach) > 0.5).astype(jnp.float32)
        steps *= 2
    ancestry = reach > 0.5
    above = jnp.sum(jnp.where(ancestry, length_row[None, :], 0), axis=1) - length_row
    moved = jnp.sum(jnp.where(member, (above - starts)[None, :], 0), axis=1)
    position = (places + moved).astype(jnp.float32)
    member_f = member.astype(jnp.float32)
    near = jnp.dot(jnp.dot(member_f, reach), member_f.T) > 0.5
    visible = near & (places[None, :] <= places[:, None])
    return (visible, position)


def rope_tables(position, head_dim):
    freq = ROPE_BASE ** (-jnp.arange(0, head_dim, 2, dtype=jnp.float32) / head_dim)
    angle = position[:, None] * freq[None, :]
    angle = jnp.concatenate([angle, angle], axis=1)
    return (jnp.cos(angle)[:, None, :], jnp.sin(angle)[:, None, :])


def rotate(field, cos_t, sin_t):
    half = field.shape[-1] // 2
    turned = jnp.concatenate([-field[..., half:], field[..., :half]], axis=-1)
    return field * cos_t + turned * sin_t


def unrotate(grad_field, cos_t, sin_t):
    half = grad_field.shape[-1] // 2
    sined = grad_field * sin_t
    turned = jnp.concatenate([sined[..., half:], -sined[..., :half]], axis=-1)
    return grad_field * cos_t + turned


def block_scores(query_block, lookups, visible, score_scale):
    raw = (
        jnp.einsum("bhd,khd->hbk", query_block, lookups, preferred_element_type=jnp.float32)
        * score_scale
    )
    return jnp.where(visible[None], raw, -1e30)


def norm_back(field, inv_rms, gain, upstream, model_width, partner_sum):
    weighted = upstream * gain
    return inv_rms[:, None] * weighted - field * (inv_rms**3 * partner_sum / model_width)[:, None]


def micro_step(
    x_rows,
    grad_rows,
    parent_row,
    length_row,
    qkv_weight,
    out_weight,
    gate_up_weight,
    down_weight,
    qk_gain,
    post_gain,
):
    tok_dev, model_width = x_rows.shape
    group_rows = tok_dev * lax.axis_size("fsdp")
    local_width = qkv_weight.shape[2]
    local_heads = local_width // HD
    score_scale = HD ** (-0.5)
    x_full = gather_rows(x_rows)
    visible, position = tree_layout(parent_row, length_row, true_rows(tok_dev))
    cos_t, sin_t = rope_tables(position, HD)
    projected = jnp.einsum("td,nde->tne", x_full, qkv_weight, preferred_element_type=jnp.float32)
    query_raw = projected[:, 0]
    key_raw = projected[:, 1]
    squares = sum_row_values(
        jnp.stack([jnp.sum(query_raw * query_raw, axis=1), jnp.sum(key_raw * key_raw, axis=1)])
    )
    inv_rms = lax.rsqrt(squares / model_width + EPSILON)
    queries = rotate(
        (query_raw * inv_rms[0][:, None] * qk_gain[0]).reshape(group_rows, local_heads, HD),
        cos_t,
        sin_t,
    ).astype(jnp.bfloat16)
    lookups = rotate(
        (key_raw * inv_rms[1][:, None] * qk_gain[1]).reshape(group_rows, local_heads, HD),
        cos_t,
        sin_t,
    ).astype(jnp.bfloat16)
    contents = projected[:, 2].reshape(group_rows, local_heads, HD).astype(jnp.bfloat16)
    scores = block_scores(queries, lookups, visible, score_scale)
    row_max = jnp.max(scores, axis=2)
    raw_weights = jnp.exp(scores - row_max[:, :, None])
    row_total = jnp.sum(raw_weights, axis=2)
    prob_rows = (raw_weights / row_total[:, :, None]).astype(jnp.bfloat16)
    context_parts = jnp.einsum(
        "hbk,khd->bhd", prob_rows, contents, preferred_element_type=jnp.float32
    ).astype(jnp.bfloat16)
    total_parts = row_max + jnp.log(row_total)
    context = context_parts.reshape(group_rows, local_width)
    attn = scatter_rows(jnp.dot(context, out_weight, preferred_element_type=jnp.bfloat16))
    rms_attn = lax.rsqrt(jnp.mean(attn * attn, axis=1) + EPSILON)
    hidden = x_rows.astype(jnp.float32) + attn * rms_attn[:, None] * post_gain[0]
    hidden_full = gather_rows(hidden.astype(jnp.bfloat16))
    gate_up = jnp.einsum(
        "td,ndf->tnf", hidden_full, gate_up_weight, preferred_element_type=jnp.float32
    )
    gate_pre = gate_up[:, 0]
    up_pre = gate_up[:, 1]
    sigmoid_gate = jax.nn.sigmoid(gate_pre)
    silu_gate = gate_pre * sigmoid_gate
    swiglu = (silu_gate * up_pre).astype(jnp.bfloat16)
    mlp = scatter_rows(jnp.dot(swiglu, down_weight, preferred_element_type=jnp.bfloat16))
    rms_mlp = lax.rsqrt(jnp.mean(mlp * mlp, axis=1) + EPSILON)
    out_rows = hidden + mlp * rms_mlp[:, None] * post_gain[1]
    upstream = grad_rows.astype(jnp.float32)
    gain_mlp = jnp.sum(upstream * mlp * rms_mlp[:, None], axis=0)
    d_mlp = norm_back(
        mlp,
        rms_mlp,
        post_gain[1],
        upstream,
        model_width,
        jnp.sum(mlp * post_gain[1] * upstream, axis=1),
    ).astype(jnp.bfloat16)
    d_mlp_full = gather_rows(d_mlp)
    d_swiglu = jnp.einsum("td,fd->tf", d_mlp_full, down_weight, preferred_element_type=jnp.float32)
    d_gate = d_swiglu * up_pre * sigmoid_gate * (1.0 + gate_pre * (1.0 - sigmoid_gate))
    d_up = d_swiglu * silu_gate
    d_gate_up = jnp.stack([d_gate, d_up], axis=1).astype(jnp.bfloat16)
    d_hidden = upstream + scatter_rows(
        jnp.einsum("tnf,ndf->td", d_gate_up, gate_up_weight, preferred_element_type=jnp.bfloat16)
    )
    gain_attn = jnp.sum(d_hidden * attn * rms_attn[:, None], axis=0)
    d_attn = norm_back(
        attn,
        rms_attn,
        post_gain[0],
        d_hidden,
        model_width,
        jnp.sum(attn * post_gain[0] * d_hidden, axis=1),
    ).astype(jnp.bfloat16)
    d_attn_full = gather_rows(d_attn)
    d_context = jnp.einsum("td,cd->tc", d_attn_full, out_weight, preferred_element_type=jnp.float32)
    d_context_b = d_context.astype(jnp.bfloat16).reshape(group_rows, local_heads, HD)
    scores = block_scores(queries, lookups, visible, score_scale)
    prob_f = jnp.exp(scores - total_parts[:, :, None])
    prob_rows = prob_f.astype(jnp.bfloat16)
    d_prob = jnp.einsum("bhd,khd->hbk", d_context_b, contents, preferred_element_type=jnp.float32)
    row_delta = jnp.sum(d_prob * prob_f, axis=2)
    d_scores = (prob_f * (d_prob - row_delta[:, :, None])).astype(jnp.bfloat16)
    query_grads = (
        jnp.einsum("hbk,khd->bhd", d_scores, lookups, preferred_element_type=jnp.float32)
        * score_scale
    )
    key_grad = (
        jnp.einsum("hbk,bhd->khd", d_scores, queries, preferred_element_type=jnp.float32)
        * score_scale
    )
    value_grad = jnp.einsum(
        "hbk,bhd->khd", prob_rows, d_context_b, preferred_element_type=jnp.float32
    )
    query_norm_grad = unrotate(query_grads, cos_t, sin_t).reshape(group_rows, local_width)
    key_norm_grad = unrotate(key_grad, cos_t, sin_t).reshape(group_rows, local_width)
    gain_query = jnp.sum(query_norm_grad * query_raw * inv_rms[0][:, None], axis=0)
    gain_key = jnp.sum(key_norm_grad * key_raw * inv_rms[1][:, None], axis=0)
    feature_sums = sum_row_values(
        jnp.stack(
            [
                jnp.sum(query_raw * qk_gain[0] * query_norm_grad, axis=1),
                jnp.sum(key_raw * qk_gain[1] * key_norm_grad, axis=1),
            ]
        )
    )
    d_query_raw = norm_back(
        query_raw, inv_rms[0], qk_gain[0], query_norm_grad, model_width, feature_sums[0]
    )
    d_key_raw = norm_back(
        key_raw, inv_rms[1], qk_gain[1], key_norm_grad, model_width, feature_sums[1]
    )
    d_projected = jnp.stack(
        [d_query_raw, d_key_raw, value_grad.reshape(group_rows, local_width)], axis=1
    ).astype(jnp.bfloat16)
    input_rows = d_hidden + scatter_rows(
        jnp.einsum("tne,nde->td", d_projected, qkv_weight, preferred_element_type=jnp.bfloat16)
    )
    saved = (
        x_full,
        d_projected.reshape(group_rows, -1),
        context,
        d_attn_full,
        hidden_full,
        d_gate_up.reshape(group_rows, -1),
        swiglu,
        d_mlp_full,
    )
    return (
        out_rows,
        input_rows,
        saved,
        d_mlp,
        jnp.stack([gain_attn, gain_mlp]),
        jnp.stack([gain_query, gain_key]),
    )


def grad_blocks(order, lefts, rights, width, adds, kind):
    blocks = order.shape[0]
    sets = len(lefts)
    rows = [left.shape[0] for left in lefts]
    block = lefts[0].shape[1] // lax.axis_size("replica")
    tile = min(512, width)

    def kernel(order_ref, *refs):
        left_refs = refs[: sets * blocks]
        right_refs = refs[sets * blocks : sets * blocks + sets]
        add_refs = refs[sets * blocks + sets : sets * blocks + sets + len(adds)]
        out_ref = refs[sets * blocks + sets + len(adds)]
        turned = refs[sets * blocks + sets + len(adds) + 1 :]

        @pl.when(pl.program_id(0) == 0)
        def _():
            for k in range(sets):
                for b in range(blocks):
                    turned[k][pl.ds(b * block, block), :] = left_refs[k * blocks + b][...].T

        total = jnp.dot(turned[0][...], right_refs[0][...], preferred_element_type=jnp.float32)
        for k in range(1, sets):
            total += jnp.dot(turned[k][...], right_refs[k][...], preferred_element_type=jnp.float32)
        for add_ref in add_refs:
            total += add_ref[...].astype(jnp.float32)
        out_ref[...] = total.astype(out_ref.dtype)

    def left_spec(k, b):
        return pl.BlockSpec((rows[k], block), lambda f, order_ref: (0, order_ref[b]))

    in_specs = [left_spec(k, b) for k in range(sets) for b in range(blocks)]
    in_specs += [
        pl.BlockSpec((rows[k], tile), lambda f, order_ref, at=first_col // tile: (0, at + f))
        for k, (_, first_col) in enumerate(rights)
    ]
    in_specs += [
        pl.BlockSpec((blocks * block, tile), lambda f, order_ref, at=group: (at, f))
        for _, group in adds
    ]
    depth = sum(rows)
    return pl.pallas_call(
        kernel,
        out_shape=jax.ShapeDtypeStruct((blocks * block, width), kind),
        grid_spec=pltpu.PrefetchScalarGridSpec(
            num_scalar_prefetch=1,
            grid=(width // tile,),
            in_specs=in_specs,
            out_specs=pl.BlockSpec((blocks * block, tile), lambda f, order_ref: (0, f)),
            scratch_shapes=[pltpu.VMEM((blocks * block, count), jnp.bfloat16) for count in rows],
        ),
        compiler_params=pltpu.CompilerParams(dimension_semantics=("arbitrary",)),
        cost_estimate=pl.CostEstimate(
            flops=2 * depth * blocks * block * width,
            bytes_accessed=2 * depth * (blocks * block + width)
            + (4 if kind == jnp.float32 else 2) * blocks * block * width * (1 + len(adds)),
            transcendentals=0,
        ),
    )(
        order,
        *[lefts[k] for k in range(sets) for _ in range(blocks)],
        *[right for right, _ in rights],
        *[add for add, _ in adds],
    )


def mlp_units(hidden, d_mlp, gate_up_weight, down_weight):
    rows, model_width = hidden.shape
    units = down_weight.shape[0]
    tile = min(256, units)

    def kernel(hidden_ref, d_mlp_ref, gate_ref, up_ref, down_ref, d_gate_ref, d_up_ref, swiglu_ref):
        gate = jnp.dot(hidden_ref[...], gate_ref[...], preferred_element_type=jnp.float32)
        up = jnp.dot(hidden_ref[...], up_ref[...], preferred_element_type=jnp.float32)
        d_swiglu = lax.dot_general(
            d_mlp_ref[...],
            down_ref[...],
            (((1,), (1,)), ((), ())),
            preferred_element_type=jnp.float32,
        )
        sigmoid = jax.nn.sigmoid(gate)
        silu = gate * sigmoid
        swiglu_ref[...] = (silu * up).astype(jnp.bfloat16)
        d_gate_ref[...] = (d_swiglu * up * sigmoid * (1.0 + gate * (1.0 - sigmoid))).astype(
            jnp.bfloat16
        )
        d_up_ref[...] = (d_swiglu * silu).astype(jnp.bfloat16)

    whole = pl.BlockSpec((rows, model_width), lambda f: (0, 0))
    out = pl.BlockSpec((rows, tile), lambda f: (0, f))
    return pl.pallas_call(
        kernel,
        out_shape=[jax.ShapeDtypeStruct((rows, units), jnp.bfloat16)] * 3,
        grid=(units // tile,),
        in_specs=[
            whole,
            whole,
            pl.BlockSpec((None, model_width, tile), lambda f: (0, 0, f)),
            pl.BlockSpec((None, model_width, tile), lambda f: (1, 0, f)),
            pl.BlockSpec((tile, model_width), lambda f: (f, 0)),
        ],
        out_specs=[out, out, out],
        compiler_params=pltpu.CompilerParams(dimension_semantics=("arbitrary",)),
        cost_estimate=pl.CostEstimate(
            flops=6 * rows * model_width * units,
            bytes_accessed=2 * (2 * rows * model_width + 3 * model_width * units + 3 * rows * units),
            transcendentals=rows * units,
        ),
    )(hidden, d_mlp, gate_up_weight, gate_up_weight, down_weight)


def send_order(top):
    def halves(codes, bit):
        if len(codes) == 1:
            return codes
        return halves([c for c in codes if c & bit], 2 * bit) + halves(
            [c for c in codes if not c & bit], 2 * bit
        )

    stages = []
    bit = 1
    while bit < top:
        stages.append((bit, [bit + c for c in halves(list(range(0, top, 2 * bit)), 2 * bit)]))
        bit *= 2
    return stages


def owners_sum(lefts, rights, width, top):
    me = lax.axis_index("replica")
    received = []

    def part(codes, kind):
        adds = [(array, held.index(codes[0]) // len(codes)) for array, held in received]
        order = me ^ jnp.array(codes, jnp.int32)
        return grad_blocks(order, lefts, rights, width, adds, kind)

    for bit, codes in send_order(top):
        sent = part(codes, jnp.bfloat16)
        received.append((exchange(sent, "replica", bit), [code ^ bit for code in codes]))
    return part([0], jnp.float32)


def weight_grads(saved, partner, qkv_width, units):
    replicas = lax.axis_size("replica")
    parts = [list(group) for group in zip(*saved)]
    x_full, d_projected, context, d_attn, hidden, d_gate_up, swiglu, d_mlp = parts
    far_hidden, far_d_mlp, far_d_gate, far_d_up, far_swiglu = partner
    near = replicas // 2
    down = owners_sum(
        d_mlp + [far_d_mlp], [(own, 0) for own in swiglu] + [(far_swiglu, 0)], units, near
    )
    gate = owners_sum(
        hidden + [far_hidden], [(own, 0) for own in d_gate_up] + [(far_d_gate, 0)], units, near
    )
    up = owners_sum(
        hidden + [far_hidden], [(own, units) for own in d_gate_up] + [(far_d_up, 0)], units, near
    )
    out = owners_sum(d_attn, [(own, 0) for own in context], qkv_width, replicas)
    qkv = owners_sum(x_full, [(own, 0) for own in d_projected], 3 * qkv_width, replicas)
    qkv = jnp.stack([qkv[:, n * qkv_width : (n + 1) * qkv_width] for n in range(3)])
    return (qkv, out.T, jnp.stack([gate, up]), down.T)


def on_device(
    tokens,
    cotangent,
    parents,
    lengths,
    qkv_weight,
    out_weight,
    gate_up_weight,
    down_weight,
    qk_gain,
    post_gain,
):
    micro, tok_dev, model_width = tokens.shape
    local_width = qkv_weight.shape[2]
    outputs = []
    input_grads = []
    saved = []
    gains = []
    d_mlp_rows = []
    for micro_idx in range(micro):
        out_rows, input_rows, kept, d_mlp, gain_add, query_key_add = micro_step(
            tokens[micro_idx],
            cotangent[micro_idx],
            parents[micro_idx, 0],
            lengths[micro_idx, 0],
            qkv_weight,
            out_weight,
            gate_up_weight,
            down_weight,
            qk_gain,
            post_gain,
        )
        outputs.append(out_rows)
        input_grads.append(input_rows)
        saved.append(kept)
        d_mlp_rows.append(d_mlp)
        gains.append((gain_add, query_key_add))
    far = lax.axis_size("replica") // 2
    far_hidden = exchange(jnp.concatenate([kept[4] for kept in saved], axis=0), "replica", far)
    far_rows = exchange(jnp.stack(d_mlp_rows), "replica", far)
    far_d_mlp = jnp.concatenate(
        [far_rows]
        + [exchange(far_rows, "fsdp", flip) for flip in range(1, lax.axis_size("fsdp"))],
        axis=1,
    ).reshape(far_hidden.shape)
    far_d_gate, far_d_up, far_swiglu = mlp_units(far_hidden, far_d_mlp, gate_up_weight, down_weight)
    grads = weight_grads(
        saved,
        (far_hidden, far_d_mlp, far_d_gate, far_d_up, far_swiglu),
        local_width,
        down_weight.shape[0],
    )
    gain_rows = sum(gain for gain, _ in gains)
    query_key_rows = sum(gain for _, gain in gains)
    size = lax.axis_size("fsdp")
    me = lax.axis_index("fsdp")
    split = gain_rows.reshape(2, size, local_width)
    post_rows = lax.dynamic_index_in_dim(split, me, 1, keepdims=False)
    for flip in range(1, size):
        sent = lax.dynamic_index_in_dim(split, me ^ flip, 1, keepdims=False)
        post_rows = post_rows + exchange(sent, "fsdp", flip)
    sums = sum_small(jnp.concatenate([query_key_rows, post_rows], axis=0), "replica")
    return (
        jnp.stack(outputs),
        jnp.stack(input_grads),
        grads[0],
        grads[1],
        grads[2],
        grads[3],
        sums[:2],
        sums[2:],
    )


def solution(mesh):
    in_specs = (
        P(None, ("replica", "fsdp"), None),
        P(None, ("replica", "fsdp"), None),
        P(None, "replica", None),
        P(None, "replica", None),
        P(None, None, "fsdp"),
        P("fsdp", None),
        P(None, None, "fsdp"),
        P("fsdp", None),
        P(None, "fsdp"),
        P(),
    )
    out_specs = (
        P(None, ("replica", "fsdp"), None),
        P(None, ("replica", "fsdp"), None),
        P(None, "replica", "fsdp"),
        P("fsdp", "replica"),
        P(None, "replica", "fsdp"),
        P("fsdp", "replica"),
        P(None, "fsdp"),
        P(None, "fsdp"),
    )
    return jax.shard_map(
        on_device, mesh=mesh, in_specs=in_specs, out_specs=out_specs, check_vma=False
    )
```

```python
import jax
import jax.numpy as jnp
from jax import lax
from jax.experimental import pallas as pl
from jax.experimental.pallas import tpu as pltpu
from jax.sharding import PartitionSpec as P

HD = 128


EPSILON = 1e-06
ROPE_BASE = 500000.0
BF = jnp.bfloat16
F32 = jnp.float32


def exchange(value, axis, flip):
    size = lax.axis_size(axis)
    return lax.ppermute(value, axis, [(i, i ^ flip) for i in range(size)])


def gather_blocks(rows):
    return [rows] + [exchange(rows, "fsdp", flip) for flip in range(1, lax.axis_size("fsdp"))]


def swap_blocks(blocks):
    return [blocks[0]] + [exchange(blocks[flip], "fsdp", flip) for flip in range(1, len(blocks))]


def sum_small(value, axis):
    size = lax.axis_size(axis)
    flip = 1
    while flip < size:
        value = value + exchange(value, axis, flip)
        flip *= 2
    return value


def cost(flops, moved, transcendentals=0):
    return pl.CostEstimate(
        flops=int(flops), bytes_accessed=int(moved), transcendentals=int(transcendentals)
    )


def shape(dims, kind):
    return jax.ShapeDtypeStruct(dims, kind)


def dot(left, right):
    return jnp.dot(left, right, preferred_element_type=F32)


def dot_t(left, right):
    return lax.dot_general(left, right, (((1,), (1,)), ((), ())), preferred_element_type=F32)


def t_dot(left, right):
    return lax.dot_general(left, right, (((0,), (0,)), ((), ())), preferred_element_type=F32)


def lane_sums(field):
    ones = jnp.ones((8, field.shape[1]), F32)
    return lax.dot_general(
        ones,
        field,
        (((1,), (1,)), ((), ())),
        precision=lax.Precision.HIGHEST,
        preferred_element_type=F32,
    )


def join(block_refs, rows_ref):
    tok = block_refs[0].shape[0]
    for j, block_ref in enumerate(block_refs):
        rows_ref[pl.ds(j * tok, tok), :] = block_ref[...]


def write_blocks(rows, block_refs):
    tok = block_refs[0].shape[0]
    for j, block_ref in enumerate(block_refs):
        block_ref[...] = rows[j * tok : (j + 1) * tok].astype(block_ref.dtype)


def block_shapes(count, tok, width):
    return [shape((tok, width), F32)] + [shape((tok, width), BF)] * (count - 1)


def aligned_total(parts, tok):
    total = parts[0].T
    count = len(parts)
    for flip in range(1, count):
        column = parts[flip].T
        total = total + jnp.concatenate(
            [column[(j ^ flip) * tok : ((j ^ flip) + 1) * tok] for j in range(count)], axis=0
        )
    return total


def turn(field, cos_t, sin_t):
    return field * cos_t + pltpu.roll(field, HD // 2, 1) * sin_t


def turn_back(field, cos_t, sin_t):
    return field * cos_t - pltpu.roll(field, HD // 2, 1) * sin_t


VMEM = pl.BlockSpec(memory_space=pltpu.VMEM)
WHOLE = pltpu.CompilerParams(dimension_semantics=("arbitrary",))


def project(x_blocks, qkv_weight):
    count = len(x_blocks)
    tok, model_width = x_blocks[0].shape
    rows = count * tok
    width = qkv_weight.shape[2]

    def kernel(*refs):
        x_refs = refs[:count]
        weight_ref, raw_ref, values_ref, squares_ref, x_ref = refs[count:]
        step = pl.program_id(0)

        @pl.when(step == 0)
        def _():
            join(x_refs, x_ref)

        product = dot(x_ref[...], weight_ref[...])

        @pl.when(step < 2)
        def _():
            raw_ref[...] = product
            squares_ref[pl.ds(step, 1), :] = lane_sums(product * product)[:1]

        @pl.when(step == 2)
        def _():
            values_ref[...] = product.astype(BF)
            squares_ref[2:, :] = jnp.zeros((6, rows), F32)

    whole = pl.BlockSpec((tok, model_width), lambda n: (0, 0))
    return pl.pallas_call(
        kernel,
        out_shape=[
            shape((2, rows, width), F32),
            shape((rows, width), BF),
            shape((8, rows), F32),
            shape((rows, model_width), BF),
        ],
        grid=(3,),
        in_specs=[whole] * count + [pl.BlockSpec((None, model_width, width), lambda n: (n, 0, 0))],
        out_specs=[
            pl.BlockSpec((None, rows, width), lambda n: (jnp.minimum(n, 1), 0, 0)),
            pl.BlockSpec((rows, width), lambda n: (0, 0)),
            pl.BlockSpec((8, rows), lambda n: (0, 0)),
            pl.BlockSpec((rows, model_width), lambda n: (0, 0)),
        ],
        compiler_params=WHOLE,
        cost_estimate=cost(6 * rows * model_width * width, 6 * model_width * width + 8 * rows * width),
    )(*x_blocks, qkv_weight)


def attend(raw, values, squares, bias, cos_t, sin_t, qk_gain, out_weight):
    count = len(squares)
    _, rows, width = raw.shape
    heads = width // HD
    tok = rows // count
    model_width = out_weight.shape[1]
    total_width = model_width
    scale = HD ** (-0.5)

    def kernel(raw_ref, values_ref, bias_ref, cos_ref, sin_ref, gain_ref, out_weight_ref, *refs):
        parts = [ref[...] for ref in refs[:count]]
        context_ref, queries_ref, keys_ref, inv_ref = refs[count : count + 4]
        block_refs = refs[count + 4 :]
        inv = lax.rsqrt(aligned_total(parts, tok) / total_width + EPSILON)
        inv_ref[...] = inv
        cos_v, sin_v, bias_v = cos_ref[...], sin_ref[...], bias_ref[...]
        for h in range(heads):
            at = slice(h * HD, (h + 1) * HD)
            q = turn(raw_ref[0, :, at] * inv[:, 0:1] * gain_ref[0:1, at], cos_v, sin_v).astype(BF)
            k = turn(raw_ref[1, :, at] * inv[:, 1:2] * gain_ref[1:2, at], cos_v, sin_v).astype(BF)
            queries_ref[:, at] = q
            keys_ref[:, at] = k
            scores = dot_t(q, k) * scale + bias_v
            weights = jnp.exp(scores - jnp.max(scores, axis=1, keepdims=True))
            probs = (weights / jnp.sum(weights, axis=1, keepdims=True)).astype(BF)
            context_ref[:, at] = dot(probs, values_ref[:, at]).astype(BF)
        write_blocks(dot(context_ref[...], out_weight_ref[...]), block_refs)

    return pl.pallas_call(
        kernel,
        out_shape=[
            shape((rows, width), BF),
            shape((rows, width), BF),
            shape((rows, width), BF),
            shape((rows, 8), F32),
        ]
        + block_shapes(count, tok, model_width),
        in_specs=[VMEM] * (7 + count),
        out_specs=[VMEM] * (4 + count),
        cost_estimate=cost(
            4 * rows * rows * width + 2 * rows * width * model_width,
            2 * width * model_width + 14 * rows * width + 2 * rows * model_width,
            heads * rows * rows,
        ),
    )(raw, values, bias, cos_t, sin_t, qk_gain, out_weight, *squares)


def attend_back(
    d_attn_blocks, out_weight, queries, keys, values, raw, inv, bias, cos_t, sin_t, qk_gain
):
    count = len(d_attn_blocks)
    tok, model_width = d_attn_blocks[0].shape
    _, rows, width = raw.shape
    heads = width // HD
    scale = HD ** (-0.5)

    def kernel(*refs):
        (
            out_weight_ref,
            queries_ref,
            keys_ref,
            values_ref,
            raw_ref,
            inv_ref,
            bias_ref,
            cos_ref,
            sin_ref,
            gain_ref,
            d_attn_ref,
            d_norm_ref,
            d_values_ref,
            sums_ref,
            gain_sums_ref,
        ) = refs[count:]
        join(refs[:count], d_attn_ref)
        d_context = dot_t(d_attn_ref[...], out_weight_ref[...]).astype(BF)
        cos_v, sin_v, bias_v = cos_ref[...], sin_ref[...], bias_ref[...]
        inv = inv_ref[...]
        sums = [jnp.zeros((rows, HD), F32), jnp.zeros((rows, HD), F32)]
        for h in range(heads):
            at = slice(h * HD, (h + 1) * HD)
            q, k, v, d_out = queries_ref[:, at], keys_ref[:, at], values_ref[:, at], d_context[:, at]
            scores = dot_t(q, k) * scale + bias_v
            weights = jnp.exp(scores - jnp.max(scores, axis=1, keepdims=True))
            probs = weights / jnp.sum(weights, axis=1, keepdims=True)
            d_probs = dot_t(d_out, v)
            delta = jnp.sum(d_probs * probs, axis=1, keepdims=True)
            d_scores = (probs * (d_probs - delta)).astype(BF)
            d_values_ref[:, at] = t_dot(probs.astype(BF), d_out).astype(BF)
            turned = (dot(d_scores, k) * scale, t_dot(d_scores, q) * scale)
            for n in range(2):
                d_norm = turn_back(turned[n], cos_v, sin_v)
                d_norm_ref[n, :, at] = d_norm
                field = raw_ref[n, :, at] * d_norm
                sums[n] += field * gain_ref[n : n + 1, at]
                gain_sums_ref[n : n + 1, at] = jnp.sum(field * inv[:, n : n + 1], axis=0, keepdims=True)
        sums_ref[0:1, :] = lane_sums(sums[0])[:1]
        sums_ref[1:2, :] = lane_sums(sums[1])[:1]
        sums_ref[2:, :] = jnp.zeros((6, rows), F32)

    return pl.pallas_call(
        kernel,
        out_shape=[
            shape((rows, model_width), BF),
            shape((2, rows, width), F32),
            shape((rows, width), BF),
            shape((8, rows), F32),
            shape((2, width), F32),
        ],
        in_specs=[VMEM] * (10 + count),
        out_specs=[VMEM] * 5,
        cost_estimate=cost(
            10 * rows * rows * width + 2 * rows * width * model_width,
            2 * width * model_width + 24 * rows * width + 2 * rows * model_width,
            heads * rows * rows,
        ),
    )(
        *d_attn_blocks,
        out_weight,
        queries,
        keys,
        values,
        raw,
        inv,
        bias,
        cos_t,
        sin_t,
        qk_gain,
    )


def project_back(d_norm, d_values, raw, inv, sums, qk_gain, qkv_weight):
    count = len(sums)
    _, rows, width = raw.shape
    tok = rows // count
    model_width = qkv_weight.shape[1]

    def kernel(d_norm_ref, d_values_ref, raw_ref, inv_ref, gain_ref, weight_ref, *refs):
        parts = refs[:count]
        d_projected_ref = refs[count]
        block_refs = refs[count + 1 : 2 * count + 1]
        total_ref = refs[2 * count + 1]
        step = pl.program_id(0)
        inv = inv_ref[...]

        @pl.when(step == 0)
        def _():
            d_projected_ref[...] = d_values_ref[...]

        @pl.when(step > 0)
        def _():
            shared = aligned_total([part[...] for part in parts], tok)
            first = step == 1
            r = jnp.where(first, inv[:, 0:1], inv[:, 1:2])
            s = jnp.where(first, shared[:, 0:1], shared[:, 1:2])
            gain = jnp.where(first, gain_ref[0:1, :], gain_ref[1:2, :])
            d_projected_ref[...] = (
                r * (d_norm_ref[...] * gain) - raw_ref[...] * (r * r * r * s / model_width)
            ).astype(BF)

        product = dot_t(d_projected_ref[...], weight_ref[...])

        @pl.when(step == 0)
        def _():
            total_ref[...] = product

        @pl.when(step > 0)
        def _():
            total_ref[...] += product

        @pl.when(step == 2)
        def _():
            write_blocks(total_ref[...], block_refs)

    def part_at(n):
        return lax.rem(n + 2, 3)

    field = pl.BlockSpec((None, rows, width), lambda n: (jnp.maximum(n - 1, 0), 0, 0))
    return pl.pallas_call(
        kernel,
        out_shape=[shape((3, rows, width), BF)] + block_shapes(count, tok, model_width),
        grid=(3,),
        in_specs=[
            field,
            pl.BlockSpec((rows, width), lambda n: (0, 0)),
            field,
            pl.BlockSpec((rows, 8), lambda n: (0, 0)),
            pl.BlockSpec((2, width), lambda n: (0, 0)),
            pl.BlockSpec((None, model_width, width), lambda n: (part_at(n), 0, 0)),
        ]
        + [pl.BlockSpec((8, rows), lambda n: (0, 0))] * count,
        out_specs=[pl.BlockSpec((None, rows, width), lambda n: (part_at(n), 0, 0))]
        + [pl.BlockSpec((tok, model_width), lambda n: (0, 0))] * count,
        scratch_shapes=[pltpu.VMEM((rows, model_width), F32)],
        compiler_params=WHOLE,
        cost_estimate=cost(
            6 * rows * model_width * width, 6 * model_width * width + 22 * rows * width + 2 * rows * model_width
        ),
    )(d_norm, d_values, raw, inv, qk_gain, qkv_weight, *sums)


def mlp_forward(hidden_blocks, gate_up_weight, down_weight):
    count = len(hidden_blocks)
    tok, model_width = hidden_blocks[0].shape
    rows = count * tok
    units = down_weight.shape[0]
    tile = min(512, units)
    last = units // tile - 1

    def kernel(*refs):
        gate_w_ref, up_w_ref, down_w_ref, gate_up_ref, swiglu_ref, hidden_ref = refs[
            count : count + 6
        ]
        block_refs = refs[count + 6 : 2 * count + 6]
        total_ref = refs[2 * count + 6]
        step = pl.program_id(0)

        @pl.when(step == 0)
        def _():
            join(refs[:count], hidden_ref)

        gate = dot(hidden_ref[...], gate_w_ref[...])
        up = dot(hidden_ref[...], up_w_ref[...])
        swiglu = (gate * jax.nn.sigmoid(gate) * up).astype(BF)
        gate_up_ref[0] = gate.astype(BF)
        gate_up_ref[1] = up.astype(BF)
        swiglu_ref[...] = swiglu
        product = dot(swiglu, down_w_ref[...])

        @pl.when(step == 0)
        def _():
            total_ref[...] = product

        @pl.when(step > 0)
        def _():
            total_ref[...] += product

        @pl.when(step == last)
        def _():
            write_blocks(total_ref[...], block_refs)

    field = pl.BlockSpec((rows, tile), lambda f: (0, f))
    return pl.pallas_call(
        kernel,
        out_shape=[
            shape((2, rows, units), BF),
            shape((rows, units), BF),
            shape((rows, model_width), BF),
        ]
        + block_shapes(count, tok, model_width),
        grid=(units // tile,),
        in_specs=[pl.BlockSpec((tok, model_width), lambda f: (0, 0))] * count
        + [
            pl.BlockSpec((None, model_width, tile), lambda f: (0, 0, f)),
            pl.BlockSpec((None, model_width, tile), lambda f: (1, 0, f)),
            pl.BlockSpec((tile, model_width), lambda f: (f, 0)),
        ],
        out_specs=[pl.BlockSpec((2, rows, tile), lambda f: (0, 0, f)), field]
        + [pl.BlockSpec((rows, model_width), lambda f: (0, 0))]
        + [pl.BlockSpec((tok, model_width), lambda f: (0, 0))] * count,
        scratch_shapes=[pltpu.VMEM((rows, model_width), F32)],
        compiler_params=WHOLE,
        cost_estimate=cost(
            6 * rows * model_width * units,
            6 * model_width * units + 6 * rows * units + 8 * rows * model_width,
            rows * units,
        ),
    )(*hidden_blocks, gate_up_weight, gate_up_weight, down_weight)


def unit_grads(gate, up, d_swiglu):
    sigmoid = jax.nn.sigmoid(gate)
    d_gate = d_swiglu * up * sigmoid * (1.0 + gate * (1.0 - sigmoid))
    return (d_gate.astype(BF), (d_swiglu * (gate * sigmoid)).astype(BF))


def mlp_back(d_mlp_blocks, gate_up, gate_up_weight, down_weight):
    count = len(d_mlp_blocks)
    tok, model_width = d_mlp_blocks[0].shape
    rows = count * tok
    units = down_weight.shape[0]
    tile = min(512, units)
    last = units // tile - 1

    def kernel(*refs):
        gate_up_ref, gate_w_ref, up_w_ref, down_w_ref, d_gate_up_ref, d_mlp_ref = refs[
            count : count + 6
        ]
        block_refs = refs[count + 6 : 2 * count + 6]
        total_ref = refs[2 * count + 6]
        step = pl.program_id(0)

        @pl.when(step == 0)
        def _():
            join(refs[:count], d_mlp_ref)

        d_swiglu = dot_t(d_mlp_ref[...], down_w_ref[...])
        d_gate, d_up = unit_grads(gate_up_ref[0].astype(F32), gate_up_ref[1].astype(F32), d_swiglu)
        d_gate_up_ref[0] = d_gate
        d_gate_up_ref[1] = d_up
        product = dot_t(d_gate, gate_w_ref[...]) + dot_t(d_up, up_w_ref[...])

        @pl.when(step == 0)
        def _():
            total_ref[...] = product

        @pl.when(step > 0)
        def _():
            total_ref[...] += product

        @pl.when(step == last)
        def _():
            write_blocks(total_ref[...], block_refs)

    field = pl.BlockSpec((2, rows, tile), lambda f: (0, 0, f))
    return pl.pallas_call(
        kernel,
        out_shape=[shape((2, rows, units), BF), shape((rows, model_width), BF)]
        + block_shapes(count, tok, model_width),
        grid=(units // tile,),
        in_specs=[pl.BlockSpec((tok, model_width), lambda f: (0, 0))] * count
        + [
            field,
            pl.BlockSpec((None, model_width, tile), lambda f: (0, 0, f)),
            pl.BlockSpec((None, model_width, tile), lambda f: (1, 0, f)),
            pl.BlockSpec((tile, model_width), lambda f: (f, 0)),
        ],
        out_specs=[field]
        + [pl.BlockSpec((rows, model_width), lambda f: (0, 0))]
        + [pl.BlockSpec((tok, model_width), lambda f: (0, 0))] * count,
        scratch_shapes=[pltpu.VMEM((rows, model_width), F32)],
        compiler_params=WHOLE,
        cost_estimate=cost(
            6 * rows * model_width * units,
            6 * model_width * units + 8 * rows * units + 8 * rows * model_width,
            rows * units,
        ),
    )(*d_mlp_blocks, gate_up, gate_up_weight, gate_up_weight, down_weight)


def mlp_units(hidden, d_mlp_blocks, gate_up_weight, down_weight):
    micro = len(hidden)
    count = len(d_mlp_blocks)
    tok, model_width = d_mlp_blocks[0].shape[1:]
    group = count * tok
    rows = micro * group
    units = down_weight.shape[0]
    tile = min(256, units)

    def kernel(*refs):
        hidden_refs = refs[:micro]
        block_refs = refs[micro : micro + count]
        gate_w_ref, up_w_ref, down_w_ref, d_gate_up_ref, swiglu_ref, d_mlp_ref, rows_ref = refs[
            micro + count :
        ]

        @pl.when(pl.program_id(0) == 0)
        def _():
            for m in range(micro):
                rows_ref[pl.ds(m * group, group), :] = hidden_refs[m][...]
                for j in range(count):
                    d_mlp_ref[pl.ds(m * group + j * tok, tok), :] = block_refs[j][m]

        gate = dot(rows_ref[...], gate_w_ref[...])
        up = dot(rows_ref[...], up_w_ref[...])
        d_gate, d_up = unit_grads(gate, up, dot_t(d_mlp_ref[...], down_w_ref[...]))
        swiglu_ref[...] = (gate * jax.nn.sigmoid(gate) * up).astype(BF)
        d_gate_up_ref[0] = d_gate
        d_gate_up_ref[1] = d_up

    return pl.pallas_call(
        kernel,
        out_shape=[
            shape((2, rows, units), BF),
            shape((rows, units), BF),
            shape((rows, model_width), BF),
        ],
        grid=(units // tile,),
        in_specs=[pl.BlockSpec((group, model_width), lambda f: (0, 0))] * micro
        + [pl.BlockSpec((micro, tok, model_width), lambda f: (0, 0, 0))] * count
        + [
            pl.BlockSpec((None, model_width, tile), lambda f: (0, 0, f)),
            pl.BlockSpec((None, model_width, tile), lambda f: (1, 0, f)),
            pl.BlockSpec((tile, model_width), lambda f: (f, 0)),
        ],
        out_specs=[
            pl.BlockSpec((2, rows, tile), lambda f: (0, 0, f)),
            pl.BlockSpec((rows, tile), lambda f: (0, f)),
            pl.BlockSpec((rows, model_width), lambda f: (0, 0)),
        ],
        scratch_shapes=[pltpu.VMEM((rows, model_width), BF)],
        compiler_params=WHOLE,
        cost_estimate=cost(
            6 * rows * model_width * units,
            6 * rows * model_width + 6 * model_width * units + 6 * rows * units,
            rows * units,
        ),
    )(*hidden, *d_mlp_blocks, gate_up_weight, gate_up_weight, down_weight)


def sum_parts(part_refs):
    total = part_refs[0][...].astype(F32)
    for part_ref in part_refs[1:]:
        total += part_ref[...].astype(F32)
    return total


def norm_back(field, gain, upstream):
    width = field.shape[1]
    inv = lax.rsqrt(jnp.sum(field * field, axis=1, keepdims=True) / width + EPSILON)
    weighted = upstream * gain
    shared = jnp.sum(field * weighted, axis=1, keepdims=True)
    gain_sum = jnp.sum(upstream * field * inv, axis=0, keepdims=True)
    return (inv * weighted - field * (inv * inv * inv * shared / width), gain_sum)


def after_attention(parts, x_rows, post_gain):
    tok, width = x_rows.shape
    count = len(parts)

    def kernel(*refs):
        x_ref, gain_ref, attn_ref, hidden_ref, rounded_ref = refs[count:]
        attn = sum_parts(refs[:count])
        inv = lax.rsqrt(jnp.sum(attn * attn, axis=1, keepdims=True) / width + EPSILON)
        hidden = x_ref[...].astype(F32) + attn * inv * gain_ref[0:1, :]
        attn_ref[...] = attn
        hidden_ref[...] = hidden
        rounded_ref[...] = hidden.astype(BF)

    return pl.pallas_call(
        kernel,
        out_shape=[shape((tok, width), F32), shape((tok, width), F32), shape((tok, width), BF)],
        in_specs=[VMEM] * (count + 2),
        out_specs=[VMEM] * 3,
        cost_estimate=cost(8 * tok * width, 24 * tok * width),
    )(*parts, x_rows, post_gain)


def after_mlp(parts, hidden, grad_rows, post_gain):
    tok, width = hidden.shape
    count = len(parts)

    def kernel(*refs):
        hidden_ref, grad_ref, gain_ref, out_ref, d_mlp_ref, gain_sum_ref = refs[count:]
        mlp = sum_parts(refs[:count])
        gain = gain_ref[1:2, :]
        inv = lax.rsqrt(jnp.sum(mlp * mlp, axis=1, keepdims=True) / width + EPSILON)
        out_ref[...] = hidden_ref[...] + mlp * inv * gain
        d_mlp, gain_sum = norm_back(mlp, gain, grad_ref[...].astype(F32))
        d_mlp_ref[...] = d_mlp.astype(BF)
        gain_sum_ref[...] = gain_sum

    return pl.pallas_call(
        kernel,
        out_shape=[shape((tok, width), F32), shape((tok, width), BF), shape((1, width), F32)],
        in_specs=[VMEM] * (count + 3),
        out_specs=[VMEM] * 3,
        cost_estimate=cost(16 * tok * width, 24 * tok * width),
    )(*parts, hidden, grad_rows, post_gain)


def before_attention(parts, grad_rows, attn, post_gain):
    tok, width = attn.shape
    count = len(parts)

    def kernel(*refs):
        grad_ref, attn_ref, gain_ref, d_hidden_ref, d_attn_ref, gain_sum_ref = refs[count:]
        d_hidden = grad_ref[...].astype(F32) + sum_parts(refs[:count])
        d_hidden_ref[...] = d_hidden
        d_attn, gain_sum = norm_back(attn_ref[...], gain_ref[0:1, :], d_hidden)
        d_attn_ref[...] = d_attn.astype(BF)
        gain_sum_ref[...] = gain_sum

    return pl.pallas_call(
        kernel,
        out_shape=[shape((tok, width), F32), shape((tok, width), BF), shape((1, width), F32)],
        in_specs=[VMEM] * (count + 3),
        out_specs=[VMEM] * 3,
        cost_estimate=cost(16 * tok * width, 24 * tok * width),
    )(*parts, grad_rows, attn, post_gain)


def send_order(top):
    def halves(codes, bit):
        if len(codes) == 1:
            return codes
        return halves([c for c in codes if c & bit], 2 * bit) + halves(
            [c for c in codes if not c & bit], 2 * bit
        )

    stages = []
    bit = 1
    while bit < top:
        stages.append((bit, [bit + c for c in halves(list(range(0, top, 2 * bit)), 2 * bit)]))
        bit *= 2
    return stages


def grad_rows_of(splits, sets):
    codes = [code for split in splits for code in split]
    blocks = len(codes)
    replicas = lax.axis_size("replica")
    order = lax.axis_index("replica") ^ jnp.array(codes, jnp.int32)
    block = sets[0][0].shape[1] // replicas
    planes, _, units = sets[0][1].shape
    tile = min(512, units)
    tiles = units // tile
    width = planes * units
    depth = sum(rows for _, _, _, rows in sets)
    count = len(sets)
    kinds = [BF] * (len(splits) - 1) + [F32]

    def kernel(order_ref, *refs):
        left_refs = refs[: count * blocks]
        right_refs = refs[count * blocks : count * blocks + count]
        out_refs = refs[count * blocks + count : count * blocks + count + len(splits)]
        turned_ref, right_ref = refs[count * blocks + count + len(splits) :]

        @pl.when(pl.program_id(0) == 0)
        def _():
            at = 0
            for k, (_, _, _, rows) in enumerate(sets):
                for b in range(blocks):
                    turned_ref[pl.ds(b * block, block), pl.ds(at, rows)] = left_refs[k * blocks + b][
                        ...
                    ].T
                at += rows

        at = 0
        for k, (_, _, _, rows) in enumerate(sets):
            right_ref[pl.ds(at, rows), :] = right_refs[k][...]
            at += rows
        first = 0
        for split, out_ref in zip(splits, out_refs):
            rows = len(split) * block
            out_ref[...] = dot(turned_ref[pl.ds(first, rows), :], right_ref[...]).astype(out_ref.dtype)
            first += rows

    in_specs = [
        pl.BlockSpec((rows, block), lambda f, order_ref, group=group, b=b: (group, order_ref[b]))
        for _, _, group, rows in sets
        for b in range(blocks)
    ] + [
        pl.BlockSpec(
            (None, rows, tile),
            lambda f, order_ref, group=group: (lax.div(f, tiles), group, lax.rem(f, tiles)),
        )
        for _, _, group, rows in sets
    ]
    return pl.pallas_call(
        kernel,
        out_shape=[shape((len(split) * block, width), kind) for split, kind in zip(splits, kinds)],
        grid_spec=pltpu.PrefetchScalarGridSpec(
            num_scalar_prefetch=1,
            grid=(planes * tiles,),
            in_specs=in_specs,
            out_specs=[
                pl.BlockSpec((len(split) * block, tile), lambda f, order_ref: (0, f))
                for split in splits
            ],
            scratch_shapes=[
                pltpu.VMEM((blocks * block, depth), BF),
                pltpu.VMEM((depth, tile), BF),
            ],
        ),
        compiler_params=WHOLE,
        cost_estimate=cost(
            2 * depth * blocks * block * width,
            2 * depth * (blocks * block + width) + 2 * blocks * block * width,
        ),
    )(
        order,
        *[left for left, _, _, _ in sets for _ in range(blocks)],
        *[right for _, right, _, _ in sets],
    )


def owners_parts(sets, top):
    stages = send_order(top)
    outs = grad_rows_of([codes for _, codes in stages] + [[0]], sets)
    received = []

    def with_adds(codes, out):
        rows = out.shape[0]
        parts = [out]
        for array, held in received:
            first = held.index(codes[0]) // len(codes) * rows
            parts.append(array[first : first + rows])
        return parts

    for (bit, codes), out in zip(stages, outs):
        parts = with_adds(codes, out)
        if len(parts) > 1:
            out = sum(part.astype(F32) for part in parts).astype(BF)
        received.append((exchange(out, "replica", bit), [code ^ bit for code in codes]))
    return (outs[-1], [(array, held.index(0)) for array, held in received])


def finish(parts, planes, turned):
    kept, adds = parts
    rows, width = kept.shape
    units = width // planes
    tile = min(512, units)
    tiles = units // tile

    def kernel(kept_ref, *refs):
        total = kept_ref[...]
        for add_ref in refs[:-1]:
            total += add_ref[...].astype(F32)
        refs[-1][...] = total.T if turned else total

    if turned:
        out_shape = shape((units, rows), F32)
        out_spec = pl.BlockSpec((tile, rows), lambda f: (f, 0))
    else:
        out_shape = shape((planes, rows, units), F32)
        out_spec = pl.BlockSpec(
            (None, rows, tile), lambda f: (lax.div(f, tiles), 0, lax.rem(f, tiles))
        )
    return pl.pallas_call(
        kernel,
        out_shape=out_shape,
        grid=(planes * tiles,),
        in_specs=[pl.BlockSpec((rows, tile), lambda f: (0, f))]
        + [pl.BlockSpec((rows, tile), lambda f, group=group: (group, f)) for _, group in adds],
        out_specs=out_spec,
        compiler_params=WHOLE,
        cost_estimate=cost(rows * width * len(adds), rows * width * (8 + 2 * len(adds))),
    )(kept, *[array for array, _ in adds])


def true_rows(tok_dev):
    size = lax.axis_size("fsdp")
    block = jnp.arange(size, dtype=jnp.int32) ^ lax.axis_index("fsdp")
    return (block[:, None] * tok_dev + jnp.arange(tok_dev, dtype=jnp.int32)[None, :]).reshape(-1)


def tree_tables(parent_row, length_row, places):
    segments = parent_row.shape[0]
    labels = jnp.arange(segments, dtype=jnp.int32)
    before = labels[:, None] >= labels[None, :]
    ends = jnp.sum(jnp.where(before, length_row[None, :], 0), axis=1)
    starts = ends - length_row
    segment_of = jnp.sum((places[:, None] >= ends[None, :]).astype(jnp.int32), axis=1)
    member = segment_of[:, None] == labels[None, :]
    reach = ((labels[:, None] == labels[None, :]) | (parent_row[:, None] == labels[None, :])).astype(F32)
    steps = 1
    while steps < segments - 1:
        reach = (jnp.dot(reach, reach) > 0.5).astype(F32)
        steps *= 2
    ancestry = reach > 0.5
    above = jnp.sum(jnp.where(ancestry, length_row[None, :], 0), axis=1) - length_row
    moved = jnp.sum(jnp.where(member, (above - starts)[None, :], 0), axis=1)
    position = (places + moved).astype(F32)
    member_f = member.astype(F32)
    near = jnp.dot(jnp.dot(member_f, reach), member_f.T) > 0.5
    visible = near & (places[None, :] <= places[:, None])
    freq = ROPE_BASE ** (-jnp.arange(0, HD, 2, dtype=F32) / HD)
    angle = position[:, None] * freq[None, :]
    cos_half, sin_half = jnp.cos(angle), jnp.sin(angle)
    return (
        jnp.where(visible, 0.0, -1e30).astype(F32),
        jnp.concatenate([cos_half, cos_half], axis=1),
        jnp.concatenate([-sin_half, sin_half], axis=1),
    )


def on_device(
    tokens,
    cotangent,
    parents,
    lengths,
    qkv_weight,
    out_weight,
    gate_up_weight,
    down_weight,
    qk_gain,
    post_gain,
):
    micro, tok_dev, model_width = tokens.shape
    local_width = qkv_weight.shape[2]
    size = lax.axis_size("fsdp")
    replicas = lax.axis_size("replica")
    rows = tok_dev * size
    units = down_weight.shape[0]
    micros = range(micro)
    places = true_rows(tok_dev)
    x_blocks = gather_blocks(tokens)
    tables = [tree_tables(parents[m, 0], lengths[m, 0], places) for m in micros]

    projected = [project([block[m] for block in x_blocks], qkv_weight) for m in micros]
    attended = []
    for m in micros:
        raw, values, squares, _ = projected[m]
        attended.append(
            attend(raw, values, gather_blocks(squares), *tables[m], qk_gain, out_weight)
        )
    residual = []
    for m in micros:
        parts = swap_blocks(attended[m][4:])
        residual.append(after_attention(parts, tokens[m], post_gain))
    expanded = [
        mlp_forward(gather_blocks(residual[m][2]), gate_up_weight, down_weight) for m in micros
    ]
    far = replicas // 2
    far_hidden = [exchange(expanded[m][2], "replica", far) for m in micros]
    finals = []
    for m in micros:
        parts = swap_blocks(expanded[m][3:])
        finals.append(after_mlp(parts, residual[m][1], cotangent[m], post_gain))
    shrunk = [
        mlp_back(gather_blocks(finals[m][1]), expanded[m][0], gate_up_weight, down_weight)
        for m in micros
    ]
    far_d_mlp = gather_blocks(exchange(jnp.stack([final[1] for final in finals]), "replica", far))
    far_d_gate_up, far_swiglu, far_d_mlp = mlp_units(
        far_hidden, far_d_mlp, gate_up_weight, down_weight
    )
    down_parts = owners_parts(
        [(shrunk[m][1], expanded[m][1][None], 0, rows) for m in micros]
        + [(far_d_mlp, far_swiglu[None], 0, micro * rows)],
        far,
    )
    gate_up_parts = owners_parts(
        [(expanded[m][2], shrunk[m][0], 0, rows) for m in micros]
        + [(jnp.concatenate(far_hidden, axis=0), far_d_gate_up, 0, micro * rows)],
        far,
    )
    entering = []
    for m in micros:
        parts = swap_blocks(shrunk[m][2:])
        entering.append(before_attention(parts, cotangent[m], residual[m][0], post_gain))
    unattended = []
    for m in micros:
        raw, values = projected[m][:2]
        _, queries, keys, inv = attended[m][:4]
        unattended.append(
            attend_back(
                gather_blocks(entering[m][1]),
                out_weight,
                queries,
                keys,
                values,
                raw,
                inv,
                *tables[m],
                qk_gain,
            )
        )
    out_parts = owners_parts(
        [(unattended[m][0], attended[m][0][None], 0, rows) for m in micros], replicas
    )
    unprojected = []
    for m in micros:
        _, d_norm, d_values, sums, _ = unattended[m]
        unprojected.append(
            project_back(
                d_norm,
                d_values,
                projected[m][0],
                attended[m][3],
                gather_blocks(sums),
                qk_gain,
                qkv_weight,
            )
        )
    qkv_parts = owners_parts(
        [(projected[m][3], unprojected[m][0], 0, rows) for m in micros], replicas
    )
    input_grads = []
    for m in micros:
        parts = swap_blocks(unprojected[m][1:])
        input_grads.append(entering[m][0] + sum(part.astype(F32) for part in parts))

    query_key_rows = sum(unattended[m][4] for m in micros)
    gain_rows = jnp.concatenate(
        [sum(entering[m][2] for m in micros), sum(finals[m][2] for m in micros)], axis=0
    )
    me = lax.axis_index("fsdp")
    split = gain_rows.reshape(2, size, local_width)
    post_rows = lax.dynamic_index_in_dim(split, me, 1, keepdims=False)
    for flip in range(1, size):
        sent = lax.dynamic_index_in_dim(split, me ^ flip, 1, keepdims=False)
        post_rows = post_rows + exchange(sent, "fsdp", flip)
    sums = sum_small(jnp.concatenate([query_key_rows, post_rows], axis=0), "replica")
    return (
        jnp.stack([final[0] for final in finals]),
        jnp.stack(input_grads),
        finish(qkv_parts, 3, False),
        finish(out_parts, 1, True),
        finish(gate_up_parts, 2, False),
        finish(down_parts, 1, True),
        sums[:2],
        sums[2:],
    )


def solution(mesh):
    in_specs = (
        P(None, ("replica", "fsdp"), None),
        P(None, ("replica", "fsdp"), None),
        P(None, "replica", None),
        P(None, "replica", None),
        P(None, None, "fsdp"),
        P("fsdp", None),
        P(None, None, "fsdp"),
        P("fsdp", None),
        P(None, "fsdp"),
        P(),
    )
    out_specs = (
        P(None, ("replica", "fsdp"), None),
        P(None, ("replica", "fsdp"), None),
        P(None, "replica", "fsdp"),
        P("fsdp", "replica"),
        P(None, "replica", "fsdp"),
        P("fsdp", "replica"),
        P(None, "fsdp"),
        P(None, "fsdp"),
    )
    return jax.shard_map(
        on_device, mesh=mesh, in_specs=in_specs, out_specs=out_specs, check_vma=False
    )
```

```python
import jax
import jax.numpy as jnp
from jax import lax
from jax.experimental import pallas as pl
from jax.experimental.pallas import tpu as pltpu
from jax.sharding import PartitionSpec as P

HD = 128


EPSILON = 1e-06
ROPE_BASE = 500000.0
BF = jnp.bfloat16
F32 = jnp.float32


def exchange(value, axis, flip):
    size = lax.axis_size(axis)
    return lax.ppermute(value, axis, [(i, i ^ flip) for i in range(size)])


def gather_blocks(rows):
    return [rows] + [exchange(rows, "fsdp", flip) for flip in range(1, lax.axis_size("fsdp"))]


def swap_blocks(blocks):
    return [blocks[0]] + [exchange(blocks[flip], "fsdp", flip) for flip in range(1, len(blocks))]


def cost(flops, moved, transcendentals=0):
    return (flops, moved, transcendentals)


class Order(list):
    pace = 0.001


def shape(dims, kind):
    return jax.ShapeDtypeStruct(dims, kind)


def dot(left, right):
    return jnp.dot(left, right, preferred_element_type=F32)


def dot_t(left, right):
    return lax.dot_general(left, right, (((1,), (1,)), ((), ())), preferred_element_type=F32)


def t_dot(left, right):
    return lax.dot_general(left, right, (((0,), (0,)), ((), ())), preferred_element_type=F32)


def lane_sums(field):
    ones = jnp.ones((8, field.shape[1]), F32)
    return lax.dot_general(
        ones,
        field,
        (((1,), (1,)), ((), ())),
        precision=lax.Precision.HIGHEST,
        preferred_element_type=F32,
    )


def join(block_refs, rows_ref):
    tok = block_refs[0].shape[0]
    for j, block_ref in enumerate(block_refs):
        rows_ref[pl.ds(j * tok, tok), :] = block_ref[...]


def write_blocks(rows, block_refs):
    tok = block_refs[0].shape[0]
    for j, block_ref in enumerate(block_refs):
        block_ref[...] = rows[j * tok : (j + 1) * tok].astype(block_ref.dtype)


def block_shapes(count, tok, width):
    return [shape((tok, width), F32)] + [shape((tok, width), BF)] * (count - 1)


def aligned_total(parts, tok):
    total = parts[0].T
    count = len(parts)
    for flip in range(1, count):
        column = parts[flip].T
        total = total + jnp.concatenate(
            [column[(j ^ flip) * tok : ((j ^ flip) + 1) * tok] for j in range(count)], axis=0
        )
    return total


def turn(field, cos_t, sin_t):
    return field * cos_t + pltpu.roll(field, HD // 2, 1) * sin_t


def turn_back(field, cos_t, sin_t):
    return field * cos_t - pltpu.roll(field, HD // 2, 1) * sin_t


VMEM = pl.BlockSpec(memory_space=pltpu.VMEM)
WHOLE = pltpu.CompilerParams(dimension_semantics=("arbitrary",))


def launch(
    order, kernel, args, in_specs, grid_spec=None, *, cost_estimate, pace=None, **settings
):
    waits = list(order)
    count = len(args)

    def body(*refs):
        kernel(*refs[:count], *refs[count + len(waits) :])

    flops, moved, transcendentals = [
        int(part * (order.pace if pace is None else pace)) for part in cost_estimate
    ]
    settings["cost_estimate"] = pl.CostEstimate(
        flops=flops, bytes_accessed=moved, transcendentals=transcendentals
    )
    specs = list(in_specs) + [pl.BlockSpec(memory_space=pl.ANY)] * len(waits)
    if grid_spec is None:
        settings["in_specs"] = specs
    else:
        settings["grid_spec"] = grid_spec(specs)
    settings["name"] = kernel.__qualname__.split(".<")[0].replace(".", "_")
    results = pl.pallas_call(body, **settings)(*args, *waits)
    order[:] = [results[0] if isinstance(results, (list, tuple)) else results]
    return results


def fence(order, arrays):
    order.extend(arrays)

    def kernel(out_ref):
        out_ref[...] = jnp.zeros((8, HD), F32)

    launch(
        order,
        kernel,
        [],
        in_specs=[],
        out_shape=shape((8, HD), F32),
        out_specs=VMEM,
        cost_estimate=cost(0, 1 << 30),
        pace=1,
    )


def gate(order, arrays):
    def kernel(*refs):
        pass

    held = pl.BlockSpec(memory_space=pl.ANY)
    return launch(
        order,
        kernel,
        arrays,
        in_specs=[held] * len(arrays),
        out_shape=[shape(array.shape, array.dtype) for array in arrays],
        out_specs=[held] * len(arrays),
        input_output_aliases={k: k for k in range(len(arrays))},
        cost_estimate=cost(0, 1000),
    )


def project(order, x_blocks, qkv_weight):
    count = len(x_blocks)
    tok, model_width = x_blocks[0].shape
    rows = count * tok
    width = qkv_weight.shape[2]

    def kernel(*refs):
        x_refs = refs[:count]
        weight_ref, raw_ref, values_ref, squares_ref, x_ref = refs[count:]
        step = pl.program_id(0)

        @pl.when(step == 0)
        def _():
            join(x_refs, x_ref)

        product = dot(x_ref[...], weight_ref[...])

        @pl.when(step < 2)
        def _():
            raw_ref[...] = product
            squares_ref[pl.ds(step, 1), :] = lane_sums(product * product)[:1]

        @pl.when(step == 2)
        def _():
            values_ref[...] = product.astype(BF)
            squares_ref[2:, :] = jnp.zeros((6, rows), F32)

    whole = pl.BlockSpec((tok, model_width), lambda n: (0, 0))
    return launch(
        order,
        kernel,
        [*x_blocks, qkv_weight],
        out_shape=[
            shape((2, rows, width), F32),
            shape((rows, width), BF),
            shape((8, rows), F32),
            shape((rows, model_width), BF),
        ],
        grid=(3,),
        in_specs=[whole] * count + [pl.BlockSpec((None, model_width, width), lambda n: (n, 0, 0))],
        out_specs=[
            pl.BlockSpec((None, rows, width), lambda n: (jnp.minimum(n, 1), 0, 0)),
            pl.BlockSpec((rows, width), lambda n: (0, 0)),
            pl.BlockSpec((8, rows), lambda n: (0, 0)),
            pl.BlockSpec((rows, model_width), lambda n: (0, 0)),
        ],
        compiler_params=WHOLE,
        cost_estimate=cost(6 * rows * model_width * width, 6 * model_width * width + 8 * rows * width),
    )


def pick(field, m, each, tok, at):
    return jnp.concatenate(
        [
            field[j * tok + m * each : j * tok + (m + 1) * each, at]
            for j in range(field.shape[0] // tok)
        ],
        axis=0,
    )


def place(ref, m, each, tok, at, rows):
    for j in range(ref.shape[0] // tok):
        ref[pl.ds(j * tok + m * each, each), at] = rows[j * each : (j + 1) * each]


def attend(order, raw, values, squares, tables, qk_gain, out_weight):
    count = len(squares)
    micro = len(tables)
    _, rows, width = raw.shape
    heads = width // HD
    tok = rows // count
    each = tok // micro
    pack = rows // micro
    model_width = out_weight.shape[1]
    total_width = model_width
    scale = HD ** (-0.5)

    def kernel(raw_ref, values_ref, gain_ref, out_weight_ref, *refs):
        table_refs = refs[: 3 * micro]
        parts = [ref[...] for ref in refs[3 * micro : 3 * micro + count]]
        refs = refs[3 * micro + count :]
        context_ref, queries_ref, keys_ref, inv_ref = refs[:4]
        block_refs = refs[4:]
        inv = lax.rsqrt(aligned_total(parts, tok) / total_width + EPSILON)
        inv_ref[...] = inv
        for m in range(micro):
            bias_v, cos_v, sin_v = [ref[...] for ref in table_refs[3 * m : 3 * m + 3]]
            inv_q = pick(inv, m, each, tok, slice(0, 1))
            inv_k = pick(inv, m, each, tok, slice(1, 2))
            own = slice(m * pack, (m + 1) * pack)
            for h in range(heads):
                at = slice(h * HD, (h + 1) * HD)
                q_raw = pick(raw_ref.at[0], m, each, tok, at)
                k_raw = pick(raw_ref.at[1], m, each, tok, at)
                q = turn(q_raw * inv_q * gain_ref[0:1, at], cos_v, sin_v).astype(BF)
                k = turn(k_raw * inv_k * gain_ref[1:2, at], cos_v, sin_v).astype(BF)
                queries_ref[own, at] = q
                keys_ref[own, at] = k
                scores = dot_t(q, k) * scale + bias_v
                weights = jnp.exp(scores - jnp.max(scores, axis=1, keepdims=True))
                probs = (weights / jnp.sum(weights, axis=1, keepdims=True)).astype(BF)
                context = dot(probs, pick(values_ref, m, each, tok, at)).astype(BF)
                place(context_ref, m, each, tok, at, context)
        write_blocks(dot(context_ref[...], out_weight_ref[...]), block_refs)

    return launch(
        order,
        kernel,
        [raw, values, qk_gain, out_weight, *[t for table in tables for t in table], *squares],
        out_shape=[
            shape((rows, width), BF),
            shape((rows, width), BF),
            shape((rows, width), BF),
            shape((rows, 8), F32),
        ]
        + block_shapes(count, tok, model_width),
        in_specs=[VMEM] * (4 + 3 * micro + count),
        out_specs=[VMEM] * (4 + count),
        cost_estimate=cost(
            4 * rows * pack * width + 2 * rows * width * model_width,
            2 * width * model_width + 14 * rows * width + 2 * rows * model_width,
            heads * rows * pack,
        ),
    )


def attend_back(order, d_attn_blocks, out_weight, queries, keys, values, raw, inv, tables, qk_gain):
    count = len(d_attn_blocks)
    micro = len(tables)
    tok, model_width = d_attn_blocks[0].shape
    _, rows, width = raw.shape
    heads = width // HD
    each = tok // micro
    pack = rows // micro
    scale = HD ** (-0.5)

    def kernel(*refs):
        block_refs = refs[:count]
        table_refs = refs[count : count + 3 * micro]
        (
            out_weight_ref,
            queries_ref,
            keys_ref,
            values_ref,
            raw_ref,
            inv_ref,
            gain_ref,
            d_attn_ref,
            d_norm_ref,
            d_values_ref,
            sums_ref,
            gain_sums_ref,
        ) = refs[count + 3 * micro :]
        join(block_refs, d_attn_ref)
        d_context = dot_t(d_attn_ref[...], out_weight_ref[...]).astype(BF)
        inv = inv_ref[...]
        sums = [[], []]
        gain_sums_ref[...] = jnp.zeros((2, width), F32)
        for m in range(micro):
            bias_v, cos_v, sin_v = [ref[...] for ref in table_refs[3 * m : 3 * m + 3]]
            invs = [pick(inv, m, each, tok, slice(n, n + 1)) for n in range(2)]
            own = slice(m * pack, (m + 1) * pack)
            totals = [jnp.zeros((pack, HD), F32), jnp.zeros((pack, HD), F32)]
            for h in range(heads):
                at = slice(h * HD, (h + 1) * HD)
                q, k = queries_ref[own, at], keys_ref[own, at]
                v = pick(values_ref, m, each, tok, at)
                d_out = pick(d_context, m, each, tok, at)
                scores = dot_t(q, k) * scale + bias_v
                weights = jnp.exp(scores - jnp.max(scores, axis=1, keepdims=True))
                probs = weights / jnp.sum(weights, axis=1, keepdims=True)
                d_probs = dot_t(d_out, v)
                delta = jnp.sum(d_probs * probs, axis=1, keepdims=True)
                d_scores = (probs * (d_probs - delta)).astype(BF)
                d_values = t_dot(probs.astype(BF), d_out).astype(BF)
                place(d_values_ref, m, each, tok, at, d_values)
                turned = (dot(d_scores, k) * scale, t_dot(d_scores, q) * scale)
                for n in range(2):
                    d_norm = turn_back(turned[n], cos_v, sin_v)
                    place(d_norm_ref.at[n], m, each, tok, at, d_norm)
                    field = pick(raw_ref.at[n], m, each, tok, at) * d_norm
                    totals[n] += field * gain_ref[n : n + 1, at]
                    gain_sums_ref[n : n + 1, at] += jnp.sum(field * invs[n], axis=0, keepdims=True)
            for n in range(2):
                sums[n].append(totals[n])
        for n in range(2):
            ordered = [
                sums[n][m][j * each : (j + 1) * each] for j in range(count) for m in range(micro)
            ]
            sums_ref[n : n + 1, :] = lane_sums(jnp.concatenate(ordered, axis=0))[:1]
        sums_ref[2:, :] = jnp.zeros((6, rows), F32)

    return launch(
        order,
        kernel,
        [
            *d_attn_blocks,
            *[t for table in tables for t in table],
            out_weight,
            queries,
            keys,
            values,
            raw,
            inv,
            qk_gain,
        ],
        out_shape=[
            shape((rows, model_width), BF),
            shape((2, rows, width), F32),
            shape((rows, width), BF),
            shape((8, rows), F32),
            shape((2, width), F32),
        ],
        in_specs=[VMEM] * (7 + 3 * micro + count),
        out_specs=[VMEM] * 5,
        cost_estimate=cost(
            10 * rows * pack * width + 2 * rows * width * model_width,
            2 * width * model_width + 24 * rows * width + 2 * rows * model_width,
            heads * rows * pack,
        ),
    )


def project_back(order, d_norm, d_values, raw, inv, sums, qk_gain, qkv_weight):
    count = len(sums)
    _, rows, width = raw.shape
    tok = rows // count
    model_width = qkv_weight.shape[1]

    def kernel(d_norm_ref, d_values_ref, raw_ref, inv_ref, gain_ref, weight_ref, *refs):
        parts = refs[:count]
        d_projected_ref = refs[count]
        block_refs = refs[count + 1 : 2 * count + 1]
        total_ref = refs[2 * count + 1]
        step = pl.program_id(0)
        inv = inv_ref[...]

        @pl.when(step == 0)
        def _():
            d_projected_ref[...] = d_values_ref[...]

        @pl.when(step > 0)
        def _():
            shared = aligned_total([part[...] for part in parts], tok)
            first = step == 1
            r = jnp.where(first, inv[:, 0:1], inv[:, 1:2])
            s = jnp.where(first, shared[:, 0:1], shared[:, 1:2])
            gain = jnp.where(first, gain_ref[0:1, :], gain_ref[1:2, :])
            d_projected_ref[...] = (
                r * (d_norm_ref[...] * gain) - raw_ref[...] * (r * r * r * s / model_width)
            ).astype(BF)

        product = dot_t(d_projected_ref[...], weight_ref[...])

        @pl.when(step == 0)
        def _():
            total_ref[...] = product

        @pl.when(step > 0)
        def _():
            total_ref[...] += product

        @pl.when(step == 2)
        def _():
            write_blocks(total_ref[...], block_refs)

    def part_at(n):
        return lax.rem(n + 2, 3)

    field = pl.BlockSpec((None, rows, width), lambda n: (jnp.maximum(n - 1, 0), 0, 0))
    return launch(
        order,
        kernel,
        [d_norm, d_values, raw, inv, qk_gain, qkv_weight, *sums],
        out_shape=[shape((3, rows, width), BF)] + block_shapes(count, tok, model_width),
        grid=(3,),
        in_specs=[
            field,
            pl.BlockSpec((rows, width), lambda n: (0, 0)),
            field,
            pl.BlockSpec((rows, 8), lambda n: (0, 0)),
            pl.BlockSpec((2, width), lambda n: (0, 0)),
            pl.BlockSpec((None, model_width, width), lambda n: (part_at(n), 0, 0)),
        ]
        + [pl.BlockSpec((8, rows), lambda n: (0, 0))] * count,
        out_specs=[pl.BlockSpec((None, rows, width), lambda n: (part_at(n), 0, 0))]
        + [pl.BlockSpec((tok, model_width), lambda n: (0, 0))] * count,
        scratch_shapes=[pltpu.VMEM((rows, model_width), F32)],
        compiler_params=WHOLE,
        cost_estimate=cost(
            6 * rows * model_width * width, 6 * model_width * width + 22 * rows * width + 2 * rows * model_width
        ),
    )


def mlp_forward(order, hidden_blocks, gate_up_weight, down_weight):
    count = len(hidden_blocks)
    tok, model_width = hidden_blocks[0].shape
    rows = count * tok
    units = down_weight.shape[0]
    tile = min(512, units)
    last = units // tile - 1

    def kernel(*refs):
        gate_w_ref, up_w_ref, down_w_ref, gate_up_ref, swiglu_ref, hidden_ref = refs[
            count : count + 6
        ]
        block_refs = refs[count + 6 : 2 * count + 6]
        total_ref = refs[2 * count + 6]
        step = pl.program_id(0)

        @pl.when(step == 0)
        def _():
            join(refs[:count], hidden_ref)

        gate = dot(hidden_ref[...], gate_w_ref[...])
        up = dot(hidden_ref[...], up_w_ref[...])
        swiglu = (gate * jax.nn.sigmoid(gate) * up).astype(BF)
        gate_up_ref[0] = gate.astype(BF)
        gate_up_ref[1] = up.astype(BF)
        swiglu_ref[...] = swiglu
        product = dot(swiglu, down_w_ref[...])

        @pl.when(step == 0)
        def _():
            total_ref[...] = product

        @pl.when(step > 0)
        def _():
            total_ref[...] += product

        @pl.when(step == last)
        def _():
            write_blocks(total_ref[...], block_refs)

    field = pl.BlockSpec((rows, tile), lambda f: (0, f))
    return launch(
        order,
        kernel,
        [*hidden_blocks, gate_up_weight, gate_up_weight, down_weight],
        out_shape=[
            shape((2, rows, units), BF),
            shape((rows, units), BF),
            shape((rows, model_width), BF),
        ]
        + block_shapes(count, tok, model_width),
        grid=(units // tile,),
        in_specs=[pl.BlockSpec((tok, model_width), lambda f: (0, 0))] * count
        + [
            pl.BlockSpec((None, model_width, tile), lambda f: (0, 0, f)),
            pl.BlockSpec((None, model_width, tile), lambda f: (1, 0, f)),
            pl.BlockSpec((tile, model_width), lambda f: (f, 0)),
        ],
        out_specs=[pl.BlockSpec((2, rows, tile), lambda f: (0, 0, f)), field]
        + [pl.BlockSpec((rows, model_width), lambda f: (0, 0))]
        + [pl.BlockSpec((tok, model_width), lambda f: (0, 0))] * count,
        scratch_shapes=[pltpu.VMEM((rows, model_width), F32)],
        compiler_params=WHOLE,
        cost_estimate=cost(
            6 * rows * model_width * units,
            6 * model_width * units + 6 * rows * units + 8 * rows * model_width,
            rows * units,
        ),
    )


def unit_grads(gate, up, d_swiglu):
    sigmoid = jax.nn.sigmoid(gate)
    d_gate = d_swiglu * up * sigmoid * (1.0 + gate * (1.0 - sigmoid))
    return (d_gate.astype(BF), (d_swiglu * (gate * sigmoid)).astype(BF))


def mlp_back(order, d_mlp_blocks, gate_up, gate_up_weight, down_weight):
    count = len(d_mlp_blocks)
    tok, model_width = d_mlp_blocks[0].shape
    rows = count * tok
    units = down_weight.shape[0]
    tile = min(512, units)
    last = units // tile - 1

    def kernel(*refs):
        gate_up_ref, gate_w_ref, up_w_ref, down_w_ref, d_gate_up_ref, d_mlp_ref = refs[
            count : count + 6
        ]
        block_refs = refs[count + 6 : 2 * count + 6]
        total_ref = refs[2 * count + 6]
        step = pl.program_id(0)

        @pl.when(step == 0)
        def _():
            join(refs[:count], d_mlp_ref)

        d_swiglu = dot_t(d_mlp_ref[...], down_w_ref[...])
        d_gate, d_up = unit_grads(gate_up_ref[0].astype(F32), gate_up_ref[1].astype(F32), d_swiglu)
        d_gate_up_ref[0] = d_gate
        d_gate_up_ref[1] = d_up
        product = dot_t(d_gate, gate_w_ref[...]) + dot_t(d_up, up_w_ref[...])

        @pl.when(step == 0)
        def _():
            total_ref[...] = product

        @pl.when(step > 0)
        def _():
            total_ref[...] += product

        @pl.when(step == last)
        def _():
            write_blocks(total_ref[...], block_refs)

    field = pl.BlockSpec((2, rows, tile), lambda f: (0, 0, f))
    return launch(
        order,
        kernel,
        [*d_mlp_blocks, gate_up, gate_up_weight, gate_up_weight, down_weight],
        out_shape=[shape((2, rows, units), BF), shape((rows, model_width), BF)]
        + block_shapes(count, tok, model_width),
        grid=(units // tile,),
        in_specs=[pl.BlockSpec((tok, model_width), lambda f: (0, 0))] * count
        + [
            field,
            pl.BlockSpec((None, model_width, tile), lambda f: (0, 0, f)),
            pl.BlockSpec((None, model_width, tile), lambda f: (1, 0, f)),
            pl.BlockSpec((tile, model_width), lambda f: (f, 0)),
        ],
        out_specs=[field]
        + [pl.BlockSpec((rows, model_width), lambda f: (0, 0))]
        + [pl.BlockSpec((tok, model_width), lambda f: (0, 0))] * count,
        scratch_shapes=[pltpu.VMEM((rows, model_width), F32)],
        compiler_params=WHOLE,
        cost_estimate=cost(
            6 * rows * model_width * units,
            6 * model_width * units + 8 * rows * units + 8 * rows * model_width,
            rows * units,
        ),
    )


def mlp_units(order, hidden_blocks, d_mlp_blocks, gate_up_weight, down_weight):
    count = len(d_mlp_blocks)
    tok, model_width = d_mlp_blocks[0].shape
    rows = count * tok
    units = down_weight.shape[0]
    tile = min(256, units)

    def kernel(*refs):
        gate_w_ref, up_w_ref, down_w_ref = refs[2 * count : 2 * count + 3]
        d_gate_up_ref, swiglu_ref, d_mlp_ref, hidden_ref = refs[2 * count + 3 :]

        @pl.when(pl.program_id(0) == 0)
        def _():
            join(refs[:count], hidden_ref)
            join(refs[count : 2 * count], d_mlp_ref)

        gate = dot(hidden_ref[...], gate_w_ref[...])
        up = dot(hidden_ref[...], up_w_ref[...])
        d_gate, d_up = unit_grads(gate, up, dot_t(d_mlp_ref[...], down_w_ref[...]))
        swiglu_ref[...] = (gate * jax.nn.sigmoid(gate) * up).astype(BF)
        d_gate_up_ref[0] = d_gate
        d_gate_up_ref[1] = d_up

    return launch(
        order,
        kernel,
        [*hidden_blocks, *d_mlp_blocks, gate_up_weight, gate_up_weight, down_weight],
        out_shape=[
            shape((2, rows, units), BF),
            shape((rows, units), BF),
            shape((rows, model_width), BF),
            shape((rows, model_width), BF),
        ],
        grid=(units // tile,),
        in_specs=[pl.BlockSpec((tok, model_width), lambda f: (0, 0))] * (2 * count)
        + [
            pl.BlockSpec((None, model_width, tile), lambda f: (0, 0, f)),
            pl.BlockSpec((None, model_width, tile), lambda f: (1, 0, f)),
            pl.BlockSpec((tile, model_width), lambda f: (f, 0)),
        ],
        out_specs=[
            pl.BlockSpec((2, rows, tile), lambda f: (0, 0, f)),
            pl.BlockSpec((rows, tile), lambda f: (0, f)),
            pl.BlockSpec((rows, model_width), lambda f: (0, 0)),
            pl.BlockSpec((rows, model_width), lambda f: (0, 0)),
        ],
        compiler_params=WHOLE,
        cost_estimate=cost(
            6 * rows * model_width * units,
            6 * rows * model_width + 6 * model_width * units + 6 * rows * units,
            rows * units,
        ),
    )


def sum_parts(part_refs):
    total = part_refs[0][...].astype(F32)
    for part_ref in part_refs[1:]:
        total += part_ref[...].astype(F32)
    return total


def norm_back(field, gain, upstream):
    width = field.shape[1]
    inv = lax.rsqrt(jnp.sum(field * field, axis=1, keepdims=True) / width + EPSILON)
    weighted = upstream * gain
    shared = jnp.sum(field * weighted, axis=1, keepdims=True)
    gain_sum = jnp.sum(upstream * field * inv, axis=0, keepdims=True)
    return (inv * weighted - field * (inv * inv * inv * shared / width), gain_sum)


def after_attention(order, parts, x_rows, post_gain):
    tok, width = x_rows.shape
    count = len(parts)

    def kernel(*refs):
        x_ref, gain_ref, attn_ref, hidden_ref, rounded_ref = refs[count:]
        attn = sum_parts(refs[:count])
        inv = lax.rsqrt(jnp.sum(attn * attn, axis=1, keepdims=True) / width + EPSILON)
        hidden = x_ref[...].astype(F32) + attn * inv * gain_ref[0:1, :]
        attn_ref[...] = attn
        hidden_ref[...] = hidden
        rounded_ref[...] = hidden.astype(BF)

    return launch(
        order,
        kernel,
        [*parts, x_rows, post_gain],
        out_shape=[shape((tok, width), F32), shape((tok, width), F32), shape((tok, width), BF)],
        in_specs=[VMEM] * (count + 2),
        out_specs=[VMEM] * 3,
        cost_estimate=cost(8 * tok * width, 24 * tok * width),
    )


def after_mlp(order, parts, hidden, grad_rows, post_gain):
    tok, width = hidden.shape
    count = len(parts)

    def kernel(*refs):
        hidden_ref, grad_ref, gain_ref, out_ref, d_mlp_ref, gain_sum_ref = refs[count:]
        mlp = sum_parts(refs[:count])
        gain = gain_ref[1:2, :]
        inv = lax.rsqrt(jnp.sum(mlp * mlp, axis=1, keepdims=True) / width + EPSILON)
        out_ref[...] = hidden_ref[...] + mlp * inv * gain
        d_mlp, gain_sum = norm_back(mlp, gain, grad_ref[...].astype(F32))
        d_mlp_ref[...] = d_mlp.astype(BF)
        gain_sum_ref[...] = gain_sum

    return launch(
        order,
        kernel,
        [*parts, hidden, grad_rows, post_gain],
        out_shape=[shape((tok, width), F32), shape((tok, width), BF), shape((1, width), F32)],
        in_specs=[VMEM] * (count + 3),
        out_specs=[VMEM] * 3,
        cost_estimate=cost(16 * tok * width, 24 * tok * width),
    )


def before_attention(order, parts, grad_rows, attn, post_gain):
    tok, width = attn.shape
    count = len(parts)

    def kernel(*refs):
        grad_ref, attn_ref, gain_ref, d_hidden_ref, d_attn_ref, gain_sum_ref = refs[count:]
        d_hidden = grad_ref[...].astype(F32) + sum_parts(refs[:count])
        d_hidden_ref[...] = d_hidden
        d_attn, gain_sum = norm_back(attn_ref[...], gain_ref[0:1, :], d_hidden)
        d_attn_ref[...] = d_attn.astype(BF)
        gain_sum_ref[...] = gain_sum

    return launch(
        order,
        kernel,
        [*parts, grad_rows, attn, post_gain],
        out_shape=[shape((tok, width), F32), shape((tok, width), BF), shape((1, width), F32)],
        in_specs=[VMEM] * (count + 3),
        out_specs=[VMEM] * 3,
        cost_estimate=cost(16 * tok * width, 24 * tok * width),
    )


def send_order(top):
    def halves(codes, bit):
        if len(codes) == 1:
            return codes
        return halves([c for c in codes if c & bit], 2 * bit) + halves(
            [c for c in codes if not c & bit], 2 * bit
        )

    stages = []
    bit = 1
    while bit < top:
        stages.append((bit, [bit + c for c in halves(list(range(0, top, 2 * bit)), 2 * bit)]))
        bit *= 2
    return stages


def grad_rows_of(order, splits, sets):
    codes = [code for split in splits for code in split]
    blocks = len(codes)
    replicas = lax.axis_size("replica")
    picks = lax.axis_index("replica") ^ jnp.array(codes, jnp.int32)
    block = sets[0][0].shape[1] // replicas
    planes, _, units = sets[0][1].shape
    tile = min(512, units)
    tiles = units // tile
    width = planes * units
    depth = sum(rows for _, _, _, rows in sets)
    count = len(sets)
    kinds = [BF] * (len(splits) - 1) + [F32]

    def kernel(picks_ref, *refs):
        left_refs = refs[: count * blocks]
        right_refs = refs[count * blocks : count * blocks + count]
        out_refs = refs[count * blocks + count : count * blocks + count + len(splits)]
        turned_ref, right_ref = refs[count * blocks + count + len(splits) :]

        @pl.when(pl.program_id(0) == 0)
        def _():
            at = 0
            for k, (_, _, _, rows) in enumerate(sets):
                for b in range(blocks):
                    turned_ref[pl.ds(b * block, block), pl.ds(at, rows)] = left_refs[k * blocks + b][
                        ...
                    ].T
                at += rows

        at = 0
        for k, (_, _, _, rows) in enumerate(sets):
            right_ref[pl.ds(at, rows), :] = right_refs[k][...]
            at += rows
        first = 0
        for split, out_ref in zip(splits, out_refs):
            rows = len(split) * block
            out_ref[...] = dot(turned_ref[pl.ds(first, rows), :], right_ref[...]).astype(out_ref.dtype)
            first += rows

    in_specs = [
        pl.BlockSpec((rows, block), lambda f, picks_ref, group=group, b=b: (group, picks_ref[b]))
        for _, _, group, rows in sets
        for b in range(blocks)
    ] + [
        pl.BlockSpec(
            (None, rows, tile),
            lambda f, picks_ref, group=group: (lax.div(f, tiles), group, lax.rem(f, tiles)),
        )
        for _, _, group, rows in sets
    ]
    return launch(
        order,
        kernel,
        [picks]
        + [left for left, _, _, _ in sets for _ in range(blocks)]
        + [right for _, right, _, _ in sets],
        in_specs,
        lambda specs: pltpu.PrefetchScalarGridSpec(
            num_scalar_prefetch=1,
            grid=(planes * tiles,),
            in_specs=specs,
            out_specs=[
                pl.BlockSpec((len(split) * block, tile), lambda f, picks_ref: (0, f))
                for split in splits
            ],
            scratch_shapes=[
                pltpu.VMEM((blocks * block, depth), BF),
                pltpu.VMEM((depth, tile), BF),
            ],
        ),
        out_shape=[shape((len(split) * block, width), kind) for split, kind in zip(splits, kinds)],
        compiler_params=WHOLE,
        cost_estimate=cost(
            2 * depth * blocks * block * width,
            2 * depth * (blocks * block + width) + 2 * blocks * block * width,
        ),
    )


def add_parts(order, own, adds, column, width):
    rows = own.shape[0]
    tile = min(2048, width)
    tiles = width // tile

    def kernel(own_ref, *refs):
        refs[-1][...] = sum_parts([own_ref, *refs[:-1]]).astype(BF)

    return launch(
        order,
        kernel,
        [own] + [array for array, _, _ in adds],
        in_specs=[
            pl.BlockSpec((rows, tile), lambda f, group=group, at=at: (group, at * tiles + f))
            for group, at in [(0, column)] + [(group, at) for _, group, at in adds]
        ],
        out_shape=shape((rows, width), BF),
        grid=(tiles,),
        out_specs=pl.BlockSpec((rows, tile), lambda f: (0, f)),
        compiler_params=WHOLE,
        cost_estimate=cost(rows * width * len(adds), 2 * rows * width * (2 + len(adds))),
    )


class OwnersSum:
    def __init__(self, order, sets, top, pieces=1):
        self.stages = send_order(top)
        self.outs = grad_rows_of(order, [codes for _, codes in self.stages] + [[0]], sets)
        self.pieces = pieces
        self.at = 0
        self.received = [[] for _ in range(pieces)]
        bit, codes = self.stages[0]
        whole = exchange(self.outs[0], "replica", bit)
        for n in range(pieces):
            self.received[n].append((whole, [code ^ bit for code in codes], n))

    def adds(self, n, codes):
        return [
            (array, held.index(codes[0]) // len(codes), column)
            for array, held, column in self.received[n]
        ]

    def latest(self):
        return self.received[-1][-1][0]

    def step(self, order):
        self.at += 1
        bit, codes = self.stages[self.at]
        own = self.outs[self.at]
        width = own.shape[1] // self.pieces
        for n in range(self.pieces):
            sent = add_parts(order, own, self.adds(n, codes), n, width)
            self.received[n].append(
                (exchange(sent, "replica", bit), [code ^ bit for code in codes], 0)
            )

    def finish(self, order, planes, turned):
        kept = self.outs[-1]
        rows, width = kept.shape
        units = width // planes
        span = width // self.pieces
        tile = min(512 if turned else 1024, units)
        tiles = units // tile
        grid = planes * tiles
        count = grid // self.pieces
        adds = [
            (array, group, column * count if array.shape[1] == width else -1, n)
            for n in range(self.pieces)
            for array, group, column in self.adds(n, [0])
        ]
        each = len(adds) // self.pieces

        def kernel(kept_ref, *refs):
            out_ref = refs[-1]
            for n in range(self.pieces):

                @pl.when(lax.div(pl.program_id(0), count) == n)
                def _():
                    total = kept_ref[...]
                    for add_ref in refs[n * each : (n + 1) * each]:
                        total += add_ref[...].astype(F32)
                    out_ref[...] = total.T if turned else total

        def add_spec(group, whole, n):
            def at(f):
                own = jnp.clip(f - n * count, 0, count - 1)
                return (group, own + n * count if whole else own)

            return pl.BlockSpec((rows, tile), at)

        if turned:
            out_shape = shape((units, rows), F32)
            out_spec = pl.BlockSpec((tile, rows), lambda f: (f, 0))
        else:
            out_shape = shape((planes, rows, units), F32)
            out_spec = pl.BlockSpec(
                (None, rows, tile), lambda f: (lax.div(f, tiles), 0, lax.rem(f, tiles))
            )
        return launch(
            order,
            kernel,
            [kept] + [array for array, _, _, _ in adds],
            in_specs=[pl.BlockSpec((rows, tile), lambda f: (0, f))]
            + [add_spec(group, first >= 0, n) for _, group, first, n in adds],
            out_shape=out_shape,
            grid=(grid,),
            out_specs=out_spec,
            compiler_params=WHOLE,
            cost_estimate=cost(rows * width * len(adds), rows * width * (8 + 2 * each)),
        )


def true_rows(tok_dev):
    size = lax.axis_size("fsdp")
    block = jnp.arange(size, dtype=jnp.int32) ^ lax.axis_index("fsdp")
    return (block[:, None] * tok_dev + jnp.arange(tok_dev, dtype=jnp.int32)[None, :]).reshape(-1)


def tree_tables(parent_row, length_row, places):
    segments = parent_row.shape[0]
    labels = jnp.arange(segments, dtype=jnp.int32)
    before = labels[:, None] >= labels[None, :]
    ends = jnp.sum(jnp.where(before, length_row[None, :], 0), axis=1)
    starts = ends - length_row
    segment_of = jnp.sum((places[:, None] >= ends[None, :]).astype(jnp.int32), axis=1)
    member = segment_of[:, None] == labels[None, :]
    reach = ((labels[:, None] == labels[None, :]) | (parent_row[:, None] == labels[None, :])).astype(F32)
    steps = 1
    while steps < segments - 1:
        reach = (jnp.dot(reach, reach) > 0.5).astype(F32)
        steps *= 2
    ancestry = reach > 0.5
    above = jnp.sum(jnp.where(ancestry, length_row[None, :], 0), axis=1) - length_row
    moved = jnp.sum(jnp.where(member, (above - starts)[None, :], 0), axis=1)
    position = (places + moved).astype(F32)
    member_f = member.astype(F32)
    near = jnp.dot(jnp.dot(member_f, reach), member_f.T) > 0.5
    visible = near & (places[None, :] <= places[:, None])
    freq = ROPE_BASE ** (-jnp.arange(0, HD, 2, dtype=F32) / HD)
    angle = position[:, None] * freq[None, :]
    cos_half, sin_half = jnp.cos(angle), jnp.sin(angle)
    return (
        jnp.where(visible, 0.0, -1e30).astype(F32),
        jnp.concatenate([cos_half, cos_half], axis=1),
        jnp.concatenate([-sin_half, sin_half], axis=1),
    )


def on_device(
    tokens,
    cotangent,
    parents,
    lengths,
    qkv_weight,
    out_weight,
    gate_up_weight,
    down_weight,
    qk_gain,
    post_gain,
):
    micro, tok_dev, model_width = tokens.shape
    local_width = qkv_weight.shape[2]
    size = lax.axis_size("fsdp")
    replicas = lax.axis_size("replica")
    tok = micro * tok_dev
    rows = tok * size
    far = replicas // 2
    places = true_rows(tok_dev)
    x_rows = tokens.reshape(tok, model_width)
    grad_rows = cotangent.reshape(tok, model_width)
    order = Order()
    x_blocks = gather_blocks(x_rows)
    tables = [tree_tables(parents[m, 0], lengths[m, 0], places) for m in range(micro)]
    raw, values, squares, x_full = project(order, x_blocks, qkv_weight)
    context, queries, keys, inv, *attn_blocks = attend(
        order, raw, values, gather_blocks(squares), tables, qk_gain, out_weight
    )
    attn, hidden, hidden_b = after_attention(order, swap_blocks(attn_blocks), x_rows, post_gain)
    hidden_blocks = gather_blocks(hidden_b)
    far_hidden_blocks = gather_blocks(exchange(hidden_b, "replica", far))
    gate_up, swiglu, hidden_full, *mlp_blocks = mlp_forward(
        order, hidden_blocks, gate_up_weight, down_weight
    )
    order.extend(far_hidden_blocks[1:])
    mlp_blocks = gate(order, mlp_blocks)
    out_rows, d_mlp, mlp_gain_sum = after_mlp(
        order, swap_blocks(mlp_blocks), hidden, grad_rows, post_gain
    )
    d_mlp_blocks = gather_blocks(d_mlp)
    far_d_mlp_blocks = gather_blocks(exchange(d_mlp, "replica", far))
    d_gate_up, d_mlp_full, *d_hidden_blocks = mlp_back(
        order, d_mlp_blocks, gate_up, gate_up_weight, down_weight
    )
    d_hidden_parts = swap_blocks(d_hidden_blocks)
    fence(order, far_d_mlp_blocks[1:])
    far_d_gate_up, far_swiglu, far_d_mlp, far_hidden = mlp_units(
        order, far_hidden_blocks, far_d_mlp_blocks, gate_up_weight, down_weight
    )
    gate_up_sum = OwnersSum(
        order, [(hidden_full, d_gate_up, 0, rows), (far_hidden, far_d_gate_up, 0, rows)], far
    )
    d_hidden, d_attn, attn_gain_sum = before_attention(
        order, d_hidden_parts, grad_rows, attn, post_gain
    )
    d_attn_blocks = gather_blocks(d_attn)
    order.pace = 100
    down_sum = OwnersSum(
        order, [(d_mlp_full, swiglu[None], 0, rows), (far_d_mlp, far_swiglu[None], 0, rows)], far
    )
    order.pace = 0.001
    gate_up_sum.step(order)
    gain_rows = jnp.concatenate([attn_gain_sum, mlp_gain_sum], axis=0)
    me = lax.axis_index("fsdp")
    split = gain_rows.reshape(2, size, local_width)
    post_rows = lax.dynamic_index_in_dim(split, me, 1, keepdims=False)
    for flip in range(1, size):
        sent = lax.dynamic_index_in_dim(split, me ^ flip, 1, keepdims=False)
        post_rows = post_rows + exchange(sent, "fsdp", flip)
    order.append(post_rows)
    order.pace = 100
    d_attn_full, d_norm, d_values, sums, qk_gain_sums = attend_back(
        order, d_attn_blocks, out_weight, queries, keys, values, raw, inv, tables, qk_gain
    )
    order.pace = 0.001
    sums_parts = gather_blocks(sums)
    down_sum.step(order)
    d_projected, *input_blocks = project_back(
        order, d_norm, d_values, raw, inv, sums_parts, qk_gain, qkv_weight
    )
    order.append(gate_up_sum.latest())
    qkv_sum = OwnersSum(order, [(x_full, d_projected, 0, rows)], replicas, 3)
    out_sum = OwnersSum(order, [(d_attn_full, context[None], 0, rows)], replicas)
    order.append(down_sum.latest())
    order.pace = 100
    out_sum.step(order)
    qkv_sum.step(order)
    gate_up_grad = gate_up_sum.finish(order, 2, False)
    down_grad = down_sum.finish(order, 1, True)
    order.pace = 1
    out_sum.step(order)
    qkv_sum.step(order)
    gains = jnp.concatenate([qk_gain_sums, post_rows], axis=0)
    gains = gains + exchange(gains, "replica", 1)
    [gains] = gate(order, [gains])
    flip = 2
    while flip < far:
        gains = gains + exchange(gains, "replica", flip)
        flip *= 2
    order.append(gains)
    out_grad = out_sum.finish(order, 1, True)
    gains = gains + exchange(gains, "replica", far)
    qkv_grad = qkv_sum.finish(order, 3, False)
    input_grad = d_hidden + sum(part.astype(F32) for part in swap_blocks(input_blocks))
    return (
        out_rows.reshape(micro, tok_dev, model_width),
        input_grad.reshape(micro, tok_dev, model_width),
        qkv_grad,
        out_grad,
        gate_up_grad,
        down_grad,
        gains[:2],
        gains[2:],
    )


def solution(mesh):
    in_specs = (
        P(None, ("replica", "fsdp"), None),
        P(None, ("replica", "fsdp"), None),
        P(None, "replica", None),
        P(None, "replica", None),
        P(None, None, "fsdp"),
        P("fsdp", None),
        P(None, None, "fsdp"),
        P("fsdp", None),
        P(None, "fsdp"),
        P(),
    )
    out_specs = (
        P(None, ("replica", "fsdp"), None),
        P(None, ("replica", "fsdp"), None),
        P(None, "replica", "fsdp"),
        P("fsdp", "replica"),
        P(None, "replica", "fsdp"),
        P("fsdp", "replica"),
        P(None, "fsdp"),
        P(None, "fsdp"),
    )
    return jax.shard_map(
        on_device, mesh=mesh, in_specs=in_specs, out_specs=out_specs, check_vma=False
    )
```

```python
import jax
import jax.numpy as jnp
from jax import lax
from jax.experimental import pallas as pl
from jax.experimental.pallas import tpu as pltpu
from jax.sharding import PartitionSpec as P

HD = 128


EPSILON = 1e-06
ROPE_BASE = 500000.0
BF = jnp.bfloat16
F32 = jnp.float32


def exchange(value, axis, flip):
    size = lax.axis_size(axis)
    return lax.ppermute(value, axis, [(i, i ^ flip) for i in range(size)])


def gather_blocks(rows):
    return [rows] + [exchange(rows, "fsdp", flip) for flip in range(1, lax.axis_size("fsdp"))]


def swap_blocks(blocks):
    return [blocks[0]] + [exchange(blocks[flip], "fsdp", flip) for flip in range(1, len(blocks))]


def cost(flops, moved, transcendentals=0):
    return (flops, moved, transcendentals)


class Order(list):
    pace = 0.001


def shape(dims, kind):
    return jax.ShapeDtypeStruct(dims, kind)


def dot(left, right):
    return jnp.dot(left, right, preferred_element_type=F32)


def dot_t(left, right):
    return lax.dot_general(left, right, (((1,), (1,)), ((), ())), preferred_element_type=F32)


def t_dot(left, right):
    return lax.dot_general(left, right, (((0,), (0,)), ((), ())), preferred_element_type=F32)


def lane_sums(field):
    ones = jnp.ones((8, field.shape[1]), F32)
    return lax.dot_general(
        ones,
        field,
        (((1,), (1,)), ((), ())),
        precision=lax.Precision.HIGHEST,
        preferred_element_type=F32,
    )


def join(block_refs, rows_ref):
    tok = block_refs[0].shape[0]
    for j, block_ref in enumerate(block_refs):
        rows_ref[pl.ds(j * tok, tok), :] = block_ref[...]


def write_blocks(rows, block_refs):
    tok = block_refs[0].shape[0]
    for j, block_ref in enumerate(block_refs):
        block_ref[...] = rows[j * tok : (j + 1) * tok].astype(block_ref.dtype)


def block_shapes(count, tok, width):
    return [shape((tok, width), F32)] + [shape((tok, width), BF)] * (count - 1)


def aligned_total(parts, tok):
    total = parts[0].T
    count = len(parts)
    for flip in range(1, count):
        column = parts[flip].T
        total = total + jnp.concatenate(
            [column[(j ^ flip) * tok : ((j ^ flip) + 1) * tok] for j in range(count)], axis=0
        )
    return total


def turn(field, cos_t, sin_t):
    return field * cos_t + pltpu.roll(field, HD // 2, 1) * sin_t


def turn_back(field, cos_t, sin_t):
    return field * cos_t - pltpu.roll(field, HD // 2, 1) * sin_t


VMEM = pl.BlockSpec(memory_space=pltpu.VMEM)
WHOLE = pltpu.CompilerParams(dimension_semantics=("arbitrary",))


def launch(
    order, kernel, args, in_specs, grid_spec=None, *, cost_estimate, pace=None, **settings
):
    waits = list(order)
    count = len(args)

    def body(*refs):
        kernel(*refs[:count], *refs[count + len(waits) :])

    flops, moved, transcendentals = [
        int(part * (order.pace if pace is None else pace)) for part in cost_estimate
    ]
    settings["cost_estimate"] = pl.CostEstimate(
        flops=flops, bytes_accessed=moved, transcendentals=transcendentals
    )
    specs = list(in_specs) + [pl.BlockSpec(memory_space=pl.ANY)] * len(waits)
    if grid_spec is None:
        settings["in_specs"] = specs
    else:
        settings["grid_spec"] = grid_spec(specs)
    settings["name"] = kernel.__qualname__.split(".<")[0].replace(".", "_")
    results = pl.pallas_call(body, **settings)(*args, *waits)
    order[:] = [results[0] if isinstance(results, (list, tuple)) else results]
    return results


def fence(order, arrays):
    order.extend(arrays)

    def kernel(out_ref):
        out_ref[...] = jnp.zeros((8, HD), F32)

    launch(
        order,
        kernel,
        [],
        in_specs=[],
        out_shape=shape((8, HD), F32),
        out_specs=VMEM,
        cost_estimate=cost(1 << 40, 1 << 30),
        pace=1,
    )


def gate(order, arrays):
    def kernel(*refs):
        pass

    held = pl.BlockSpec(memory_space=pl.ANY)
    return launch(
        order,
        kernel,
        arrays,
        in_specs=[held] * len(arrays),
        out_shape=[shape(array.shape, array.dtype) for array in arrays],
        out_specs=[held] * len(arrays),
        input_output_aliases={k: k for k in range(len(arrays))},
        cost_estimate=cost(0, 1000),
    )


def project(order, x_blocks, qkv_weight):
    count = len(x_blocks)
    tok, model_width = x_blocks[0].shape
    rows = count * tok
    width = qkv_weight.shape[2]

    def kernel(*refs):
        x_refs = refs[:count]
        weight_ref, raw_ref, values_ref, squares_ref, x_ref = refs[count:]
        step = pl.program_id(0)

        @pl.when(step == 0)
        def _():
            join(x_refs, x_ref)

        product = dot(x_ref[...], weight_ref[...])

        @pl.when(step < 2)
        def _():
            raw_ref[...] = product
            squares_ref[pl.ds(step, 1), :] = lane_sums(product * product)[:1]

        @pl.when(step == 2)
        def _():
            values_ref[...] = product.astype(BF)
            squares_ref[2:, :] = jnp.zeros((6, rows), F32)

    whole = pl.BlockSpec((tok, model_width), lambda n: (0, 0))
    return launch(
        order,
        kernel,
        [*x_blocks, qkv_weight],
        out_shape=[
            shape((2, rows, width), F32),
            shape((rows, width), BF),
            shape((8, rows), F32),
            shape((rows, model_width), BF),
        ],
        grid=(3,),
        in_specs=[whole] * count + [pl.BlockSpec((None, model_width, width), lambda n: (n, 0, 0))],
        out_specs=[
            pl.BlockSpec((None, rows, width), lambda n: (jnp.minimum(n, 1), 0, 0)),
            pl.BlockSpec((rows, width), lambda n: (0, 0)),
            pl.BlockSpec((8, rows), lambda n: (0, 0)),
            pl.BlockSpec((rows, model_width), lambda n: (0, 0)),
        ],
        compiler_params=WHOLE,
        cost_estimate=cost(6 * rows * model_width * width, 6 * model_width * width + 8 * rows * width),
    )


def pick(field, m, each, tok, at):
    return jnp.concatenate(
        [
            field[j * tok + m * each : j * tok + (m + 1) * each, at]
            for j in range(field.shape[0] // tok)
        ],
        axis=0,
    )


def place(ref, m, each, tok, at, rows):
    for j in range(ref.shape[0] // tok):
        ref[pl.ds(j * tok + m * each, each), at] = rows[j * each : (j + 1) * each]


def attend(order, raw, values, squares, tables, qk_gain, out_weight):
    count = len(squares)
    micro = len(tables)
    _, rows, width = raw.shape
    heads = width // HD
    tok = rows // count
    each = tok // micro
    pack = rows // micro
    model_width = out_weight.shape[1]
    total_width = model_width
    scale = HD ** (-0.5)

    def kernel(raw_ref, values_ref, gain_ref, out_weight_ref, *refs):
        table_refs = refs[: 3 * micro]
        parts = [ref[...] for ref in refs[3 * micro : 3 * micro + count]]
        refs = refs[3 * micro + count :]
        context_ref, queries_ref, keys_ref, inv_ref = refs[:4]
        block_refs = refs[4:]
        inv = lax.rsqrt(aligned_total(parts, tok) / total_width + EPSILON)
        inv_ref[...] = inv
        for m in range(micro):
            bias_v, cos_v, sin_v = [ref[...] for ref in table_refs[3 * m : 3 * m + 3]]
            inv_q = pick(inv, m, each, tok, slice(0, 1))
            inv_k = pick(inv, m, each, tok, slice(1, 2))
            own = slice(m * pack, (m + 1) * pack)
            for h in range(heads):
                at = slice(h * HD, (h + 1) * HD)
                q_raw = pick(raw_ref.at[0], m, each, tok, at)
                k_raw = pick(raw_ref.at[1], m, each, tok, at)
                q = turn(q_raw * inv_q * gain_ref[0:1, at], cos_v, sin_v).astype(BF)
                k = turn(k_raw * inv_k * gain_ref[1:2, at], cos_v, sin_v).astype(BF)
                queries_ref[own, at] = q
                keys_ref[own, at] = k
                scores = dot_t(q, k) * scale + bias_v
                weights = jnp.exp(scores - jnp.max(scores, axis=1, keepdims=True))
                probs = (weights / jnp.sum(weights, axis=1, keepdims=True)).astype(BF)
                context = dot(probs, pick(values_ref, m, each, tok, at)).astype(BF)
                place(context_ref, m, each, tok, at, context)
        write_blocks(dot(context_ref[...], out_weight_ref[...]), block_refs)

    return launch(
        order,
        kernel,
        [raw, values, qk_gain, out_weight, *[t for table in tables for t in table], *squares],
        out_shape=[
            shape((rows, width), BF),
            shape((rows, width), BF),
            shape((rows, width), BF),
            shape((rows, 8), F32),
        ]
        + block_shapes(count, tok, model_width),
        in_specs=[VMEM] * (4 + 3 * micro + count),
        out_specs=[VMEM] * (4 + count),
        cost_estimate=cost(
            4 * rows * pack * width + 2 * rows * width * model_width,
            2 * width * model_width + 14 * rows * width + 2 * rows * model_width,
            heads * rows * pack,
        ),
    )


def attend_back(order, d_attn_blocks, out_weight, queries, keys, values, raw, inv, tables, qk_gain):
    count = len(d_attn_blocks)
    micro = len(tables)
    tok, model_width = d_attn_blocks[0].shape
    _, rows, width = raw.shape
    heads = width // HD
    each = tok // micro
    pack = rows // micro
    scale = HD ** (-0.5)

    def kernel(*refs):
        block_refs = refs[:count]
        table_refs = refs[count : count + 3 * micro]
        (
            out_weight_ref,
            queries_ref,
            keys_ref,
            values_ref,
            raw_ref,
            inv_ref,
            gain_ref,
            d_attn_ref,
            d_norm_ref,
            d_values_ref,
            sums_ref,
            gain_sums_ref,
        ) = refs[count + 3 * micro :]
        join(block_refs, d_attn_ref)
        d_context = dot_t(d_attn_ref[...], out_weight_ref[...]).astype(BF)
        inv = inv_ref[...]
        sums = [[], []]
        gain_sums_ref[...] = jnp.zeros((2, width), F32)
        for m in range(micro):
            bias_v, cos_v, sin_v = [ref[...] for ref in table_refs[3 * m : 3 * m + 3]]
            invs = [pick(inv, m, each, tok, slice(n, n + 1)) for n in range(2)]
            own = slice(m * pack, (m + 1) * pack)
            totals = [jnp.zeros((pack, HD), F32), jnp.zeros((pack, HD), F32)]
            for h in range(heads):
                at = slice(h * HD, (h + 1) * HD)
                q, k = queries_ref[own, at], keys_ref[own, at]
                v = pick(values_ref, m, each, tok, at)
                d_out = pick(d_context, m, each, tok, at)
                scores = dot_t(q, k) * scale + bias_v
                weights = jnp.exp(scores - jnp.max(scores, axis=1, keepdims=True))
                probs = weights / jnp.sum(weights, axis=1, keepdims=True)
                d_probs = dot_t(d_out, v)
                delta = jnp.sum(d_probs * probs, axis=1, keepdims=True)
                d_scores = (probs * (d_probs - delta)).astype(BF)
                d_values = t_dot(probs.astype(BF), d_out).astype(BF)
                place(d_values_ref, m, each, tok, at, d_values)
                turned = (dot(d_scores, k) * scale, t_dot(d_scores, q) * scale)
                for n in range(2):
                    d_norm = turn_back(turned[n], cos_v, sin_v)
                    place(d_norm_ref.at[n], m, each, tok, at, d_norm)
                    field = pick(raw_ref.at[n], m, each, tok, at) * d_norm
                    totals[n] += field * gain_ref[n : n + 1, at]
                    gain_sums_ref[n : n + 1, at] += jnp.sum(field * invs[n], axis=0, keepdims=True)
            for n in range(2):
                sums[n].append(totals[n])
        for n in range(2):
            ordered = [
                sums[n][m][j * each : (j + 1) * each] for j in range(count) for m in range(micro)
            ]
            sums_ref[n : n + 1, :] = lane_sums(jnp.concatenate(ordered, axis=0))[:1]
        sums_ref[2:, :] = jnp.zeros((6, rows), F32)

    return launch(
        order,
        kernel,
        [
            *d_attn_blocks,
            *[t for table in tables for t in table],
            out_weight,
            queries,
            keys,
            values,
            raw,
            inv,
            qk_gain,
        ],
        out_shape=[
            shape((rows, model_width), BF),
            shape((2, rows, width), F32),
            shape((rows, width), BF),
            shape((8, rows), F32),
            shape((2, width), F32),
        ],
        in_specs=[VMEM] * (7 + 3 * micro + count),
        out_specs=[VMEM] * 5,
        cost_estimate=cost(
            10 * rows * pack * width + 2 * rows * width * model_width,
            2 * width * model_width + 24 * rows * width + 2 * rows * model_width,
            heads * rows * pack,
        ),
    )


def project_back(order, d_norm, d_values, raw, inv, sums, qk_gain, qkv_weight):
    count = len(sums)
    _, rows, width = raw.shape
    tok = rows // count
    model_width = qkv_weight.shape[1]

    def kernel(d_norm_ref, d_values_ref, raw_ref, inv_ref, gain_ref, weight_ref, *refs):
        parts = refs[:count]
        d_projected_ref = refs[count]
        block_refs = refs[count + 1 : 2 * count + 1]
        total_ref = refs[2 * count + 1]
        step = pl.program_id(0)
        inv = inv_ref[...]

        @pl.when(step == 0)
        def _():
            d_projected_ref[...] = d_values_ref[...]

        @pl.when(step > 0)
        def _():
            shared = aligned_total([part[...] for part in parts], tok)
            first = step == 1
            r = jnp.where(first, inv[:, 0:1], inv[:, 1:2])
            s = jnp.where(first, shared[:, 0:1], shared[:, 1:2])
            gain = jnp.where(first, gain_ref[0:1, :], gain_ref[1:2, :])
            d_projected_ref[...] = (
                r * (d_norm_ref[...] * gain) - raw_ref[...] * (r * r * r * s / model_width)
            ).astype(BF)

        product = dot_t(d_projected_ref[...], weight_ref[...])

        @pl.when(step == 0)
        def _():
            total_ref[...] = product

        @pl.when(step > 0)
        def _():
            total_ref[...] += product

        @pl.when(step == 2)
        def _():
            write_blocks(total_ref[...], block_refs)

    def part_at(n):
        return lax.rem(n + 2, 3)

    field = pl.BlockSpec((None, rows, width), lambda n: (jnp.maximum(n - 1, 0), 0, 0))
    return launch(
        order,
        kernel,
        [d_norm, d_values, raw, inv, qk_gain, qkv_weight, *sums],
        out_shape=[shape((3, rows, width), BF)] + block_shapes(count, tok, model_width),
        grid=(3,),
        in_specs=[
            field,
            pl.BlockSpec((rows, width), lambda n: (0, 0)),
            field,
            pl.BlockSpec((rows, 8), lambda n: (0, 0)),
            pl.BlockSpec((2, width), lambda n: (0, 0)),
            pl.BlockSpec((None, model_width, width), lambda n: (part_at(n), 0, 0)),
        ]
        + [pl.BlockSpec((8, rows), lambda n: (0, 0))] * count,
        out_specs=[pl.BlockSpec((None, rows, width), lambda n: (part_at(n), 0, 0))]
        + [pl.BlockSpec((tok, model_width), lambda n: (0, 0))] * count,
        scratch_shapes=[pltpu.VMEM((rows, model_width), F32)],
        compiler_params=WHOLE,
        cost_estimate=cost(
            6 * rows * model_width * width, 6 * model_width * width + 22 * rows * width + 2 * rows * model_width
        ),
    )


def mlp_forward(order, hidden_blocks, gate_up_weight, down_weight):
    count = len(hidden_blocks)
    tok, model_width = hidden_blocks[0].shape
    rows = count * tok
    units = down_weight.shape[0]
    tile = min(512, units)
    last = units // tile - 1

    def kernel(*refs):
        gate_w_ref, up_w_ref, down_w_ref, gate_up_ref, swiglu_ref, hidden_ref = refs[
            count : count + 6
        ]
        block_refs = refs[count + 6 : 2 * count + 6]
        total_ref = refs[2 * count + 6]
        step = pl.program_id(0)

        @pl.when(step == 0)
        def _():
            join(refs[:count], hidden_ref)

        gate = dot(hidden_ref[...], gate_w_ref[...])
        up = dot(hidden_ref[...], up_w_ref[...])
        swiglu = (gate * jax.nn.sigmoid(gate) * up).astype(BF)
        gate_up_ref[0] = gate.astype(BF)
        gate_up_ref[1] = up.astype(BF)
        swiglu_ref[...] = swiglu
        product = dot(swiglu, down_w_ref[...])

        @pl.when(step == 0)
        def _():
            total_ref[...] = product

        @pl.when(step > 0)
        def _():
            total_ref[...] += product

        @pl.when(step == last)
        def _():
            write_blocks(total_ref[...], block_refs)

    field = pl.BlockSpec((rows, tile), lambda f: (0, f))
    return launch(
        order,
        kernel,
        [*hidden_blocks, gate_up_weight, gate_up_weight, down_weight],
        out_shape=[
            shape((2, rows, units), BF),
            shape((rows, units), BF),
            shape((rows, model_width), BF),
        ]
        + block_shapes(count, tok, model_width),
        grid=(units // tile,),
        in_specs=[pl.BlockSpec((tok, model_width), lambda f: (0, 0))] * count
        + [
            pl.BlockSpec((None, model_width, tile), lambda f: (0, 0, f)),
            pl.BlockSpec((None, model_width, tile), lambda f: (1, 0, f)),
            pl.BlockSpec((tile, model_width), lambda f: (f, 0)),
        ],
        out_specs=[pl.BlockSpec((2, rows, tile), lambda f: (0, 0, f)), field]
        + [pl.BlockSpec((rows, model_width), lambda f: (0, 0))]
        + [pl.BlockSpec((tok, model_width), lambda f: (0, 0))] * count,
        scratch_shapes=[pltpu.VMEM((rows, model_width), F32)],
        compiler_params=WHOLE,
        cost_estimate=cost(
            6 * rows * model_width * units,
            6 * model_width * units + 6 * rows * units + 8 * rows * model_width,
            rows * units,
        ),
    )


def unit_grads(gate, up, d_swiglu):
    sigmoid = jax.nn.sigmoid(gate)
    d_gate = d_swiglu * up * sigmoid * (1.0 + gate * (1.0 - sigmoid))
    return (d_gate.astype(BF), (d_swiglu * (gate * sigmoid)).astype(BF))


def mlp_back(order, d_mlp_blocks, gate_up, gate_up_weight, down_weight):
    count = len(d_mlp_blocks)
    tok, model_width = d_mlp_blocks[0].shape
    rows = count * tok
    units = down_weight.shape[0]
    tile = min(512, units)
    last = units // tile - 1

    def kernel(*refs):
        gate_up_ref, gate_w_ref, up_w_ref, down_w_ref, d_gate_up_ref, d_mlp_ref = refs[
            count : count + 6
        ]
        block_refs = refs[count + 6 : 2 * count + 6]
        total_ref = refs[2 * count + 6]
        step = pl.program_id(0)

        @pl.when(step == 0)
        def _():
            join(refs[:count], d_mlp_ref)

        d_swiglu = dot_t(d_mlp_ref[...], down_w_ref[...])
        d_gate, d_up = unit_grads(gate_up_ref[0].astype(F32), gate_up_ref[1].astype(F32), d_swiglu)
        d_gate_up_ref[0] = d_gate
        d_gate_up_ref[1] = d_up
        product = dot_t(d_gate, gate_w_ref[...]) + dot_t(d_up, up_w_ref[...])

        @pl.when(step == 0)
        def _():
            total_ref[...] = product

        @pl.when(step > 0)
        def _():
            total_ref[...] += product

        @pl.when(step == last)
        def _():
            write_blocks(total_ref[...], block_refs)

    field = pl.BlockSpec((2, rows, tile), lambda f: (0, 0, f))
    return launch(
        order,
        kernel,
        [*d_mlp_blocks, gate_up, gate_up_weight, gate_up_weight, down_weight],
        out_shape=[shape((2, rows, units), BF), shape((rows, model_width), BF)]
        + block_shapes(count, tok, model_width),
        grid=(units // tile,),
        in_specs=[pl.BlockSpec((tok, model_width), lambda f: (0, 0))] * count
        + [
            field,
            pl.BlockSpec((None, model_width, tile), lambda f: (0, 0, f)),
            pl.BlockSpec((None, model_width, tile), lambda f: (1, 0, f)),
            pl.BlockSpec((tile, model_width), lambda f: (f, 0)),
        ],
        out_specs=[field]
        + [pl.BlockSpec((rows, model_width), lambda f: (0, 0))]
        + [pl.BlockSpec((tok, model_width), lambda f: (0, 0))] * count,
        scratch_shapes=[pltpu.VMEM((rows, model_width), F32)],
        compiler_params=WHOLE,
        cost_estimate=cost(
            6 * rows * model_width * units,
            6 * model_width * units + 8 * rows * units + 8 * rows * model_width,
            rows * units,
        ),
    )


def mlp_units(order, hidden_blocks, d_mlp_blocks, gate_up_weight, down_weight):
    count = len(d_mlp_blocks)
    tok, model_width = d_mlp_blocks[0].shape
    rows = count * tok
    units = down_weight.shape[0]
    tile = min(256, units)

    def kernel(*refs):
        gate_w_ref, up_w_ref, down_w_ref = refs[2 * count : 2 * count + 3]
        d_gate_up_ref, swiglu_ref, d_mlp_ref, hidden_ref = refs[2 * count + 3 :]

        @pl.when(pl.program_id(0) == 0)
        def _():
            join(refs[:count], hidden_ref)
            join(refs[count : 2 * count], d_mlp_ref)

        gate = dot(hidden_ref[...], gate_w_ref[...])
        up = dot(hidden_ref[...], up_w_ref[...])
        d_gate, d_up = unit_grads(gate, up, dot_t(d_mlp_ref[...], down_w_ref[...]))
        swiglu_ref[...] = (gate * jax.nn.sigmoid(gate) * up).astype(BF)
        d_gate_up_ref[0] = d_gate
        d_gate_up_ref[1] = d_up

    return launch(
        order,
        kernel,
        [*hidden_blocks, *d_mlp_blocks, gate_up_weight, gate_up_weight, down_weight],
        out_shape=[
            shape((2, rows, units), BF),
            shape((rows, units), BF),
            shape((rows, model_width), BF),
            shape((rows, model_width), BF),
        ],
        grid=(units // tile,),
        in_specs=[pl.BlockSpec((tok, model_width), lambda f: (0, 0))] * (2 * count)
        + [
            pl.BlockSpec((None, model_width, tile), lambda f: (0, 0, f)),
            pl.BlockSpec((None, model_width, tile), lambda f: (1, 0, f)),
            pl.BlockSpec((tile, model_width), lambda f: (f, 0)),
        ],
        out_specs=[
            pl.BlockSpec((2, rows, tile), lambda f: (0, 0, f)),
            pl.BlockSpec((rows, tile), lambda f: (0, f)),
            pl.BlockSpec((rows, model_width), lambda f: (0, 0)),
            pl.BlockSpec((rows, model_width), lambda f: (0, 0)),
        ],
        compiler_params=WHOLE,
        cost_estimate=cost(
            6 * rows * model_width * units,
            6 * rows * model_width + 6 * model_width * units + 6 * rows * units,
            rows * units,
        ),
    )


def sum_parts(part_refs):
    total = part_refs[0][...].astype(F32)
    for part_ref in part_refs[1:]:
        total += part_ref[...].astype(F32)
    return total


def norm_back(field, gain, upstream):
    width = field.shape[1]
    inv = lax.rsqrt(jnp.sum(field * field, axis=1, keepdims=True) / width + EPSILON)
    weighted = upstream * gain
    shared = jnp.sum(field * weighted, axis=1, keepdims=True)
    gain_sum = jnp.sum(upstream * field * inv, axis=0, keepdims=True)
    return (inv * weighted - field * (inv * inv * inv * shared / width), gain_sum)


def after_attention(order, parts, x_rows, post_gain):
    tok, width = x_rows.shape
    count = len(parts)

    def kernel(*refs):
        x_ref, gain_ref, attn_ref, hidden_ref, rounded_ref = refs[count:]
        attn = sum_parts(refs[:count])
        inv = lax.rsqrt(jnp.sum(attn * attn, axis=1, keepdims=True) / width + EPSILON)
        hidden = x_ref[...].astype(F32) + attn * inv * gain_ref[0:1, :]
        attn_ref[...] = attn
        hidden_ref[...] = hidden
        rounded_ref[...] = hidden.astype(BF)

    return launch(
        order,
        kernel,
        [*parts, x_rows, post_gain],
        out_shape=[shape((tok, width), F32), shape((tok, width), F32), shape((tok, width), BF)],
        in_specs=[VMEM] * (count + 2),
        out_specs=[VMEM] * 3,
        cost_estimate=cost(8 * tok * width, 24 * tok * width),
    )


def after_mlp(order, parts, hidden, grad_rows, post_gain):
    tok, width = hidden.shape
    count = len(parts)

    def kernel(*refs):
        hidden_ref, grad_ref, gain_ref, out_ref, d_mlp_ref, gain_sum_ref = refs[count:]
        mlp = sum_parts(refs[:count])
        gain = gain_ref[1:2, :]
        inv = lax.rsqrt(jnp.sum(mlp * mlp, axis=1, keepdims=True) / width + EPSILON)
        out_ref[...] = hidden_ref[...] + mlp * inv * gain
        d_mlp, gain_sum = norm_back(mlp, gain, grad_ref[...].astype(F32))
        d_mlp_ref[...] = d_mlp.astype(BF)
        gain_sum_ref[...] = gain_sum

    return launch(
        order,
        kernel,
        [*parts, hidden, grad_rows, post_gain],
        out_shape=[shape((tok, width), F32), shape((tok, width), BF), shape((1, width), F32)],
        in_specs=[VMEM] * (count + 3),
        out_specs=[VMEM] * 3,
        cost_estimate=cost(16 * tok * width, 24 * tok * width),
    )


def before_attention(order, parts, grad_rows, attn, post_gain):
    tok, width = attn.shape
    count = len(parts)

    def kernel(*refs):
        grad_ref, attn_ref, gain_ref, d_hidden_ref, d_attn_ref, gain_sum_ref = refs[count:]
        d_hidden = grad_ref[...].astype(F32) + sum_parts(refs[:count])
        d_hidden_ref[...] = d_hidden
        d_attn, gain_sum = norm_back(attn_ref[...], gain_ref[0:1, :], d_hidden)
        d_attn_ref[...] = d_attn.astype(BF)
        gain_sum_ref[...] = gain_sum

    return launch(
        order,
        kernel,
        [*parts, grad_rows, attn, post_gain],
        out_shape=[shape((tok, width), F32), shape((tok, width), BF), shape((1, width), F32)],
        in_specs=[VMEM] * (count + 3),
        out_specs=[VMEM] * 3,
        cost_estimate=cost(16 * tok * width, 24 * tok * width),
    )


def send_order(top):
    def halves(codes, bit):
        if len(codes) == 1:
            return codes
        return halves([c for c in codes if c & bit], 2 * bit) + halves(
            [c for c in codes if not c & bit], 2 * bit
        )

    stages = []
    bit = 1
    while bit < top:
        stages.append((bit, [bit + c for c in halves(list(range(0, top, 2 * bit)), 2 * bit)]))
        bit *= 2
    return stages


def grad_rows_of(order, splits, sets):
    codes = [code for split in splits for code in split]
    blocks = len(codes)
    replicas = lax.axis_size("replica")
    picks = lax.axis_index("replica") ^ jnp.array(codes, jnp.int32)
    block = sets[0][0].shape[1] // replicas
    planes, _, units = sets[0][1].shape
    tile = min(512, units)
    tiles = units // tile
    width = planes * units
    depth = sum(rows for _, _, _, rows in sets)
    count = len(sets)
    kinds = [BF] * (len(splits) - 1) + [F32]

    def kernel(picks_ref, *refs):
        left_refs = refs[: count * blocks]
        right_refs = refs[count * blocks : count * blocks + count]
        out_refs = refs[count * blocks + count : count * blocks + count + len(splits)]
        turned_ref, right_ref = refs[count * blocks + count + len(splits) :]

        @pl.when(pl.program_id(0) == 0)
        def _():
            at = 0
            for k, (_, _, _, rows) in enumerate(sets):
                for b in range(blocks):
                    turned_ref[pl.ds(b * block, block), pl.ds(at, rows)] = left_refs[k * blocks + b][
                        ...
                    ].T
                at += rows

        at = 0
        for k, (_, _, _, rows) in enumerate(sets):
            right_ref[pl.ds(at, rows), :] = right_refs[k][...]
            at += rows
        first = 0
        for split, out_ref in zip(splits, out_refs):
            rows = len(split) * block
            out_ref[...] = dot(turned_ref[pl.ds(first, rows), :], right_ref[...]).astype(out_ref.dtype)
            first += rows

    in_specs = [
        pl.BlockSpec((rows, block), lambda f, picks_ref, group=group, b=b: (group, picks_ref[b]))
        for _, _, group, rows in sets
        for b in range(blocks)
    ] + [
        pl.BlockSpec(
            (None, rows, tile),
            lambda f, picks_ref, group=group: (lax.div(f, tiles), group, lax.rem(f, tiles)),
        )
        for _, _, group, rows in sets
    ]
    return launch(
        order,
        kernel,
        [picks]
        + [left for left, _, _, _ in sets for _ in range(blocks)]
        + [right for _, right, _, _ in sets],
        in_specs,
        lambda specs: pltpu.PrefetchScalarGridSpec(
            num_scalar_prefetch=1,
            grid=(planes * tiles,),
            in_specs=specs,
            out_specs=[
                pl.BlockSpec((len(split) * block, tile), lambda f, picks_ref: (0, f))
                for split in splits
            ],
            scratch_shapes=[
                pltpu.VMEM((blocks * block, depth), BF),
                pltpu.VMEM((depth, tile), BF),
            ],
        ),
        out_shape=[shape((len(split) * block, width), kind) for split, kind in zip(splits, kinds)],
        compiler_params=WHOLE,
        cost_estimate=cost(
            2 * depth * blocks * block * width,
            2 * depth * (blocks * block + width) + 2 * blocks * block * width,
        ),
    )


def add_parts(order, own, adds, column, width):
    rows = own.shape[0]
    tile = min(2048, width)
    tiles = width // tile

    def kernel(own_ref, *refs):
        refs[-1][...] = sum_parts([own_ref, *refs[:-1]]).astype(BF)

    return launch(
        order,
        kernel,
        [own] + [array for array, _, _ in adds],
        in_specs=[
            pl.BlockSpec((rows, tile), lambda f, group=group, at=at: (group, at * tiles + f))
            for group, at in [(0, column)] + [(group, at) for _, group, at in adds]
        ],
        out_shape=shape((rows, width), BF),
        grid=(tiles,),
        out_specs=pl.BlockSpec((rows, tile), lambda f: (0, f)),
        compiler_params=WHOLE,
        cost_estimate=cost(rows * width * len(adds), 2 * rows * width * (2 + len(adds))),
    )


class OwnersSum:
    def __init__(self, order, sets, top, pieces=1):
        self.stages = send_order(top)
        self.outs = grad_rows_of(order, [codes for _, codes in self.stages] + [[0]], sets)
        self.pieces = pieces
        self.at = 0
        self.received = [[] for _ in range(pieces)]
        bit, codes = self.stages[0]
        whole = exchange(self.outs[0], "replica", bit)
        for n in range(pieces):
            self.received[n].append((whole, [code ^ bit for code in codes], n))

    def adds(self, n, codes):
        return [
            (array, held.index(codes[0]) // len(codes), column)
            for array, held, column in self.received[n]
        ]

    def latest(self, n=0):
        return self.received[n][-1][0]

    def step(self, order):
        self.at += 1
        for n in range(self.pieces):
            self.send(order, n)

    def send(self, order, n):
        bit, codes = self.stages[self.at]
        own = self.outs[self.at]
        sent = add_parts(order, own, self.adds(n, codes), n, own.shape[1] // self.pieces)
        self.received[n].append((exchange(sent, "replica", bit), [code ^ bit for code in codes], 0))

    def finish(self, order, planes, turned):
        kept = self.outs[-1]
        rows, width = kept.shape
        units = width // planes
        span = width // self.pieces
        tile = min(512 if turned else 1024, units)
        tiles = units // tile
        grid = planes * tiles
        count = grid // self.pieces
        adds = [
            (array, group, column * count if array.shape[1] == width else -1, n)
            for n in range(self.pieces)
            for array, group, column in self.adds(n, [0])
        ]
        each = len(adds) // self.pieces

        def kernel(kept_ref, *refs):
            out_ref = refs[-1]
            for n in range(self.pieces):

                @pl.when(lax.div(pl.program_id(0), count) == n)
                def _():
                    total = kept_ref[...]
                    for add_ref in refs[n * each : (n + 1) * each]:
                        total += add_ref[...].astype(F32)
                    out_ref[...] = total.T if turned else total

        def add_spec(group, whole, n):
            def at(f):
                own = jnp.clip(f - n * count, 0, count - 1)
                return (group, own + n * count if whole else own)

            return pl.BlockSpec((rows, tile), at)

        if turned:
            out_shape = shape((units, rows), F32)
            out_spec = pl.BlockSpec((tile, rows), lambda f: (f, 0))
        else:
            out_shape = shape((planes, rows, units), F32)
            out_spec = pl.BlockSpec(
                (None, rows, tile), lambda f: (lax.div(f, tiles), 0, lax.rem(f, tiles))
            )
        return launch(
            order,
            kernel,
            [kept] + [array for array, _, _, _ in adds],
            in_specs=[pl.BlockSpec((rows, tile), lambda f: (0, f))]
            + [add_spec(group, first >= 0, n) for _, group, first, n in adds],
            out_shape=out_shape,
            grid=(grid,),
            out_specs=out_spec,
            compiler_params=WHOLE,
            cost_estimate=cost(rows * width * len(adds), rows * width * (8 + 2 * each)),
        )


def true_rows(tok_dev):
    size = lax.axis_size("fsdp")
    block = jnp.arange(size, dtype=jnp.int32) ^ lax.axis_index("fsdp")
    return (block[:, None] * tok_dev + jnp.arange(tok_dev, dtype=jnp.int32)[None, :]).reshape(-1)


def tree_tables(parent_row, length_row, places):
    segments = parent_row.shape[0]
    labels = jnp.arange(segments, dtype=jnp.int32)
    before = labels[:, None] >= labels[None, :]
    ends = jnp.sum(jnp.where(before, length_row[None, :], 0), axis=1)
    starts = ends - length_row
    segment_of = jnp.sum((places[:, None] >= ends[None, :]).astype(jnp.int32), axis=1)
    member = segment_of[:, None] == labels[None, :]
    reach = ((labels[:, None] == labels[None, :]) | (parent_row[:, None] == labels[None, :])).astype(F32)
    steps = 1
    while steps < segments - 1:
        reach = (jnp.dot(reach, reach) > 0.5).astype(F32)
        steps *= 2
    ancestry = reach > 0.5
    above = jnp.sum(jnp.where(ancestry, length_row[None, :], 0), axis=1) - length_row
    moved = jnp.sum(jnp.where(member, (above - starts)[None, :], 0), axis=1)
    position = (places + moved).astype(F32)
    member_f = member.astype(F32)
    near = jnp.dot(jnp.dot(member_f, reach), member_f.T) > 0.5
    visible = near & (places[None, :] <= places[:, None])
    freq = ROPE_BASE ** (-jnp.arange(0, HD, 2, dtype=F32) / HD)
    angle = position[:, None] * freq[None, :]
    cos_half, sin_half = jnp.cos(angle), jnp.sin(angle)
    return (
        jnp.where(visible, 0.0, -1e30).astype(F32),
        jnp.concatenate([cos_half, cos_half], axis=1),
        jnp.concatenate([-sin_half, sin_half], axis=1),
    )


def on_device(
    tokens,
    cotangent,
    parents,
    lengths,
    qkv_weight,
    out_weight,
    gate_up_weight,
    down_weight,
    qk_gain,
    post_gain,
):
    micro, tok_dev, model_width = tokens.shape
    local_width = qkv_weight.shape[2]
    size = lax.axis_size("fsdp")
    replicas = lax.axis_size("replica")
    tok = micro * tok_dev
    rows = tok * size
    far = replicas // 2
    places = true_rows(tok_dev)
    x_rows = tokens.reshape(tok, model_width)
    grad_rows = cotangent.reshape(tok, model_width)
    order = Order()
    x_blocks = gather_blocks(x_rows)
    tables = [tree_tables(parents[m, 0], lengths[m, 0], places) for m in range(micro)]
    raw, values, squares, x_full = project(order, x_blocks, qkv_weight)
    context, queries, keys, inv, *attn_blocks = attend(
        order, raw, values, gather_blocks(squares), tables, qk_gain, out_weight
    )
    attn, hidden, hidden_b = after_attention(order, swap_blocks(attn_blocks), x_rows, post_gain)
    hidden_blocks = gather_blocks(hidden_b)
    far_hidden_blocks = gather_blocks(exchange(hidden_b, "replica", far))
    gate_up, swiglu, hidden_full, *mlp_blocks = mlp_forward(
        order, hidden_blocks, gate_up_weight, down_weight
    )
    order.extend(far_hidden_blocks[1:])
    mlp_blocks = gate(order, mlp_blocks)
    out_rows, d_mlp, mlp_gain_sum = after_mlp(
        order, swap_blocks(mlp_blocks), hidden, grad_rows, post_gain
    )
    d_mlp_blocks = gather_blocks(d_mlp)
    far_d_mlp_blocks = gather_blocks(exchange(d_mlp, "replica", far))
    d_gate_up, d_mlp_full, *d_hidden_blocks = mlp_back(
        order, d_mlp_blocks, gate_up, gate_up_weight, down_weight
    )
    d_hidden_parts = swap_blocks(d_hidden_blocks)
    fence(order, far_d_mlp_blocks[1:])
    far_d_gate_up, far_swiglu, far_d_mlp, far_hidden = mlp_units(
        order, far_hidden_blocks, far_d_mlp_blocks, gate_up_weight, down_weight
    )
    gate_up_sum = OwnersSum(
        order, [(hidden_full, d_gate_up, 0, rows), (far_hidden, far_d_gate_up, 0, rows)], far, 2
    )
    d_hidden, d_attn, attn_gain_sum = before_attention(
        order, d_hidden_parts, grad_rows, attn, post_gain
    )
    d_attn_blocks = gather_blocks(d_attn)
    order.pace = 100
    down_sum = OwnersSum(
        order, [(d_mlp_full, swiglu[None], 0, rows), (far_d_mlp, far_swiglu[None], 0, rows)], far
    )
    order.pace = 0.001
    gate_up_sum.step(order)
    order.pace = 100
    d_attn_full, d_norm, d_values, sums, qk_gain_sums = attend_back(
        order, d_attn_blocks, out_weight, queries, keys, values, raw, inv, tables, qk_gain
    )
    order.pace = 0.001
    sums_parts = gather_blocks(sums)
    down_sum.step(order)
    order.append(gate_up_sum.latest(0))
    d_projected, *input_blocks = project_back(
        order, d_norm, d_values, raw, inv, sums_parts, qk_gain, qkv_weight
    )
    input_parts = swap_blocks(input_blocks)
    [gain_rows] = gate(order, [jnp.concatenate([attn_gain_sum, mlp_gain_sum], axis=0)])
    me = lax.axis_index("fsdp")
    split = gain_rows.reshape(2, size, local_width)
    post_rows = lax.dynamic_index_in_dim(split, me, 1, keepdims=False)
    for flip in range(1, size):
        sent = lax.dynamic_index_in_dim(split, me ^ flip, 1, keepdims=False)
        post_rows = post_rows + exchange(sent, "fsdp", flip)
    gains = jnp.concatenate([qk_gain_sums, post_rows], axis=0)
    gains = gains + exchange(gains, "replica", 1)
    order.append(gate_up_sum.latest(1))
    qkv_sum = OwnersSum(order, [(x_full, d_projected, 0, rows)], replicas, 3)
    out_sum = OwnersSum(order, [(d_attn_full, context[None], 0, rows)], replicas)
    fence(order, [down_sum.latest(), *input_parts[1:], gains])
    qkv_sum.step(order)
    out_sum.step(order)
    gate_up_grad = gate_up_sum.finish(order, 2, False)
    qkv_sum.at += 1
    qkv_sum.send(order, 0)
    down_grad = down_sum.finish(order, 1, True)
    qkv_sum.send(order, 1)
    order.append(qkv_sum.latest(0))
    qkv_sum.send(order, 2)
    order.append(qkv_sum.latest(1))
    out_sum.step(order)
    [gains] = gate(order, [gains])
    flip = 2
    while flip < far:
        gains = gains + exchange(gains, "replica", flip)
        flip *= 2
    order.append(gains)
    qkv_grad = qkv_sum.finish(order, 3, False)
    gains = gains + exchange(gains, "replica", far)
    out_grad = out_sum.finish(order, 1, True)
    input_grad = d_hidden + sum(part.astype(F32) for part in input_parts)
    return (
        out_rows.reshape(micro, tok_dev, model_width),
        input_grad.reshape(micro, tok_dev, model_width),
        qkv_grad,
        out_grad,
        gate_up_grad,
        down_grad,
        gains[:2],
        gains[2:],
    )


def solution(mesh):
    in_specs = (
        P(None, ("replica", "fsdp"), None),
        P(None, ("replica", "fsdp"), None),
        P(None, "replica", None),
        P(None, "replica", None),
        P(None, None, "fsdp"),
        P("fsdp", None),
        P(None, None, "fsdp"),
        P("fsdp", None),
        P(None, "fsdp"),
        P(),
    )
    out_specs = (
        P(None, ("replica", "fsdp"), None),
        P(None, ("replica", "fsdp"), None),
        P(None, "replica", "fsdp"),
        P("fsdp", "replica"),
        P(None, "replica", "fsdp"),
        P("fsdp", "replica"),
        P(None, "fsdp"),
        P(None, "fsdp"),
    )
    return jax.shard_map(
        on_device, mesh=mesh, in_specs=in_specs, out_specs=out_specs, check_vma=False
    )
```

```python
import jax
import jax.numpy as jnp
from jax import lax
from jax.experimental import pallas as pl
from jax.experimental.pallas import tpu as pltpu
from jax.sharding import PartitionSpec as P

HD = 128


EPSILON = 1e-06
ROPE_BASE = 500000.0
BF = jnp.bfloat16
F32 = jnp.float32


def exchange(value, axis, flip):
    size = lax.axis_size(axis)
    return lax.ppermute(value, axis, [(i, i ^ flip) for i in range(size)])


def gather_blocks(rows):
    return [rows] + [exchange(rows, "fsdp", flip) for flip in range(1, lax.axis_size("fsdp"))]


def swap_blocks(blocks):
    return [blocks[0]] + [exchange(blocks[flip], "fsdp", flip) for flip in range(1, len(blocks))]


def cost(flops, moved, transcendentals=0):
    return (flops, moved, transcendentals)


class Order(list):
    pace = 0.001


def shape(dims, kind):
    return jax.ShapeDtypeStruct(dims, kind)


def dot(left, right):
    return jnp.dot(left, right, preferred_element_type=F32)


def dot_t(left, right):
    return lax.dot_general(left, right, (((1,), (1,)), ((), ())), preferred_element_type=F32)


def t_dot(left, right):
    return lax.dot_general(left, right, (((0,), (0,)), ((), ())), preferred_element_type=F32)


def lane_sums(field):
    ones = jnp.ones((8, field.shape[1]), F32)
    return lax.dot_general(
        ones,
        field,
        (((1,), (1,)), ((), ())),
        precision=lax.Precision.HIGHEST,
        preferred_element_type=F32,
    )


def join(block_refs, rows_ref):
    tok = block_refs[0].shape[0]
    for j, block_ref in enumerate(block_refs):
        rows_ref[pl.ds(j * tok, tok), :] = block_ref[...]


def write_blocks(rows, block_refs):
    tok = block_refs[0].shape[0]
    for j, block_ref in enumerate(block_refs):
        block_ref[...] = rows[j * tok : (j + 1) * tok].astype(block_ref.dtype)


def block_shapes(count, tok, width):
    return [shape((tok, width), F32)] + [shape((tok, width), BF)] * (count - 1)


def aligned_total(parts, tok):
    total = parts[0].T
    count = len(parts)
    for flip in range(1, count):
        column = parts[flip].T
        total = total + jnp.concatenate(
            [column[(j ^ flip) * tok : ((j ^ flip) + 1) * tok] for j in range(count)], axis=0
        )
    return total


def turn(field, cos_t, sin_t):
    return field * cos_t + pltpu.roll(field, HD // 2, 1) * sin_t


def turn_back(field, cos_t, sin_t):
    return field * cos_t - pltpu.roll(field, HD // 2, 1) * sin_t


VMEM = pl.BlockSpec(memory_space=pltpu.VMEM)
WHOLE = pltpu.CompilerParams(dimension_semantics=("arbitrary",))


def launch(
    order, kernel, args, in_specs, grid_spec=None, *, cost_estimate, pace=None, **settings
):
    waits = list(order)
    count = len(args)

    def body(*refs):
        kernel(*refs[:count], *refs[count + len(waits) :])

    flops, moved, transcendentals = [
        int(part * (order.pace if pace is None else pace)) for part in cost_estimate
    ]
    settings["cost_estimate"] = pl.CostEstimate(
        flops=flops, bytes_accessed=moved, transcendentals=transcendentals
    )
    specs = list(in_specs) + [pl.BlockSpec(memory_space=pl.ANY)] * len(waits)
    if grid_spec is None:
        settings["in_specs"] = specs
    else:
        settings["grid_spec"] = grid_spec(specs)
    settings["name"] = kernel.__qualname__.split(".<")[0].replace(".", "_")
    results = pl.pallas_call(body, **settings)(*args, *waits)
    order[:] = [results[0] if isinstance(results, (list, tuple)) else results]
    return results


def fence(order, arrays):
    order.extend(arrays)

    def kernel(out_ref):
        out_ref[...] = jnp.zeros((8, HD), F32)

    launch(
        order,
        kernel,
        [],
        in_specs=[],
        out_shape=shape((8, HD), F32),
        out_specs=VMEM,
        cost_estimate=cost(1 << 40, 1 << 30),
        pace=1,
    )


def gate(order, arrays):
    def kernel(*refs):
        pass

    held = pl.BlockSpec(memory_space=pl.ANY)
    return launch(
        order,
        kernel,
        arrays,
        in_specs=[held] * len(arrays),
        out_shape=[shape(array.shape, array.dtype) for array in arrays],
        out_specs=[held] * len(arrays),
        input_output_aliases={k: k for k in range(len(arrays))},
        cost_estimate=cost(0, 1000),
    )


def project(order, x_blocks, qkv_weight):
    count = len(x_blocks)
    tok, model_width = x_blocks[0].shape
    rows = count * tok
    width = qkv_weight.shape[2]

    def kernel(*refs):
        x_refs = refs[:count]
        weight_ref, raw_ref, values_ref, squares_ref, x_ref = refs[count:]
        step = pl.program_id(0)

        @pl.when(step == 0)
        def _():
            join(x_refs, x_ref)

        product = dot(x_ref[...], weight_ref[...])

        @pl.when(step < 2)
        def _():
            raw_ref[...] = product
            squares_ref[pl.ds(step, 1), :] = lane_sums(product * product)[:1]

        @pl.when(step == 2)
        def _():
            values_ref[...] = product.astype(BF)
            squares_ref[2:, :] = jnp.zeros((6, rows), F32)

    whole = pl.BlockSpec((tok, model_width), lambda n: (0, 0))
    return launch(
        order,
        kernel,
        [*x_blocks, qkv_weight],
        out_shape=[
            shape((2, rows, width), F32),
            shape((rows, width), BF),
            shape((8, rows), F32),
            shape((rows, model_width), BF),
        ],
        grid=(3,),
        in_specs=[whole] * count + [pl.BlockSpec((None, model_width, width), lambda n: (n, 0, 0))],
        out_specs=[
            pl.BlockSpec((None, rows, width), lambda n: (jnp.minimum(n, 1), 0, 0)),
            pl.BlockSpec((rows, width), lambda n: (0, 0)),
            pl.BlockSpec((8, rows), lambda n: (0, 0)),
            pl.BlockSpec((rows, model_width), lambda n: (0, 0)),
        ],
        compiler_params=WHOLE,
        cost_estimate=cost(6 * rows * model_width * width, 6 * model_width * width + 8 * rows * width),
    )


def pick(ref, m, each, tok, at):
    return jnp.concatenate(
        [
            ref[pl.ds(pl.multiple_of(j * tok + m * each, each), each), at]
            for j in range(ref.shape[0] // tok)
        ],
        axis=0,
    )


def place(ref, m, each, tok, at, rows):
    for j in range(ref.shape[0] // tok):
        ref[pl.ds(pl.multiple_of(j * tok + m * each, each), each), at] = rows[
            j * each : (j + 1) * each
        ]


def attend(order, raw, values, squares, tables, qk_gain, out_weight):
    count = len(squares)
    micro = tables[0].shape[0]
    _, rows, width = raw.shape
    heads = width // HD
    tok = rows // count
    each = tok // micro
    pack = rows // micro
    model_width = out_weight.shape[1]
    total_width = model_width
    scale = HD ** (-0.5)

    def kernel(
        raw_ref, values_ref, gain_ref, out_weight_ref, bias_ref, cos_ref, sin_ref, *refs
    ):
        parts = [ref[...] for ref in refs[:count]]
        context_ref, queries_ref, keys_ref, inv_ref = refs[count : count + 4]
        block_refs = refs[count + 4 :]
        inv_ref[...] = lax.rsqrt(aligned_total(parts, tok) / total_width + EPSILON)

        def one(m, carry):
            bias_v, cos_v, sin_v = bias_ref[m], cos_ref[m], sin_ref[m]
            inv = pick(inv_ref, m, each, tok, slice(None))
            own = pl.ds(pl.multiple_of(m * pack, pack), pack)
            for h in range(heads):
                at = slice(h * HD, (h + 1) * HD)
                q_raw = pick(raw_ref.at[0], m, each, tok, at)
                k_raw = pick(raw_ref.at[1], m, each, tok, at)
                q = turn(q_raw * inv[:, 0:1] * gain_ref[0:1, at], cos_v, sin_v).astype(BF)
                k = turn(k_raw * inv[:, 1:2] * gain_ref[1:2, at], cos_v, sin_v).astype(BF)
                queries_ref[own, at] = q
                keys_ref[own, at] = k
                scores = dot_t(q, k) * scale + bias_v
                weights = jnp.exp(scores - jnp.max(scores, axis=1, keepdims=True))
                probs = (weights / jnp.sum(weights, axis=1, keepdims=True)).astype(BF)
                context = dot(probs, pick(values_ref, m, each, tok, at)).astype(BF)
                place(context_ref, m, each, tok, at, context)
            return carry

        lax.fori_loop(0, micro, one, 0)
        write_blocks(dot(context_ref[...], out_weight_ref[...]), block_refs)

    return launch(
        order,
        kernel,
        [raw, values, qk_gain, out_weight, *tables, *squares],
        out_shape=[
            shape((rows, width), BF),
            shape((rows, width), BF),
            shape((rows, width), BF),
            shape((rows, 8), F32),
        ]
        + block_shapes(count, tok, model_width),
        in_specs=[VMEM] * (7 + count),
        out_specs=[VMEM] * (4 + count),
        cost_estimate=cost(
            4 * rows * pack * width + 2 * rows * width * model_width,
            2 * width * model_width + 14 * rows * width + 2 * rows * model_width,
            heads * rows * pack,
        ),
    )


def attend_back(order, d_attn_blocks, out_weight, queries, keys, values, raw, inv, tables, qk_gain):
    count = len(d_attn_blocks)
    micro = tables[0].shape[0]
    tok, model_width = d_attn_blocks[0].shape
    _, rows, width = raw.shape
    heads = width // HD
    each = tok // micro
    pack = rows // micro
    scale = HD ** (-0.5)

    def kernel(*refs):
        block_refs = refs[:count]
        (
            bias_ref,
            cos_ref,
            sin_ref,
            out_weight_ref,
            queries_ref,
            keys_ref,
            values_ref,
            raw_ref,
            inv_ref,
            gain_ref,
            d_attn_ref,
            d_norm_ref,
            d_values_ref,
            sums_ref,
            gain_sums_ref,
            d_context_ref,
            totals_ref,
        ) = refs[count:]
        join(block_refs, d_attn_ref)
        d_context_ref[...] = dot_t(d_attn_ref[...], out_weight_ref[...]).astype(BF)
        gain_sums_ref[...] = jnp.zeros((2, width), F32)

        def one(m, carry):
            bias_v, cos_v, sin_v = bias_ref[m], cos_ref[m], sin_ref[m]
            inv = pick(inv_ref, m, each, tok, slice(None))
            own = pl.ds(pl.multiple_of(m * pack, pack), pack)
            totals = [jnp.zeros((pack, HD), F32), jnp.zeros((pack, HD), F32)]
            for h in range(heads):
                at = slice(h * HD, (h + 1) * HD)
                q, k = queries_ref[own, at], keys_ref[own, at]
                v = pick(values_ref, m, each, tok, at)
                d_out = pick(d_context_ref, m, each, tok, at)
                scores = dot_t(q, k) * scale + bias_v
                weights = jnp.exp(scores - jnp.max(scores, axis=1, keepdims=True))
                probs = weights / jnp.sum(weights, axis=1, keepdims=True)
                d_probs = dot_t(d_out, v)
                delta = jnp.sum(d_probs * probs, axis=1, keepdims=True)
                d_scores = (probs * (d_probs - delta)).astype(BF)
                d_values = t_dot(probs.astype(BF), d_out).astype(BF)
                place(d_values_ref, m, each, tok, at, d_values)
                turned = (dot(d_scores, k) * scale, t_dot(d_scores, q) * scale)
                for n in range(2):
                    d_norm = turn_back(turned[n], cos_v, sin_v)
                    place(d_norm_ref.at[n], m, each, tok, at, d_norm)
                    field = pick(raw_ref.at[n], m, each, tok, at) * d_norm
                    totals[n] += field * gain_ref[n : n + 1, at]
                    gain_sums_ref[n : n + 1, at] += jnp.sum(
                        field * inv[:, n : n + 1], axis=0, keepdims=True
                    )
            for n in range(2):
                place(totals_ref.at[n], m, each, tok, slice(None), totals[n])
            return carry

        lax.fori_loop(0, micro, one, 0)
        for n in range(2):
            sums_ref[n : n + 1, :] = lane_sums(totals_ref[n])[:1]
        sums_ref[2:, :] = jnp.zeros((6, rows), F32)

    return launch(
        order,
        kernel,
        [*d_attn_blocks, *tables, out_weight, queries, keys, values, raw, inv, qk_gain],
        out_shape=[
            shape((rows, model_width), BF),
            shape((2, rows, width), F32),
            shape((rows, width), BF),
            shape((8, rows), F32),
            shape((2, width), F32),
        ],
        in_specs=[VMEM] * (10 + count),
        out_specs=[VMEM] * 5,
        scratch_shapes=[pltpu.VMEM((rows, width), BF), pltpu.VMEM((2, rows, HD), F32)],
        cost_estimate=cost(
            10 * rows * pack * width + 2 * rows * width * model_width,
            2 * width * model_width + 24 * rows * width + 2 * rows * model_width,
            heads * rows * pack,
        ),
    )


def project_back(order, d_norm, d_values, raw, inv, sums, qk_gain, qkv_weight):
    count = len(sums)
    _, rows, width = raw.shape
    tok = rows // count
    model_width = qkv_weight.shape[1]

    def kernel(d_norm_ref, d_values_ref, raw_ref, inv_ref, gain_ref, weight_ref, *refs):
        parts = refs[:count]
        d_projected_ref = refs[count]
        block_refs = refs[count + 1 : 2 * count + 1]
        total_ref = refs[2 * count + 1]
        step = pl.program_id(0)
        inv = inv_ref[...]

        @pl.when(step == 0)
        def _():
            d_projected_ref[...] = d_values_ref[...]

        @pl.when(step > 0)
        def _():
            shared = aligned_total([part[...] for part in parts], tok)
            first = step == 1
            r = jnp.where(first, inv[:, 0:1], inv[:, 1:2])
            s = jnp.where(first, shared[:, 0:1], shared[:, 1:2])
            gain = jnp.where(first, gain_ref[0:1, :], gain_ref[1:2, :])
            d_projected_ref[...] = (
                r * (d_norm_ref[...] * gain) - raw_ref[...] * (r * r * r * s / model_width)
            ).astype(BF)

        product = dot_t(d_projected_ref[...], weight_ref[...])

        total_ref[...] = jnp.where(step == 0, 0.0, total_ref[...]) + product

        @pl.when(step == 2)
        def _():
            write_blocks(total_ref[...], block_refs)

    def part_at(n):
        return lax.rem(n + 2, 3)

    field = pl.BlockSpec((None, rows, width), lambda n: (jnp.maximum(n - 1, 0), 0, 0))
    return launch(
        order,
        kernel,
        [d_norm, d_values, raw, inv, qk_gain, qkv_weight, *sums],
        out_shape=[shape((3, rows, width), BF)] + block_shapes(count, tok, model_width),
        grid=(3,),
        in_specs=[
            field,
            pl.BlockSpec((rows, width), lambda n: (0, 0)),
            field,
            pl.BlockSpec((rows, 8), lambda n: (0, 0)),
            pl.BlockSpec((2, width), lambda n: (0, 0)),
            pl.BlockSpec((None, model_width, width), lambda n: (part_at(n), 0, 0)),
        ]
        + [pl.BlockSpec((8, rows), lambda n: (0, 0))] * count,
        out_specs=[pl.BlockSpec((None, rows, width), lambda n: (part_at(n), 0, 0))]
        + [pl.BlockSpec((tok, model_width), lambda n: (0, 0))] * count,
        scratch_shapes=[pltpu.VMEM((rows, model_width), F32)],
        compiler_params=WHOLE,
        cost_estimate=cost(
            6 * rows * model_width * width, 6 * model_width * width + 22 * rows * width + 2 * rows * model_width
        ),
    )


def mlp_forward(order, hidden_blocks, gate_up_weight, down_weight):
    count = len(hidden_blocks)
    tok, model_width = hidden_blocks[0].shape
    rows = count * tok
    units = down_weight.shape[0]
    tile = min(512, units)
    last = units // tile - 1

    def kernel(*refs):
        gate_w_ref, up_w_ref, down_w_ref, gate_up_ref, swiglu_ref, hidden_ref = refs[
            count : count + 6
        ]
        block_refs = refs[count + 6 : 2 * count + 6]
        total_ref = refs[2 * count + 6]
        step = pl.program_id(0)

        @pl.when(step == 0)
        def _():
            join(refs[:count], hidden_ref)

        gate = dot(hidden_ref[...], gate_w_ref[...])
        up = dot(hidden_ref[...], up_w_ref[...])
        swiglu = (gate * jax.nn.sigmoid(gate) * up).astype(BF)
        gate_up_ref[0] = gate.astype(BF)
        gate_up_ref[1] = up.astype(BF)
        swiglu_ref[...] = swiglu
        product = dot(swiglu, down_w_ref[...])

        total_ref[...] = jnp.where(step == 0, 0.0, total_ref[...]) + product

        @pl.when(step == last)
        def _():
            write_blocks(total_ref[...], block_refs)

    field = pl.BlockSpec((rows, tile), lambda f: (0, f))
    return launch(
        order,
        kernel,
        [*hidden_blocks, gate_up_weight, gate_up_weight, down_weight],
        out_shape=[
            shape((2, rows, units), BF),
            shape((rows, units), BF),
            shape((rows, model_width), BF),
        ]
        + block_shapes(count, tok, model_width),
        grid=(units // tile,),
        in_specs=[pl.BlockSpec((tok, model_width), lambda f: (0, 0))] * count
        + [
            pl.BlockSpec((None, model_width, tile), lambda f: (0, 0, f)),
            pl.BlockSpec((None, model_width, tile), lambda f: (1, 0, f)),
            pl.BlockSpec((tile, model_width), lambda f: (f, 0)),
        ],
        out_specs=[pl.BlockSpec((2, rows, tile), lambda f: (0, 0, f)), field]
        + [pl.BlockSpec((rows, model_width), lambda f: (0, 0))]
        + [pl.BlockSpec((tok, model_width), lambda f: (0, 0))] * count,
        scratch_shapes=[pltpu.VMEM((rows, model_width), F32)],
        compiler_params=WHOLE,
        cost_estimate=cost(
            6 * rows * model_width * units,
            6 * model_width * units + 6 * rows * units + 8 * rows * model_width,
            rows * units,
        ),
    )


def unit_grads(gate, up, d_swiglu):
    sigmoid = jax.nn.sigmoid(gate)
    d_gate = d_swiglu * up * sigmoid * (1.0 + gate * (1.0 - sigmoid))
    return (d_gate.astype(BF), (d_swiglu * (gate * sigmoid)).astype(BF))


def mlp_back(order, d_mlp_blocks, gate_up, gate_up_weight, down_weight):
    count = len(d_mlp_blocks)
    tok, model_width = d_mlp_blocks[0].shape
    rows = count * tok
    units = down_weight.shape[0]
    tile = min(512, units)
    last = units // tile - 1

    def kernel(*refs):
        gate_up_ref, gate_w_ref, up_w_ref, down_w_ref, d_gate_up_ref, d_mlp_ref = refs[
            count : count + 6
        ]
        block_refs = refs[count + 6 : 2 * count + 6]
        total_ref = refs[2 * count + 6]
        step = pl.program_id(0)

        @pl.when(step == 0)
        def _():
            join(refs[:count], d_mlp_ref)

        d_swiglu = dot_t(d_mlp_ref[...], down_w_ref[...])
        d_gate, d_up = unit_grads(gate_up_ref[0].astype(F32), gate_up_ref[1].astype(F32), d_swiglu)
        d_gate_up_ref[0] = d_gate
        d_gate_up_ref[1] = d_up
        product = dot_t(d_gate, gate_w_ref[...]) + dot_t(d_up, up_w_ref[...])

        total_ref[...] = jnp.where(step == 0, 0.0, total_ref[...]) + product

        @pl.when(step == last)
        def _():
            write_blocks(total_ref[...], block_refs)

    field = pl.BlockSpec((2, rows, tile), lambda f: (0, 0, f))
    return launch(
        order,
        kernel,
        [*d_mlp_blocks, gate_up, gate_up_weight, gate_up_weight, down_weight],
        out_shape=[shape((2, rows, units), BF), shape((rows, model_width), BF)]
        + block_shapes(count, tok, model_width),
        grid=(units // tile,),
        in_specs=[pl.BlockSpec((tok, model_width), lambda f: (0, 0))] * count
        + [
            field,
            pl.BlockSpec((None, model_width, tile), lambda f: (0, 0, f)),
            pl.BlockSpec((None, model_width, tile), lambda f: (1, 0, f)),
            pl.BlockSpec((tile, model_width), lambda f: (f, 0)),
        ],
        out_specs=[field]
        + [pl.BlockSpec((rows, model_width), lambda f: (0, 0))]
        + [pl.BlockSpec((tok, model_width), lambda f: (0, 0))] * count,
        scratch_shapes=[pltpu.VMEM((rows, model_width), F32)],
        compiler_params=WHOLE,
        cost_estimate=cost(
            6 * rows * model_width * units,
            6 * model_width * units + 8 * rows * units + 8 * rows * model_width,
            rows * units,
        ),
    )


def mlp_units(order, hidden_blocks, d_mlp_blocks, gate_up_weight, down_weight):
    count = len(d_mlp_blocks)
    tok, model_width = d_mlp_blocks[0].shape
    rows = count * tok
    units = down_weight.shape[0]
    tile = min(256, units)

    def kernel(*refs):
        gate_w_ref, up_w_ref, down_w_ref = refs[2 * count : 2 * count + 3]
        d_gate_up_ref, swiglu_ref, d_mlp_ref, hidden_ref = refs[2 * count + 3 :]

        @pl.when(pl.program_id(0) == 0)
        def _():
            join(refs[:count], hidden_ref)
            join(refs[count : 2 * count], d_mlp_ref)

        gate = dot(hidden_ref[...], gate_w_ref[...])
        up = dot(hidden_ref[...], up_w_ref[...])
        d_gate, d_up = unit_grads(gate, up, dot_t(d_mlp_ref[...], down_w_ref[...]))
        swiglu_ref[...] = (gate * jax.nn.sigmoid(gate) * up).astype(BF)
        d_gate_up_ref[0] = d_gate
        d_gate_up_ref[1] = d_up

    return launch(
        order,
        kernel,
        [*hidden_blocks, *d_mlp_blocks, gate_up_weight, gate_up_weight, down_weight],
        out_shape=[
            shape((2, rows, units), BF),
            shape((rows, units), BF),
            shape((rows, model_width), BF),
            shape((rows, model_width), BF),
        ],
        grid=(units // tile,),
        in_specs=[pl.BlockSpec((tok, model_width), lambda f: (0, 0))] * (2 * count)
        + [
            pl.BlockSpec((None, model_width, tile), lambda f: (0, 0, f)),
            pl.BlockSpec((None, model_width, tile), lambda f: (1, 0, f)),
            pl.BlockSpec((tile, model_width), lambda f: (f, 0)),
        ],
        out_specs=[
            pl.BlockSpec((2, rows, tile), lambda f: (0, 0, f)),
            pl.BlockSpec((rows, tile), lambda f: (0, f)),
            pl.BlockSpec((rows, model_width), lambda f: (0, 0)),
            pl.BlockSpec((rows, model_width), lambda f: (0, 0)),
        ],
        compiler_params=WHOLE,
        cost_estimate=cost(
            6 * rows * model_width * units,
            6 * rows * model_width + 6 * model_width * units + 6 * rows * units,
            rows * units,
        ),
    )


def sum_parts(part_refs):
    total = part_refs[0][...].astype(F32)
    for part_ref in part_refs[1:]:
        total += part_ref[...].astype(F32)
    return total


def norm_back(field, gain, upstream):
    width = field.shape[1]
    inv = lax.rsqrt(jnp.sum(field * field, axis=1, keepdims=True) / width + EPSILON)
    weighted = upstream * gain
    shared = jnp.sum(field * weighted, axis=1, keepdims=True)
    gain_sum = jnp.sum(upstream * field * inv, axis=0, keepdims=True)
    return (inv * weighted - field * (inv * inv * inv * shared / width), gain_sum)


def by_rows(order, kernel, parts, rows, gains, outs, sums, work):
    tok, width = rows[0].shape
    block = min(32, tok)
    cut = pl.BlockSpec((block, width), lambda i: (i, 0))
    return launch(
        order,
        kernel,
        [*parts, *rows, gains],
        in_specs=[cut] * (len(parts) + len(rows)) + [pl.BlockSpec(gains.shape, lambda i: (0, 0))],
        out_shape=[shape((tok, width), kind) for kind in outs] + [shape((1, width), F32)] * sums,
        grid=(tok // block,),
        out_specs=[cut] * len(outs) + [pl.BlockSpec((1, width), lambda i: (0, 0))] * sums,
        compiler_params=WHOLE,
        cost_estimate=cost(work * tok * width, 24 * tok * width),
    )


def add_rows(sum_ref, value):
    @pl.when(pl.program_id(0) == 0)
    def _():
        sum_ref[...] = value

    @pl.when(pl.program_id(0) > 0)
    def _():
        sum_ref[...] += value


def after_attention(order, parts, x_rows, post_gain):
    count = len(parts)

    def kernel(*refs):
        x_ref, gain_ref, attn_ref, hidden_ref, rounded_ref = refs[count:]
        attn = sum_parts(refs[:count])
        inv = lax.rsqrt(jnp.sum(attn * attn, axis=1, keepdims=True) / attn.shape[1] + EPSILON)
        hidden = x_ref[...].astype(F32) + attn * inv * gain_ref[0:1, :]
        attn_ref[...] = attn
        hidden_ref[...] = hidden
        rounded_ref[...] = hidden.astype(BF)

    return by_rows(order, kernel, parts, [x_rows], post_gain, [F32, F32, BF], 0, 8)


def after_mlp(order, parts, hidden, grad_rows, post_gain):
    count = len(parts)

    def kernel(*refs):
        hidden_ref, grad_ref, gain_ref, out_ref, d_mlp_ref, gain_sum_ref = refs[count:]
        mlp = sum_parts(refs[:count])
        gain = gain_ref[1:2, :]
        inv = lax.rsqrt(jnp.sum(mlp * mlp, axis=1, keepdims=True) / mlp.shape[1] + EPSILON)
        out_ref[...] = hidden_ref[...] + mlp * inv * gain
        d_mlp, gain_sum = norm_back(mlp, gain, grad_ref[...].astype(F32))
        d_mlp_ref[...] = d_mlp.astype(BF)
        add_rows(gain_sum_ref, gain_sum)

    return by_rows(order, kernel, parts, [hidden, grad_rows], post_gain, [F32, BF], 1, 16)


def before_attention(order, parts, grad_rows, attn, post_gain):
    count = len(parts)

    def kernel(*refs):
        grad_ref, attn_ref, gain_ref, d_hidden_ref, d_attn_ref, gain_sum_ref = refs[count:]
        d_hidden = grad_ref[...].astype(F32) + sum_parts(refs[:count])
        d_hidden_ref[...] = d_hidden
        d_attn, gain_sum = norm_back(attn_ref[...], gain_ref[0:1, :], d_hidden)
        d_attn_ref[...] = d_attn.astype(BF)
        add_rows(gain_sum_ref, gain_sum)

    return by_rows(order, kernel, parts, [grad_rows, attn], post_gain, [F32, BF], 1, 16)


def send_order(top):
    def halves(codes, bit):
        if len(codes) == 1:
            return codes
        return halves([c for c in codes if c & bit], 2 * bit) + halves(
            [c for c in codes if not c & bit], 2 * bit
        )

    stages = []
    bit = 1
    while bit < top:
        stages.append((bit, [bit + c for c in halves(list(range(0, top, 2 * bit)), 2 * bit)]))
        bit *= 2
    return stages


def grad_rows_of(order, splits, sets):
    codes = [code for split in splits for code in split]
    blocks = len(codes)
    replicas = lax.axis_size("replica")
    picks = lax.axis_index("replica") ^ jnp.array(codes, jnp.int32)
    block = sets[0][0].shape[1] // replicas
    planes, _, units = sets[0][1].shape
    tile = min(512, units)
    tiles = units // tile
    width = planes * units
    depth = sum(rows for _, _, _, rows in sets)
    count = len(sets)
    kinds = [BF] * (len(splits) - 1) + [F32]

    def kernel(picks_ref, *refs):
        left_refs = refs[: count * blocks]
        right_refs = refs[count * blocks : count * blocks + count]
        out_refs = refs[count * blocks + count : count * blocks + count + len(splits)]
        turned_ref, right_ref = refs[count * blocks + count + len(splits) :]

        @pl.when(pl.program_id(0) == 0)
        def _():
            at = 0
            for k, (_, _, _, rows) in enumerate(sets):
                for b in range(blocks):
                    turned_ref[pl.ds(b * block, block), pl.ds(at, rows)] = left_refs[k * blocks + b][
                        ...
                    ].T
                at += rows

        at = 0
        for k, (_, _, _, rows) in enumerate(sets):
            right_ref[pl.ds(at, rows), :] = right_refs[k][...]
            at += rows
        first = 0
        for split, out_ref in zip(splits, out_refs):
            rows = len(split) * block
            out_ref[...] = dot(turned_ref[pl.ds(first, rows), :], right_ref[...]).astype(out_ref.dtype)
            first += rows

    in_specs = [
        pl.BlockSpec((rows, block), lambda f, picks_ref, group=group, b=b: (group, picks_ref[b]))
        for _, _, group, rows in sets
        for b in range(blocks)
    ] + [
        pl.BlockSpec(
            (None, rows, tile),
            lambda f, picks_ref, group=group: (lax.div(f, tiles), group, lax.rem(f, tiles)),
        )
        for _, _, group, rows in sets
    ]
    return launch(
        order,
        kernel,
        [picks]
        + [left for left, _, _, _ in sets for _ in range(blocks)]
        + [right for _, right, _, _ in sets],
        in_specs,
        lambda specs: pltpu.PrefetchScalarGridSpec(
            num_scalar_prefetch=1,
            grid=(planes * tiles,),
            in_specs=specs,
            out_specs=[
                pl.BlockSpec((len(split) * block, tile), lambda f, picks_ref: (0, f))
                for split in splits
            ],
            scratch_shapes=[
                pltpu.VMEM((blocks * block, depth), BF),
                pltpu.VMEM((depth, tile), BF),
            ],
        ),
        out_shape=[shape((len(split) * block, width), kind) for split, kind in zip(splits, kinds)],
        compiler_params=WHOLE,
        cost_estimate=cost(
            2 * depth * blocks * block * width,
            2 * depth * (blocks * block + width) + 2 * blocks * block * width,
        ),
    )


def add_parts(order, own, adds, column, width):
    rows = own.shape[0]
    tile = min(2048, width)
    tiles = width // tile

    def kernel(own_ref, *refs):
        refs[-1][...] = sum_parts([own_ref, *refs[:-1]]).astype(BF)

    return launch(
        order,
        kernel,
        [own] + [array for array, _, _ in adds],
        in_specs=[
            pl.BlockSpec((rows, tile), lambda f, group=group, at=at: (group, at * tiles + f))
            for group, at in [(0, column)] + [(group, at) for _, group, at in adds]
        ],
        out_shape=shape((rows, width), BF),
        grid=(tiles,),
        out_specs=pl.BlockSpec((rows, tile), lambda f: (0, f)),
        compiler_params=WHOLE,
        cost_estimate=cost(rows * width * len(adds), 2 * rows * width * (2 + len(adds))),
    )


class OwnersSum:
    def __init__(self, order, sets, top, pieces=1):
        self.stages = send_order(top)
        self.outs = grad_rows_of(order, [codes for _, codes in self.stages] + [[0]], sets)
        self.pieces = pieces
        self.at = 0
        self.received = [[] for _ in range(pieces)]
        bit, codes = self.stages[0]
        whole = exchange(self.outs[0], "replica", bit)
        for n in range(pieces):
            self.received[n].append((whole, [code ^ bit for code in codes], n))

    def adds(self, n, codes):
        return [
            (array, held.index(codes[0]) // len(codes), column)
            for array, held, column in self.received[n]
        ]

    def latest(self, n=0):
        return self.received[n][-1][0]

    def step(self, order):
        self.at += 1
        for n in range(self.pieces):
            self.send(order, n)

    def send(self, order, n):
        bit, codes = self.stages[self.at]
        own = self.outs[self.at]
        sent = add_parts(order, own, self.adds(n, codes), n, own.shape[1] // self.pieces)
        self.received[n].append((exchange(sent, "replica", bit), [code ^ bit for code in codes], 0))

    def finish(self, order, planes, turned):
        kept = self.outs[-1]
        rows, width = kept.shape
        units = width // planes
        span = width // self.pieces
        tile = min(512 if turned else 1024, units)
        tiles = units // tile
        grid = planes * tiles
        count = grid // self.pieces
        adds = [
            (array, group, column * count if array.shape[1] == width else -1, n)
            for n in range(self.pieces)
            for array, group, column in self.adds(n, [0])
        ]
        each = len(adds) // self.pieces

        def kernel(kept_ref, *refs):
            out_ref = refs[-1]
            for n in range(self.pieces):

                @pl.when(lax.div(pl.program_id(0), count) == n)
                def _():
                    total = kept_ref[...]
                    for add_ref in refs[n * each : (n + 1) * each]:
                        total += add_ref[...].astype(F32)
                    out_ref[...] = total.T if turned else total

        def add_spec(group, whole, n):
            def at(f):
                own = jnp.clip(f - n * count, 0, count - 1)
                return (group, own + n * count if whole else own)

            return pl.BlockSpec((rows, tile), at)

        if turned:
            out_shape = shape((units, rows), F32)
            out_spec = pl.BlockSpec((tile, rows), lambda f: (f, 0))
        else:
            out_shape = shape((planes, rows, units), F32)
            out_spec = pl.BlockSpec(
                (None, rows, tile), lambda f: (lax.div(f, tiles), 0, lax.rem(f, tiles))
            )
        return launch(
            order,
            kernel,
            [kept] + [array for array, _, _, _ in adds],
            in_specs=[pl.BlockSpec((rows, tile), lambda f: (0, f))]
            + [add_spec(group, first >= 0, n) for _, group, first, n in adds],
            out_shape=out_shape,
            grid=(grid,),
            out_specs=out_spec,
            compiler_params=WHOLE,
            cost_estimate=cost(rows * width * len(adds), rows * width * (8 + 2 * each)),
        )


def true_rows(tok_dev):
    size = lax.axis_size("fsdp")
    block = jnp.arange(size, dtype=jnp.int32) ^ lax.axis_index("fsdp")
    return (block[:, None] * tok_dev + jnp.arange(tok_dev, dtype=jnp.int32)[None, :]).reshape(-1)


def tree_tables(parent_row, length_row, places):
    segments = parent_row.shape[0]
    labels = jnp.arange(segments, dtype=jnp.int32)
    before = labels[:, None] >= labels[None, :]
    ends = jnp.sum(jnp.where(before, length_row[None, :], 0), axis=1)
    starts = ends - length_row
    segment_of = jnp.sum((places[:, None] >= ends[None, :]).astype(jnp.int32), axis=1)
    member = segment_of[:, None] == labels[None, :]
    reach = ((labels[:, None] == labels[None, :]) | (parent_row[:, None] == labels[None, :])).astype(F32)
    steps = 1
    while steps < segments - 1:
        reach = (jnp.dot(reach, reach) > 0.5).astype(F32)
        steps *= 2
    ancestry = reach > 0.5
    above = jnp.sum(jnp.where(ancestry, length_row[None, :], 0), axis=1) - length_row
    moved = jnp.sum(jnp.where(member, (above - starts)[None, :], 0), axis=1)
    position = (places + moved).astype(F32)
    member_f = member.astype(F32)
    near = jnp.dot(jnp.dot(member_f, reach), member_f.T) > 0.5
    visible = near & (places[None, :] <= places[:, None])
    freq = ROPE_BASE ** (-jnp.arange(0, HD, 2, dtype=F32) / HD)
    angle = position[:, None] * freq[None, :]
    cos_half, sin_half = jnp.cos(angle), jnp.sin(angle)
    return (
        jnp.where(visible, 0.0, -1e30).astype(F32),
        jnp.concatenate([cos_half, cos_half], axis=1),
        jnp.concatenate([-sin_half, sin_half], axis=1),
    )


def on_device(
    tokens,
    cotangent,
    parents,
    lengths,
    qkv_weight,
    out_weight,
    gate_up_weight,
    down_weight,
    qk_gain,
    post_gain,
):
    micro, tok_dev, model_width = tokens.shape
    local_width = qkv_weight.shape[2]
    size = lax.axis_size("fsdp")
    replicas = lax.axis_size("replica")
    tok = micro * tok_dev
    rows = tok * size
    far = replicas // 2
    places = true_rows(tok_dev)
    x_rows = tokens.reshape(tok, model_width)
    grad_rows = cotangent.reshape(tok, model_width)
    order = Order()
    x_blocks = gather_blocks(x_rows)
    tables = jax.vmap(tree_tables, in_axes=(0, 0, None))(parents[:, 0], lengths[:, 0], places)
    raw, values, squares, x_full = project(order, x_blocks, qkv_weight)
    context, queries, keys, inv, *attn_blocks = attend(
        order, raw, values, gather_blocks(squares), tables, qk_gain, out_weight
    )
    attn, hidden, hidden_b = after_attention(order, swap_blocks(attn_blocks), x_rows, post_gain)
    hidden_blocks = gather_blocks(hidden_b)
    far_hidden_blocks = gather_blocks(exchange(hidden_b, "replica", far))
    gate_up, swiglu, hidden_full, *mlp_blocks = mlp_forward(
        order, hidden_blocks, gate_up_weight, down_weight
    )
    order.extend(far_hidden_blocks[1:])
    mlp_blocks = gate(order, mlp_blocks)
    out_rows, d_mlp, mlp_gain_sum = after_mlp(
        order, swap_blocks(mlp_blocks), hidden, grad_rows, post_gain
    )
    d_mlp_blocks = gather_blocks(d_mlp)
    far_d_mlp_blocks = gather_blocks(exchange(d_mlp, "replica", far))
    d_gate_up, d_mlp_full, *d_hidden_blocks = mlp_back(
        order, d_mlp_blocks, gate_up, gate_up_weight, down_weight
    )
    d_hidden_parts = swap_blocks(d_hidden_blocks)
    fence(order, far_d_mlp_blocks[1:])
    far_d_gate_up, far_swiglu, far_d_mlp, far_hidden = mlp_units(
        order, far_hidden_blocks, far_d_mlp_blocks, gate_up_weight, down_weight
    )
    gate_up_sum = OwnersSum(
        order, [(hidden_full, d_gate_up, 0, rows), (far_hidden, far_d_gate_up, 0, rows)], far, 2
    )
    d_hidden, d_attn, attn_gain_sum = before_attention(
        order, d_hidden_parts, grad_rows, attn, post_gain
    )
    d_attn_blocks = gather_blocks(d_attn)
    order.pace = 100
    down_sum = OwnersSum(
        order, [(d_mlp_full, swiglu[None], 0, rows), (far_d_mlp, far_swiglu[None], 0, rows)], far
    )
    order.pace = 0.001
    gate_up_sum.step(order)
    order.pace = 100
    d_attn_full, d_norm, d_values, sums, qk_gain_sums = attend_back(
        order, d_attn_blocks, out_weight, queries, keys, values, raw, inv, tables, qk_gain
    )
    order.pace = 0.001
    sums_parts = gather_blocks(sums)
    down_sum.step(order)
    order.append(gate_up_sum.latest(0))
    d_projected, *input_blocks = project_back(
        order, d_norm, d_values, raw, inv, sums_parts, qk_gain, qkv_weight
    )
    input_parts = swap_blocks(input_blocks)
    [gain_rows] = gate(order, [jnp.concatenate([attn_gain_sum, mlp_gain_sum], axis=0)])
    me = lax.axis_index("fsdp")
    split = gain_rows.reshape(2, size, local_width)
    post_rows = lax.dynamic_index_in_dim(split, me, 1, keepdims=False)
    for flip in range(1, size):
        sent = lax.dynamic_index_in_dim(split, me ^ flip, 1, keepdims=False)
        post_rows = post_rows + exchange(sent, "fsdp", flip)
    gains = jnp.concatenate([qk_gain_sums, post_rows], axis=0)
    gains = gains + exchange(gains, "replica", 1)
    order.append(gate_up_sum.latest(1))
    qkv_sum = OwnersSum(order, [(x_full, d_projected, 0, rows)], replicas, 3)
    out_sum = OwnersSum(order, [(d_attn_full, context[None], 0, rows)], replicas)
    fence(order, [down_sum.latest(), *input_parts[1:], gains])
    qkv_sum.step(order)
    out_sum.step(order)
    gate_up_grad = gate_up_sum.finish(order, 2, False)
    qkv_sum.at += 1
    qkv_sum.send(order, 0)
    down_grad = down_sum.finish(order, 1, True)
    qkv_sum.send(order, 1)
    order.append(qkv_sum.latest(0))
    qkv_sum.send(order, 2)
    order.append(qkv_sum.latest(1))
    out_sum.step(order)
    [gains] = gate(order, [gains])
    flip = 2
    while flip < far:
        gains = gains + exchange(gains, "replica", flip)
        flip *= 2
    order.append(gains)
    qkv_grad = qkv_sum.finish(order, 3, False)
    out_grad = out_sum.finish(order, 1, True)
    [far_gains] = gate(order, [exchange(gains, "replica", far)])
    gains = gains + far_gains
    input_grad = d_hidden + sum(part.astype(F32) for part in input_parts)
    return (
        out_rows.reshape(micro, tok_dev, model_width),
        input_grad.reshape(micro, tok_dev, model_width),
        qkv_grad,
        out_grad,
        gate_up_grad,
        down_grad,
        gains[:2],
        gains[2:],
    )


def solution(mesh):
    in_specs = (
        P(None, ("replica", "fsdp"), None),
        P(None, ("replica", "fsdp"), None),
        P(None, "replica", None),
        P(None, "replica", None),
        P(None, None, "fsdp"),
        P("fsdp", None),
        P(None, None, "fsdp"),
        P("fsdp", None),
        P(None, "fsdp"),
        P(),
    )
    out_specs = (
        P(None, ("replica", "fsdp"), None),
        P(None, ("replica", "fsdp"), None),
        P(None, "replica", "fsdp"),
        P("fsdp", "replica"),
        P(None, "replica", "fsdp"),
        P("fsdp", "replica"),
        P(None, "fsdp"),
        P(None, "fsdp"),
    )
    return jax.shard_map(
        on_device, mesh=mesh, in_specs=in_specs, out_specs=out_specs, check_vma=False
    )
```

```python
import jax
import jax.numpy as jnp
from jax import lax
from jax.experimental import pallas as pl
from jax.experimental.pallas import tpu as pltpu
from jax.sharding import PartitionSpec as P

HD = 128


EPSILON = 1e-06
ROPE_BASE = 500000.0
BF = jnp.bfloat16
F32 = jnp.float32


def exchange(value, axis, flip):
    size = lax.axis_size(axis)
    return lax.ppermute(value, axis, [(i, i ^ flip) for i in range(size)])


def gather_blocks(rows):
    return [rows] + [exchange(rows, "fsdp", flip) for flip in range(1, lax.axis_size("fsdp"))]


def swap_blocks(blocks):
    return [blocks[0]] + [exchange(blocks[flip], "fsdp", flip) for flip in range(1, len(blocks))]


def cost(flops, moved, transcendentals=0):
    return (flops, moved, transcendentals)


class Order(list):
    pace = 0.001


def shape(dims, kind):
    return jax.ShapeDtypeStruct(dims, kind)


def dot(left, right):
    return jnp.dot(left, right, preferred_element_type=F32)


def dot_t(left, right):
    return lax.dot_general(left, right, (((1,), (1,)), ((), ())), preferred_element_type=F32)


def t_dot(left, right):
    return lax.dot_general(left, right, (((0,), (0,)), ((), ())), preferred_element_type=F32)


def lane_sums(field):
    ones = jnp.ones((8, field.shape[1]), F32)
    return lax.dot_general(
        ones,
        field,
        (((1,), (1,)), ((), ())),
        precision=lax.Precision.HIGHEST,
        preferred_element_type=F32,
    )


def join(block_refs, rows_ref):
    tok = block_refs[0].shape[0]
    for j, block_ref in enumerate(block_refs):
        rows_ref[pl.ds(j * tok, tok), :] = block_ref[...]


def write_blocks(rows, block_refs):
    tok = block_refs[0].shape[0]
    for j, block_ref in enumerate(block_refs):
        block_ref[...] = rows[j * tok : (j + 1) * tok].astype(block_ref.dtype)


def block_shapes(count, tok, width):
    return [shape((tok, width), F32)] + [shape((tok, width), BF)] * (count - 1)


def aligned_total(parts, tok):
    total = parts[0].T
    count = len(parts)
    for flip in range(1, count):
        column = parts[flip].T
        total = total + jnp.concatenate(
            [column[(j ^ flip) * tok : ((j ^ flip) + 1) * tok] for j in range(count)], axis=0
        )
    return total


def turn(field, cos_t, sin_t):
    return field * cos_t + pltpu.roll(field, HD // 2, 1) * sin_t


def turn_back(field, cos_t, sin_t):
    return field * cos_t - pltpu.roll(field, HD // 2, 1) * sin_t


VMEM = pl.BlockSpec(memory_space=pltpu.VMEM)
WHOLE = pltpu.CompilerParams(dimension_semantics=("arbitrary",))


def launch(
    order, kernel, args, in_specs, grid_spec=None, *, cost_estimate, pace=None, **settings
):
    waits = list(order)
    count = len(args)

    def body(*refs):
        kernel(*refs[:count], *refs[count + len(waits) :])

    flops, moved, transcendentals = [
        int(part * (order.pace if pace is None else pace)) for part in cost_estimate
    ]
    settings["cost_estimate"] = pl.CostEstimate(
        flops=flops, bytes_accessed=moved, transcendentals=transcendentals
    )
    specs = list(in_specs) + [pl.BlockSpec(memory_space=pl.ANY)] * len(waits)
    if grid_spec is None:
        settings["in_specs"] = specs
    else:
        settings["grid_spec"] = grid_spec(specs)
    settings["name"] = kernel.__qualname__.split(".<")[0].replace(".", "_")
    results = pl.pallas_call(body, **settings)(*args, *waits)
    order[:] = [results[0] if isinstance(results, (list, tuple)) else results]
    return results


def fence(order, arrays):
    order.extend(arrays)

    def kernel(out_ref):
        out_ref[...] = jnp.zeros((8, HD), F32)

    launch(
        order,
        kernel,
        [],
        in_specs=[],
        out_shape=shape((8, HD), F32),
        out_specs=VMEM,
        cost_estimate=cost(1 << 40, 1 << 30),
        pace=1,
    )


def gate(order, arrays):
    def kernel(*refs):
        pass

    held = pl.BlockSpec(memory_space=pl.ANY)
    return launch(
        order,
        kernel,
        arrays,
        in_specs=[held] * len(arrays),
        out_shape=[shape(array.shape, array.dtype) for array in arrays],
        out_specs=[held] * len(arrays),
        input_output_aliases={k: k for k in range(len(arrays))},
        cost_estimate=cost(0, 1000),
    )


def project(order, x_blocks, qkv_weight, part, parts, begun):
    count = len(x_blocks)
    tok, model_width = x_blocks[0].shape
    rows = count * tok
    width = qkv_weight.shape[2]

    def kernel(*refs):
        x_refs = refs[:count]
        weight_ref = refs[count]
        raw_ref, values_ref, squares_ref, x_ref = refs[-4:]
        step = pl.program_id(0)

        @pl.when(step == 0)
        def _():
            join(x_refs, x_ref)

        product = dot(x_ref[...], weight_ref[...])

        @pl.when(step < 2)
        def _():
            raw_ref[...] = product
            squares_ref[pl.ds(step, 1), :] = lane_sums(product * product)[:1]

        @pl.when(step == 2)
        def _():
            values_ref[...] = product.astype(BF)
            squares_ref[2:, :] = jnp.zeros((6, rows), F32)

    whole = pl.BlockSpec((tok, model_width), lambda n: (0, 0))
    return launch(
        order,
        kernel,
        [*x_blocks, qkv_weight, *begun],
        out_shape=[
            shape((2, parts * rows, width), F32),
            shape((parts * rows, width), BF),
            shape((8, parts * rows), F32),
            shape((parts * rows, model_width), BF),
        ],
        grid=(3,),
        in_specs=[whole] * count
        + [pl.BlockSpec((None, model_width, width), lambda n: (n, 0, 0))]
        + [pl.BlockSpec(memory_space=pl.ANY)] * len(begun),
        out_specs=[
            pl.BlockSpec((None, rows, width), lambda n: (jnp.minimum(n, 1), part, 0)),
            pl.BlockSpec((rows, width), lambda n: (part, 0)),
            pl.BlockSpec((8, rows), lambda n: (0, part)),
            pl.BlockSpec((rows, model_width), lambda n: (part, 0)),
        ],
        input_output_aliases={count + 1 + k: k for k in range(len(begun))},
        compiler_params=WHOLE,
        cost_estimate=cost(6 * rows * model_width * width, 6 * model_width * width + 8 * rows * width),
    )


def pick(ref, m, each, tok, at):
    return jnp.concatenate(
        [
            ref[pl.ds(pl.multiple_of(j * tok + m * each, each), each), at]
            for j in range(ref.shape[0] // tok)
        ],
        axis=0,
    )


def place(ref, m, each, tok, at, rows):
    for j in range(ref.shape[0] // tok):
        ref[pl.ds(pl.multiple_of(j * tok + m * each, each), each), at] = rows[
            j * each : (j + 1) * each
        ]


def attend(order, raw, values, squares, tables, qk_gain, out_weight):
    count = len(squares)
    micro = tables[0].shape[0]
    _, rows, width = raw.shape
    heads = width // HD
    tok = rows // count
    each = tok // micro
    pack = rows // micro
    model_width = out_weight.shape[1]
    total_width = model_width
    scale = HD ** (-0.5)

    def kernel(
        raw_ref, values_ref, gain_ref, out_weight_ref, bias_ref, cos_ref, sin_ref, *refs
    ):
        parts = [ref[...] for ref in refs[:count]]
        context_ref, queries_ref, keys_ref, inv_ref = refs[count : count + 4]
        block_refs = refs[count + 4 :]
        inv_ref[...] = lax.rsqrt(aligned_total(parts, tok) / total_width + EPSILON)

        def one(m, carry):
            bias_v, cos_v, sin_v = bias_ref[m], cos_ref[m], sin_ref[m]
            inv = pick(inv_ref, m, each, tok, slice(None))
            own = pl.ds(pl.multiple_of(m * pack, pack), pack)
            for h in range(heads):
                at = slice(h * HD, (h + 1) * HD)
                q_raw = pick(raw_ref.at[0], m, each, tok, at)
                k_raw = pick(raw_ref.at[1], m, each, tok, at)
                q = turn(q_raw * inv[:, 0:1] * gain_ref[0:1, at], cos_v, sin_v).astype(BF)
                k = turn(k_raw * inv[:, 1:2] * gain_ref[1:2, at], cos_v, sin_v).astype(BF)
                queries_ref[own, at] = q
                keys_ref[own, at] = k
                scores = dot_t(q, k) * scale + bias_v
                weights = jnp.exp(scores - jnp.max(scores, axis=1, keepdims=True))
                probs = (weights / jnp.sum(weights, axis=1, keepdims=True)).astype(BF)
                context = dot(probs, pick(values_ref, m, each, tok, at)).astype(BF)
                place(context_ref, m, each, tok, at, context)
            return carry

        lax.fori_loop(0, micro, one, 0)
        write_blocks(dot(context_ref[...], out_weight_ref[...]), block_refs)

    return launch(
        order,
        kernel,
        [raw, values, qk_gain, out_weight, *tables, *squares],
        out_shape=[
            shape((rows, width), BF),
            shape((rows, width), BF),
            shape((rows, width), BF),
            shape((rows, 8), F32),
        ]
        + block_shapes(count, tok, model_width),
        in_specs=[VMEM] * (7 + count),
        out_specs=[VMEM] * (4 + count),
        cost_estimate=cost(
            4 * rows * pack * width + 2 * rows * width * model_width,
            2 * width * model_width + 14 * rows * width + 2 * rows * model_width,
            heads * rows * pack,
        ),
    )


def attend_back(order, d_attn_blocks, out_weight, queries, keys, values, raw, inv, tables, qk_gain):
    count = len(d_attn_blocks)
    micro = tables[0].shape[0]
    tok, model_width = d_attn_blocks[0].shape
    _, rows, width = raw.shape
    heads = width // HD
    each = tok // micro
    pack = rows // micro
    scale = HD ** (-0.5)

    def kernel(*refs):
        block_refs = refs[:count]
        (
            bias_ref,
            cos_ref,
            sin_ref,
            out_weight_ref,
            queries_ref,
            keys_ref,
            values_ref,
            raw_ref,
            inv_ref,
            gain_ref,
            d_attn_ref,
            d_norm_ref,
            d_values_ref,
            sums_ref,
            gain_sums_ref,
            d_context_ref,
            totals_ref,
        ) = refs[count:]
        join(block_refs, d_attn_ref)
        d_context_ref[...] = dot_t(d_attn_ref[...], out_weight_ref[...]).astype(BF)
        gain_sums_ref[...] = jnp.zeros((2, width), F32)

        def one(m, carry):
            bias_v, cos_v, sin_v = bias_ref[m], cos_ref[m], sin_ref[m]
            inv = pick(inv_ref, m, each, tok, slice(None))
            own = pl.ds(pl.multiple_of(m * pack, pack), pack)
            totals = [jnp.zeros((pack, HD), F32), jnp.zeros((pack, HD), F32)]
            for h in range(heads):
                at = slice(h * HD, (h + 1) * HD)
                q, k = queries_ref[own, at], keys_ref[own, at]
                v = pick(values_ref, m, each, tok, at)
                d_out = pick(d_context_ref, m, each, tok, at)
                scores = dot_t(q, k) * scale + bias_v
                weights = jnp.exp(scores - jnp.max(scores, axis=1, keepdims=True))
                probs = weights / jnp.sum(weights, axis=1, keepdims=True)
                d_probs = dot_t(d_out, v)
                delta = jnp.sum(d_probs * probs, axis=1, keepdims=True)
                d_scores = (probs * (d_probs - delta)).astype(BF)
                d_values = t_dot(probs.astype(BF), d_out).astype(BF)
                place(d_values_ref, m, each, tok, at, d_values)
                turned = (dot(d_scores, k) * scale, t_dot(d_scores, q) * scale)
                for n in range(2):
                    d_norm = turn_back(turned[n], cos_v, sin_v)
                    place(d_norm_ref.at[n], m, each, tok, at, d_norm)
                    field = pick(raw_ref.at[n], m, each, tok, at) * d_norm
                    totals[n] += field * gain_ref[n : n + 1, at]
                    gain_sums_ref[n : n + 1, at] += jnp.sum(
                        field * inv[:, n : n + 1], axis=0, keepdims=True
                    )
            for n in range(2):
                place(totals_ref.at[n], m, each, tok, slice(None), totals[n])
            return carry

        lax.fori_loop(0, micro, one, 0)
        for n in range(2):
            sums_ref[n : n + 1, :] = lane_sums(totals_ref[n])[:1]
        sums_ref[2:, :] = jnp.zeros((6, rows), F32)

    return launch(
        order,
        kernel,
        [*d_attn_blocks, *tables, out_weight, queries, keys, values, raw, inv, qk_gain],
        out_shape=[
            shape((rows, model_width), BF),
            shape((2, rows, width), F32),
            shape((rows, width), BF),
            shape((8, rows), F32),
            shape((2, width), F32),
        ],
        in_specs=[VMEM] * (10 + count),
        out_specs=[VMEM] * 5,
        scratch_shapes=[pltpu.VMEM((rows, width), BF), pltpu.VMEM((2, rows, HD), F32)],
        cost_estimate=cost(
            10 * rows * pack * width + 2 * rows * width * model_width,
            2 * width * model_width + 24 * rows * width + 2 * rows * model_width,
            heads * rows * pack,
        ),
    )


def project_back(order, d_norm, d_values, raw, inv, sums, qk_gain, qkv_weight):
    count = len(sums)
    _, rows, width = raw.shape
    tok = rows // count
    model_width = qkv_weight.shape[1]

    def kernel(d_norm_ref, d_values_ref, raw_ref, inv_ref, gain_ref, weight_ref, *refs):
        parts = refs[:count]
        d_projected_ref = refs[count]
        block_refs = refs[count + 1 : 2 * count + 1]
        total_ref = refs[2 * count + 1]
        step = pl.program_id(0)
        inv = inv_ref[...]

        @pl.when(step == 0)
        def _():
            d_projected_ref[...] = d_values_ref[...]

        @pl.when(step > 0)
        def _():
            shared = aligned_total([part[...] for part in parts], tok)
            first = step == 1
            r = jnp.where(first, inv[:, 0:1], inv[:, 1:2])
            s = jnp.where(first, shared[:, 0:1], shared[:, 1:2])
            gain = jnp.where(first, gain_ref[0:1, :], gain_ref[1:2, :])
            d_projected_ref[...] = (
                r * (d_norm_ref[...] * gain) - raw_ref[...] * (r * r * r * s / model_width)
            ).astype(BF)

        product = dot_t(d_projected_ref[...], weight_ref[...])

        total_ref[...] = jnp.where(step == 0, 0.0, total_ref[...]) + product

        @pl.when(step == 2)
        def _():
            write_blocks(total_ref[...], block_refs)

    def part_at(n):
        return lax.rem(n + 2, 3)

    field = pl.BlockSpec((None, rows, width), lambda n: (jnp.maximum(n - 1, 0), 0, 0))
    return launch(
        order,
        kernel,
        [d_norm, d_values, raw, inv, qk_gain, qkv_weight, *sums],
        out_shape=[shape((3, rows, width), BF)] + block_shapes(count, tok, model_width),
        grid=(3,),
        in_specs=[
            field,
            pl.BlockSpec((rows, width), lambda n: (0, 0)),
            field,
            pl.BlockSpec((rows, 8), lambda n: (0, 0)),
            pl.BlockSpec((2, width), lambda n: (0, 0)),
            pl.BlockSpec((None, model_width, width), lambda n: (part_at(n), 0, 0)),
        ]
        + [pl.BlockSpec((8, rows), lambda n: (0, 0))] * count,
        out_specs=[pl.BlockSpec((None, rows, width), lambda n: (part_at(n), 0, 0))]
        + [pl.BlockSpec((tok, model_width), lambda n: (0, 0))] * count,
        scratch_shapes=[pltpu.VMEM((rows, model_width), F32)],
        compiler_params=WHOLE,
        cost_estimate=cost(
            6 * rows * model_width * width, 6 * model_width * width + 22 * rows * width + 2 * rows * model_width
        ),
    )


def mlp_forward(order, hidden_blocks, gate_up_weight, down_weight):
    count = len(hidden_blocks)
    tok, model_width = hidden_blocks[0].shape
    rows = count * tok
    units = down_weight.shape[0]
    tile = min(512, units)
    last = units // tile - 1

    def kernel(*refs):
        gate_w_ref, up_w_ref, down_w_ref, gate_up_ref, swiglu_ref, hidden_ref = refs[
            count : count + 6
        ]
        block_refs = refs[count + 6 : 2 * count + 6]
        total_ref = refs[2 * count + 6]
        step = pl.program_id(0)

        @pl.when(step == 0)
        def _():
            join(refs[:count], hidden_ref)

        gate = dot(hidden_ref[...], gate_w_ref[...])
        up = dot(hidden_ref[...], up_w_ref[...])
        swiglu = (gate * jax.nn.sigmoid(gate) * up).astype(BF)
        gate_up_ref[0] = gate.astype(BF)
        gate_up_ref[1] = up.astype(BF)
        swiglu_ref[...] = swiglu
        product = dot(swiglu, down_w_ref[...])

        total_ref[...] = jnp.where(step == 0, 0.0, total_ref[...]) + product

        @pl.when(step == last)
        def _():
            write_blocks(total_ref[...], block_refs)

    field = pl.BlockSpec((rows, tile), lambda f: (0, f))
    return launch(
        order,
        kernel,
        [*hidden_blocks, gate_up_weight, gate_up_weight, down_weight],
        out_shape=[
            shape((2, rows, units), BF),
            shape((rows, units), BF),
            shape((rows, model_width), BF),
        ]
        + block_shapes(count, tok, model_width),
        grid=(units // tile,),
        in_specs=[pl.BlockSpec((tok, model_width), lambda f: (0, 0))] * count
        + [
            pl.BlockSpec((None, model_width, tile), lambda f: (0, 0, f)),
            pl.BlockSpec((None, model_width, tile), lambda f: (1, 0, f)),
            pl.BlockSpec((tile, model_width), lambda f: (f, 0)),
        ],
        out_specs=[pl.BlockSpec((2, rows, tile), lambda f: (0, 0, f)), field]
        + [pl.BlockSpec((rows, model_width), lambda f: (0, 0))]
        + [pl.BlockSpec((tok, model_width), lambda f: (0, 0))] * count,
        scratch_shapes=[pltpu.VMEM((rows, model_width), F32)],
        compiler_params=WHOLE,
        cost_estimate=cost(
            6 * rows * model_width * units,
            6 * model_width * units + 6 * rows * units + 8 * rows * model_width,
            rows * units,
        ),
    )


def unit_grads(gate, up, d_swiglu):
    sigmoid = jax.nn.sigmoid(gate)
    d_gate = d_swiglu * up * sigmoid * (1.0 + gate * (1.0 - sigmoid))
    return (d_gate.astype(BF), (d_swiglu * (gate * sigmoid)).astype(BF))


def mlp_back(order, d_mlp_blocks, gate_up, gate_up_weight, down_weight):
    count = len(d_mlp_blocks)
    tok, model_width = d_mlp_blocks[0].shape
    rows = count * tok
    units = down_weight.shape[0]
    tile = min(512, units)
    last = units // tile - 1

    def kernel(*refs):
        gate_up_ref, gate_w_ref, up_w_ref, down_w_ref, d_gate_up_ref, d_mlp_ref = refs[
            count : count + 6
        ]
        block_refs = refs[count + 6 : 2 * count + 6]
        total_ref = refs[2 * count + 6]
        step = pl.program_id(0)

        @pl.when(step == 0)
        def _():
            join(refs[:count], d_mlp_ref)

        d_swiglu = dot_t(d_mlp_ref[...], down_w_ref[...])
        d_gate, d_up = unit_grads(gate_up_ref[0].astype(F32), gate_up_ref[1].astype(F32), d_swiglu)
        d_gate_up_ref[0] = d_gate
        d_gate_up_ref[1] = d_up
        product = dot_t(d_gate, gate_w_ref[...]) + dot_t(d_up, up_w_ref[...])

        total_ref[...] = jnp.where(step == 0, 0.0, total_ref[...]) + product

        @pl.when(step == last)
        def _():
            write_blocks(total_ref[...], block_refs)

    field = pl.BlockSpec((2, rows, tile), lambda f: (0, 0, f))
    return launch(
        order,
        kernel,
        [*d_mlp_blocks, gate_up, gate_up_weight, gate_up_weight, down_weight],
        out_shape=[shape((2, rows, units), BF), shape((rows, model_width), BF)]
        + block_shapes(count, tok, model_width),
        grid=(units // tile,),
        in_specs=[pl.BlockSpec((tok, model_width), lambda f: (0, 0))] * count
        + [
            field,
            pl.BlockSpec((None, model_width, tile), lambda f: (0, 0, f)),
            pl.BlockSpec((None, model_width, tile), lambda f: (1, 0, f)),
            pl.BlockSpec((tile, model_width), lambda f: (f, 0)),
        ],
        out_specs=[field]
        + [pl.BlockSpec((rows, model_width), lambda f: (0, 0))]
        + [pl.BlockSpec((tok, model_width), lambda f: (0, 0))] * count,
        scratch_shapes=[pltpu.VMEM((rows, model_width), F32)],
        compiler_params=WHOLE,
        cost_estimate=cost(
            6 * rows * model_width * units,
            6 * model_width * units + 8 * rows * units + 8 * rows * model_width,
            rows * units,
        ),
    )


def mlp_units(order, hidden_blocks, d_mlp_blocks, gate_up_weight, down_weight):
    count = len(d_mlp_blocks)
    tok, model_width = d_mlp_blocks[0].shape
    rows = count * tok
    units = down_weight.shape[0]
    tile = min(256, units)

    def kernel(*refs):
        gate_w_ref, up_w_ref, down_w_ref = refs[2 * count : 2 * count + 3]
        d_gate_up_ref, swiglu_ref, d_mlp_ref, hidden_ref = refs[2 * count + 3 :]

        @pl.when(pl.program_id(0) == 0)
        def _():
            join(refs[:count], hidden_ref)
            join(refs[count : 2 * count], d_mlp_ref)

        gate = dot(hidden_ref[...], gate_w_ref[...])
        up = dot(hidden_ref[...], up_w_ref[...])
        d_gate, d_up = unit_grads(gate, up, dot_t(d_mlp_ref[...], down_w_ref[...]))
        swiglu_ref[...] = (gate * jax.nn.sigmoid(gate) * up).astype(BF)
        d_gate_up_ref[0] = d_gate
        d_gate_up_ref[1] = d_up

    return launch(
        order,
        kernel,
        [*hidden_blocks, *d_mlp_blocks, gate_up_weight, gate_up_weight, down_weight],
        out_shape=[
            shape((2, rows, units), BF),
            shape((rows, units), BF),
            shape((rows, model_width), BF),
            shape((rows, model_width), BF),
        ],
        grid=(units // tile,),
        in_specs=[pl.BlockSpec((tok, model_width), lambda f: (0, 0))] * (2 * count)
        + [
            pl.BlockSpec((None, model_width, tile), lambda f: (0, 0, f)),
            pl.BlockSpec((None, model_width, tile), lambda f: (1, 0, f)),
            pl.BlockSpec((tile, model_width), lambda f: (f, 0)),
        ],
        out_specs=[
            pl.BlockSpec((2, rows, tile), lambda f: (0, 0, f)),
            pl.BlockSpec((rows, tile), lambda f: (0, f)),
            pl.BlockSpec((rows, model_width), lambda f: (0, 0)),
            pl.BlockSpec((rows, model_width), lambda f: (0, 0)),
        ],
        compiler_params=WHOLE,
        cost_estimate=cost(
            6 * rows * model_width * units,
            6 * rows * model_width + 6 * model_width * units + 6 * rows * units,
            rows * units,
        ),
    )


def sum_parts(part_refs):
    total = part_refs[0][...].astype(F32)
    for part_ref in part_refs[1:]:
        total += part_ref[...].astype(F32)
    return total


def norm_back(field, gain, upstream):
    width = field.shape[1]
    inv = lax.rsqrt(jnp.sum(field * field, axis=1, keepdims=True) / width + EPSILON)
    weighted = upstream * gain
    shared = jnp.sum(field * weighted, axis=1, keepdims=True)
    gain_sum = jnp.sum(upstream * field * inv, axis=0, keepdims=True)
    return (inv * weighted - field * (inv * inv * inv * shared / width), gain_sum)


def by_rows(order, kernel, parts, rows, gains, outs, sums, work):
    tok, width = rows[0].shape
    block = min(32, tok)
    cut = pl.BlockSpec((block, width), lambda i: (i, 0))
    return launch(
        order,
        kernel,
        [*parts, *rows, gains],
        in_specs=[cut] * (len(parts) + len(rows)) + [pl.BlockSpec(gains.shape, lambda i: (0, 0))],
        out_shape=[shape((tok, width), kind) for kind in outs] + [shape((1, width), F32)] * sums,
        grid=(tok // block,),
        out_specs=[cut] * len(outs) + [pl.BlockSpec((1, width), lambda i: (0, 0))] * sums,
        compiler_params=WHOLE,
        cost_estimate=cost(work * tok * width, 24 * tok * width),
    )


def add_rows(sum_ref, value):
    @pl.when(pl.program_id(0) == 0)
    def _():
        sum_ref[...] = value

    @pl.when(pl.program_id(0) > 0)
    def _():
        sum_ref[...] += value


def after_attention(order, parts, x_rows, post_gain):
    count = len(parts)

    def kernel(*refs):
        x_ref, gain_ref, attn_ref, hidden_ref, rounded_ref = refs[count:]
        attn = sum_parts(refs[:count])
        inv = lax.rsqrt(jnp.sum(attn * attn, axis=1, keepdims=True) / attn.shape[1] + EPSILON)
        hidden = x_ref[...].astype(F32) + attn * inv * gain_ref[0:1, :]
        attn_ref[...] = attn
        hidden_ref[...] = hidden
        rounded_ref[...] = hidden.astype(BF)

    return by_rows(order, kernel, parts, [x_rows], post_gain, [F32, F32, BF], 0, 8)


def after_mlp(order, parts, hidden, grad_rows, post_gain):
    count = len(parts)

    def kernel(*refs):
        hidden_ref, grad_ref, gain_ref, out_ref, d_mlp_ref, gain_sum_ref = refs[count:]
        mlp = sum_parts(refs[:count])
        gain = gain_ref[1:2, :]
        inv = lax.rsqrt(jnp.sum(mlp * mlp, axis=1, keepdims=True) / mlp.shape[1] + EPSILON)
        out_ref[...] = hidden_ref[...] + mlp * inv * gain
        d_mlp, gain_sum = norm_back(mlp, gain, grad_ref[...].astype(F32))
        d_mlp_ref[...] = d_mlp.astype(BF)
        add_rows(gain_sum_ref, gain_sum)

    return by_rows(order, kernel, parts, [hidden, grad_rows], post_gain, [F32, BF], 1, 16)


def before_attention(order, parts, grad_rows, attn, post_gain):
    count = len(parts)

    def kernel(*refs):
        grad_ref, attn_ref, gain_ref, d_hidden_ref, d_attn_ref, gain_sum_ref = refs[count:]
        d_hidden = grad_ref[...].astype(F32) + sum_parts(refs[:count])
        d_hidden_ref[...] = d_hidden
        d_attn, gain_sum = norm_back(attn_ref[...], gain_ref[0:1, :], d_hidden)
        d_attn_ref[...] = d_attn.astype(BF)
        add_rows(gain_sum_ref, gain_sum)

    return by_rows(order, kernel, parts, [grad_rows, attn], post_gain, [F32, BF], 1, 16)


def send_order(top):
    def halves(codes, bit):
        if len(codes) == 1:
            return codes
        return halves([c for c in codes if c & bit], 2 * bit) + halves(
            [c for c in codes if not c & bit], 2 * bit
        )

    stages = []
    bit = 1
    while bit < top:
        stages.append((bit, [bit + c for c in halves(list(range(0, top, 2 * bit)), 2 * bit)]))
        bit *= 2
    return stages


def grad_rows_of(order, splits, sets):
    codes = [code for split in splits for code in split]
    blocks = len(codes)
    replicas = lax.axis_size("replica")
    picks = lax.axis_index("replica") ^ jnp.array(codes, jnp.int32)
    block = sets[0][0].shape[1] // replicas
    planes, _, units = sets[0][1].shape
    tile = min(512, units)
    tiles = units // tile
    width = planes * units
    depth = sum(rows for _, _, _, rows in sets)
    count = len(sets)
    kinds = [BF] * (len(splits) - 1) + [F32]

    def kernel(picks_ref, *refs):
        left_refs = refs[: count * blocks]
        right_refs = refs[count * blocks : count * blocks + count]
        out_refs = refs[count * blocks + count : count * blocks + count + len(splits)]
        turned_ref, right_ref = refs[count * blocks + count + len(splits) :]

        @pl.when(pl.program_id(0) == 0)
        def _():
            at = 0
            for k, (_, _, _, rows) in enumerate(sets):
                for b in range(blocks):
                    turned_ref[pl.ds(b * block, block), pl.ds(at, rows)] = left_refs[k * blocks + b][
                        ...
                    ].T
                at += rows

        at = 0
        for k, (_, _, _, rows) in enumerate(sets):
            right_ref[pl.ds(at, rows), :] = right_refs[k][...]
            at += rows
        first = 0
        for split, out_ref in zip(splits, out_refs):
            rows = len(split) * block
            out_ref[...] = dot(turned_ref[pl.ds(first, rows), :], right_ref[...]).astype(out_ref.dtype)
            first += rows

    in_specs = [
        pl.BlockSpec((rows, block), lambda f, picks_ref, group=group, b=b: (group, picks_ref[b]))
        for _, _, group, rows in sets
        for b in range(blocks)
    ] + [
        pl.BlockSpec(
            (None, rows, tile),
            lambda f, picks_ref, group=group: (lax.div(f, tiles), group, lax.rem(f, tiles)),
        )
        for _, _, group, rows in sets
    ]
    return launch(
        order,
        kernel,
        [picks]
        + [left for left, _, _, _ in sets for _ in range(blocks)]
        + [right for _, right, _, _ in sets],
        in_specs,
        lambda specs: pltpu.PrefetchScalarGridSpec(
            num_scalar_prefetch=1,
            grid=(planes * tiles,),
            in_specs=specs,
            out_specs=[
                pl.BlockSpec((len(split) * block, tile), lambda f, picks_ref: (0, f))
                for split in splits
            ],
            scratch_shapes=[
                pltpu.VMEM((blocks * block, depth), BF),
                pltpu.VMEM((depth, tile), BF),
            ],
        ),
        out_shape=[shape((len(split) * block, width), kind) for split, kind in zip(splits, kinds)],
        compiler_params=WHOLE,
        cost_estimate=cost(
            2 * depth * blocks * block * width,
            2 * depth * (blocks * block + width) + 2 * blocks * block * width,
        ),
    )


def add_parts(order, own, adds, column, width):
    rows = own.shape[0]
    tile = min(2048, width)
    tiles = width // tile

    def kernel(own_ref, *refs):
        refs[-1][...] = sum_parts([own_ref, *refs[:-1]]).astype(BF)

    return launch(
        order,
        kernel,
        [own] + [array for array, _, _ in adds],
        in_specs=[
            pl.BlockSpec((rows, tile), lambda f, group=group, at=at: (group, at * tiles + f))
            for group, at in [(0, column)] + [(group, at) for _, group, at in adds]
        ],
        out_shape=shape((rows, width), BF),
        grid=(tiles,),
        out_specs=pl.BlockSpec((rows, tile), lambda f: (0, f)),
        compiler_params=WHOLE,
        cost_estimate=cost(rows * width * len(adds), 2 * rows * width * (2 + len(adds))),
    )


class OwnersSum:
    def __init__(self, order, sets, top, pieces=1):
        self.stages = send_order(top)
        self.outs = grad_rows_of(order, [codes for _, codes in self.stages] + [[0]], sets)
        self.pieces = pieces
        self.at = 0
        self.received = [[] for _ in range(pieces)]
        bit, codes = self.stages[0]
        whole = exchange(self.outs[0], "replica", bit)
        for n in range(pieces):
            self.received[n].append((whole, [code ^ bit for code in codes], n))

    def adds(self, n, codes):
        return [
            (array, held.index(codes[0]) // len(codes), column)
            for array, held, column in self.received[n]
        ]

    def latest(self, n=0):
        return self.received[n][-1][0]

    def step(self, order):
        self.at += 1
        for n in range(self.pieces):
            self.send(order, n)

    def send(self, order, n):
        bit, codes = self.stages[self.at]
        own = self.outs[self.at]
        sent = add_parts(order, own, self.adds(n, codes), n, own.shape[1] // self.pieces)
        self.received[n].append((exchange(sent, "replica", bit), [code ^ bit for code in codes], 0))

    def finish(self, order, planes, turned):
        kept = self.outs[-1]
        rows, width = kept.shape
        units = width // planes
        span = width // self.pieces
        tile = min(512 if turned else 1024, units)
        tiles = units // tile
        grid = planes * tiles
        count = grid // self.pieces
        adds = [
            (array, group, column * count if array.shape[1] == width else -1, n)
            for n in range(self.pieces)
            for array, group, column in self.adds(n, [0])
        ]
        each = len(adds) // self.pieces

        def kernel(kept_ref, *refs):
            out_ref = refs[-1]
            for n in range(self.pieces):

                @pl.when(lax.div(pl.program_id(0), count) == n)
                def _():
                    total = kept_ref[...]
                    for add_ref in refs[n * each : (n + 1) * each]:
                        total += add_ref[...].astype(F32)
                    out_ref[...] = total.T if turned else total

        def add_spec(group, whole, n):
            def at(f):
                own = jnp.clip(f - n * count, 0, count - 1)
                return (group, own + n * count if whole else own)

            return pl.BlockSpec((rows, tile), at)

        if turned:
            out_shape = shape((units, rows), F32)
            out_spec = pl.BlockSpec((tile, rows), lambda f: (f, 0))
        else:
            out_shape = shape((planes, rows, units), F32)
            out_spec = pl.BlockSpec(
                (None, rows, tile), lambda f: (lax.div(f, tiles), 0, lax.rem(f, tiles))
            )
        return launch(
            order,
            kernel,
            [kept] + [array for array, _, _, _ in adds],
            in_specs=[pl.BlockSpec((rows, tile), lambda f: (0, f))]
            + [add_spec(group, first >= 0, n) for _, group, first, n in adds],
            out_shape=out_shape,
            grid=(grid,),
            out_specs=out_spec,
            compiler_params=WHOLE,
            cost_estimate=cost(rows * width * len(adds), rows * width * (8 + 2 * each)),
        )


def true_rows(tok_dev):
    size = lax.axis_size("fsdp")
    block = jnp.arange(size, dtype=jnp.int32) ^ lax.axis_index("fsdp")
    return (block[:, None] * tok_dev + jnp.arange(tok_dev, dtype=jnp.int32)[None, :]).reshape(-1)


def tree_tables(parent_row, length_row, places):
    segments = parent_row.shape[0]
    labels = jnp.arange(segments, dtype=jnp.int32)
    before = labels[:, None] >= labels[None, :]
    ends = jnp.sum(jnp.where(before, length_row[None, :], 0), axis=1)
    starts = ends - length_row
    segment_of = jnp.sum((places[:, None] >= ends[None, :]).astype(jnp.int32), axis=1)
    member = segment_of[:, None] == labels[None, :]
    reach = ((labels[:, None] == labels[None, :]) | (parent_row[:, None] == labels[None, :])).astype(F32)
    steps = 1
    while steps < segments - 1:
        reach = (jnp.dot(reach, reach) > 0.5).astype(F32)
        steps *= 2
    ancestry = reach > 0.5
    above = jnp.sum(jnp.where(ancestry, length_row[None, :], 0), axis=1) - length_row
    moved = jnp.sum(jnp.where(member, (above - starts)[None, :], 0), axis=1)
    position = (places + moved).astype(F32)
    member_f = member.astype(F32)
    near = jnp.dot(jnp.dot(member_f, reach), member_f.T) > 0.5
    visible = near & (places[None, :] <= places[:, None])
    freq = ROPE_BASE ** (-jnp.arange(0, HD, 2, dtype=F32) / HD)
    angle = position[:, None] * freq[None, :]
    cos_half, sin_half = jnp.cos(angle), jnp.sin(angle)
    return (
        jnp.where(visible, 0.0, -1e30).astype(F32),
        jnp.concatenate([cos_half, cos_half], axis=1),
        jnp.concatenate([-sin_half, sin_half], axis=1),
    )


def on_device(
    tokens,
    cotangent,
    parents,
    lengths,
    qkv_weight,
    out_weight,
    gate_up_weight,
    down_weight,
    qk_gain,
    post_gain,
):
    micro, tok_dev, model_width = tokens.shape
    local_width = qkv_weight.shape[2]
    size = lax.axis_size("fsdp")
    replicas = lax.axis_size("replica")
    tok = micro * tok_dev
    rows = tok * size
    far = replicas // 2
    places = true_rows(tok_dev)
    x_rows = tokens.reshape(tok, model_width)
    grad_rows = cotangent.reshape(tok, model_width)
    order = Order()
    x_blocks = gather_blocks(x_rows)
    tables = jax.vmap(tree_tables, in_axes=(0, 0, None))(parents[:, 0], lengths[:, 0], places)
    half = size // 2
    begun = project(order, x_blocks[:half], qkv_weight, 0, 2, [])
    order.clear()
    raw, values, squares, x_full = project(order, x_blocks[half:], qkv_weight, 1, 2, begun)
    context, queries, keys, inv, *attn_blocks = attend(
        order, raw, values, gather_blocks(squares), tables, qk_gain, out_weight
    )
    attn, hidden, hidden_b = after_attention(order, swap_blocks(attn_blocks), x_rows, post_gain)
    hidden_blocks = gather_blocks(hidden_b)
    far_hidden_blocks = gather_blocks(exchange(hidden_b, "replica", far))
    gate_up, swiglu, hidden_full, *mlp_blocks = mlp_forward(
        order, hidden_blocks, gate_up_weight, down_weight
    )
    order.extend(far_hidden_blocks[1:])
    mlp_blocks = gate(order, mlp_blocks)
    out_rows, d_mlp, mlp_gain_sum = after_mlp(
        order, swap_blocks(mlp_blocks), hidden, grad_rows, post_gain
    )
    d_mlp_blocks = gather_blocks(d_mlp)
    far_d_mlp_blocks = gather_blocks(exchange(d_mlp, "replica", far))
    d_gate_up, d_mlp_full, *d_hidden_blocks = mlp_back(
        order, d_mlp_blocks, gate_up, gate_up_weight, down_weight
    )
    d_hidden_parts = swap_blocks(d_hidden_blocks)
    fence(order, far_d_mlp_blocks[1:])
    far_d_gate_up, far_swiglu, far_d_mlp, far_hidden = mlp_units(
        order, far_hidden_blocks, far_d_mlp_blocks, gate_up_weight, down_weight
    )
    gate_up_sum = OwnersSum(
        order, [(hidden_full, d_gate_up, 0, rows), (far_hidden, far_d_gate_up, 0, rows)], far, 2
    )
    order.pace = 1000000
    d_hidden, d_attn, attn_gain_sum = before_attention(
        order, d_hidden_parts, grad_rows, attn, post_gain
    )
    d_attn_blocks = gather_blocks(d_attn)
    order.pace = 0.001
    gate_up_sum.at += 1
    gate_up_sum.send(order, 0)
    order.pace = 100
    down_sum = OwnersSum(
        order, [(d_mlp_full, swiglu[None], 0, rows), (far_d_mlp, far_swiglu[None], 0, rows)], far
    )
    order.pace = 0.001
    gate_up_sum.send(order, 1)
    order.pace = 100
    d_attn_full, d_norm, d_values, sums, qk_gain_sums = attend_back(
        order, d_attn_blocks, out_weight, queries, keys, values, raw, inv, tables, qk_gain
    )
    order.pace = 0.001
    sums_parts = gather_blocks(sums)
    down_sum.step(order)
    order.append(gate_up_sum.latest(0))
    d_projected, *input_blocks = project_back(
        order, d_norm, d_values, raw, inv, sums_parts, qk_gain, qkv_weight
    )
    input_parts = swap_blocks(input_blocks)
    [gain_rows] = gate(order, [jnp.concatenate([attn_gain_sum, mlp_gain_sum], axis=0)])
    me = lax.axis_index("fsdp")
    split = gain_rows.reshape(2, size, local_width)
    post_rows = lax.dynamic_index_in_dim(split, me, 1, keepdims=False)
    for flip in range(1, size):
        sent = lax.dynamic_index_in_dim(split, me ^ flip, 1, keepdims=False)
        post_rows = post_rows + exchange(sent, "fsdp", flip)
    gains = jnp.concatenate([qk_gain_sums, post_rows], axis=0)
    gains = gains + exchange(gains, "replica", 1)
    order.append(gate_up_sum.latest(1))
    qkv_sum = OwnersSum(order, [(x_full, d_projected, 0, rows)], replicas, 3)
    out_sum = OwnersSum(order, [(d_attn_full, context[None], 0, rows)], replicas)
    fence(order, [down_sum.latest(), *input_parts[1:], gains])
    qkv_sum.step(order)
    out_sum.step(order)
    gate_up_grad = gate_up_sum.finish(order, 2, False)
    qkv_sum.at += 1
    qkv_sum.send(order, 0)
    down_grad = down_sum.finish(order, 1, True)
    qkv_sum.send(order, 1)
    order.append(qkv_sum.latest(0))
    qkv_sum.send(order, 2)
    order.append(qkv_sum.latest(1))
    out_sum.step(order)
    [gains] = gate(order, [gains])
    flip = 2
    while flip < far:
        gains = gains + exchange(gains, "replica", flip)
        flip *= 2
    order.append(gains)
    qkv_grad = qkv_sum.finish(order, 3, False)
    out_grad = out_sum.finish(order, 1, True)
    [far_gains] = gate(order, [exchange(gains, "replica", far)])
    gains = gains + far_gains
    input_grad = d_hidden + sum(part.astype(F32) for part in input_parts)
    return (
        out_rows.reshape(micro, tok_dev, model_width),
        input_grad.reshape(micro, tok_dev, model_width),
        qkv_grad,
        out_grad,
        gate_up_grad,
        down_grad,
        gains[:2],
        gains[2:],
    )


def solution(mesh):
    in_specs = (
        P(None, ("replica", "fsdp"), None),
        P(None, ("replica", "fsdp"), None),
        P(None, "replica", None),
        P(None, "replica", None),
        P(None, None, "fsdp"),
        P("fsdp", None),
        P(None, None, "fsdp"),
        P("fsdp", None),
        P(None, "fsdp"),
        P(),
    )
    out_specs = (
        P(None, ("replica", "fsdp"), None),
        P(None, ("replica", "fsdp"), None),
        P(None, "replica", "fsdp"),
        P("fsdp", "replica"),
        P(None, "replica", "fsdp"),
        P("fsdp", "replica"),
        P(None, "fsdp"),
        P(None, "fsdp"),
    )
    return jax.shard_map(
        on_device, mesh=mesh, in_specs=in_specs, out_specs=out_specs, check_vma=False
    )
```

```python
import jax
import jax.numpy as jnp
from jax import lax
from jax.experimental import pallas as pl
from jax.experimental.pallas import tpu as pltpu
from jax.sharding import PartitionSpec as P

HD = 128


EPSILON = 1e-06
ROPE_BASE = 500000.0
BF = jnp.bfloat16
F32 = jnp.float32


def exchange(value, axis, flip):
    size = lax.axis_size(axis)
    return lax.ppermute(value, axis, [(i, i ^ flip) for i in range(size)])


def gather_blocks(rows):
    return [rows] + [exchange(rows, "fsdp", flip) for flip in range(1, lax.axis_size("fsdp"))]


def swap_blocks(blocks):
    return [blocks[0]] + [exchange(blocks[flip], "fsdp", flip) for flip in range(1, len(blocks))]


def cost(flops, moved, transcendentals=0):
    return (flops, moved, transcendentals)


class Order(list):
    pace = 0.001


def shape(dims, kind):
    return jax.ShapeDtypeStruct(dims, kind)


def dot(left, right):
    return jnp.dot(left, right, preferred_element_type=F32)


def dot_t(left, right):
    return lax.dot_general(left, right, (((1,), (1,)), ((), ())), preferred_element_type=F32)


def t_dot(left, right):
    return lax.dot_general(left, right, (((0,), (0,)), ((), ())), preferred_element_type=F32)


def lane_sums(field):
    ones = jnp.ones((8, field.shape[1]), F32)
    return lax.dot_general(
        ones,
        field,
        (((1,), (1,)), ((), ())),
        precision=lax.Precision.HIGHEST,
        preferred_element_type=F32,
    )


def join(block_refs, rows_ref):
    tok = block_refs[0].shape[0]
    for j, block_ref in enumerate(block_refs):
        rows_ref[pl.ds(j * tok, tok), :] = block_ref[...]


def write_blocks(rows, block_refs):
    tok = block_refs[0].shape[0]
    for j, block_ref in enumerate(block_refs):
        block_ref[...] = rows[j * tok : (j + 1) * tok].astype(block_ref.dtype)


def block_shapes(count, tok, width):
    return [shape((tok, width), F32)] + [shape((tok, width), BF)] * (count - 1)


def aligned_total(parts, tok):
    total = parts[0].T
    count = len(parts)
    for flip in range(1, count):
        column = parts[flip].T
        total = total + jnp.concatenate(
            [column[(j ^ flip) * tok : ((j ^ flip) + 1) * tok] for j in range(count)], axis=0
        )
    return total


def turn(field, cos_t, sin_t):
    return field * cos_t + pltpu.roll(field, HD // 2, 1) * sin_t


def turn_back(field, cos_t, sin_t):
    return field * cos_t - pltpu.roll(field, HD // 2, 1) * sin_t


VMEM = pl.BlockSpec(memory_space=pltpu.VMEM)
WHOLE = pltpu.CompilerParams(dimension_semantics=("arbitrary",))


def launch(
    order, kernel, args, in_specs, grid_spec=None, *, cost_estimate, pace=None, **settings
):
    waits = list(order)
    count = len(args)

    def body(*refs):
        kernel(*refs[:count], *refs[count + len(waits) :])

    flops, moved, transcendentals = [
        int(part * (order.pace if pace is None else pace)) for part in cost_estimate
    ]
    settings["cost_estimate"] = pl.CostEstimate(
        flops=flops, bytes_accessed=moved, transcendentals=transcendentals
    )
    specs = list(in_specs) + [pl.BlockSpec(memory_space=pl.ANY)] * len(waits)
    if grid_spec is None:
        settings["in_specs"] = specs
    else:
        settings["grid_spec"] = grid_spec(specs)
    settings["name"] = kernel.__qualname__.split(".<")[0].replace(".", "_")
    results = pl.pallas_call(body, **settings)(*args, *waits)
    order[:] = [results[0] if isinstance(results, (list, tuple)) else results]
    return results


def fence(order, arrays):
    order.extend(arrays)

    def kernel(out_ref):
        out_ref[...] = jnp.zeros((8, HD), F32)

    launch(
        order,
        kernel,
        [],
        in_specs=[],
        out_shape=shape((8, HD), F32),
        out_specs=VMEM,
        cost_estimate=cost(1 << 40, 1 << 30),
        pace=1,
    )


def gate(order, arrays):
    def kernel(*refs):
        pass

    held = pl.BlockSpec(memory_space=pl.ANY)
    return launch(
        order,
        kernel,
        arrays,
        in_specs=[held] * len(arrays),
        out_shape=[shape(array.shape, array.dtype) for array in arrays],
        out_specs=[held] * len(arrays),
        input_output_aliases={k: k for k in range(len(arrays))},
        cost_estimate=cost(0, 1000),
    )


def project(order, x_blocks, qkv_weight, part, parts, begun):
    count = len(x_blocks)
    tok, model_width = x_blocks[0].shape
    rows = count * tok
    width = qkv_weight.shape[2]

    def kernel(*refs):
        x_refs = refs[:count]
        weight_ref = refs[count]
        raw_ref, values_ref, squares_ref, x_ref = refs[-4:]
        step = pl.program_id(0)

        @pl.when(step == 0)
        def _():
            join(x_refs, x_ref)

        product = dot(x_ref[...], weight_ref[...])

        @pl.when(step < 2)
        def _():
            raw_ref[...] = product
            squares_ref[pl.ds(step, 1), :] = lane_sums(product * product)[:1]

        @pl.when(step == 2)
        def _():
            values_ref[...] = product.astype(BF)
            squares_ref[2:, :] = jnp.zeros((6, rows), F32)

    whole = pl.BlockSpec((tok, model_width), lambda n: (0, 0))
    return launch(
        order,
        kernel,
        [*x_blocks, qkv_weight, *begun],
        out_shape=[
            shape((2, parts * rows, width), F32),
            shape((parts * rows, width), BF),
            shape((8, parts * rows), F32),
            shape((parts * rows, model_width), BF),
        ],
        grid=(3,),
        in_specs=[whole] * count
        + [pl.BlockSpec((None, model_width, width), lambda n: (n, 0, 0))]
        + [pl.BlockSpec(memory_space=pl.ANY)] * len(begun),
        out_specs=[
            pl.BlockSpec((None, rows, width), lambda n: (jnp.minimum(n, 1), part, 0)),
            pl.BlockSpec((rows, width), lambda n: (part, 0)),
            pl.BlockSpec((8, rows), lambda n: (0, part)),
            pl.BlockSpec((rows, model_width), lambda n: (part, 0)),
        ],
        input_output_aliases={count + 1 + k: k for k in range(len(begun))},
        compiler_params=WHOLE,
        cost_estimate=cost(6 * rows * model_width * width, 6 * model_width * width + 8 * rows * width),
    )


def pick(ref, m, each, tok, at):
    return jnp.concatenate(
        [
            ref[pl.ds(pl.multiple_of(j * tok + m * each, each), each), at]
            for j in range(ref.shape[0] // tok)
        ],
        axis=0,
    )


def place(ref, m, each, tok, at, rows):
    for j in range(ref.shape[0] // tok):
        ref[pl.ds(pl.multiple_of(j * tok + m * each, each), each), at] = rows[
            j * each : (j + 1) * each
        ]


def attend(order, raw, values, squares, tables, qk_gain, out_weight):
    count = len(squares)
    micro = tables[0].shape[0]
    _, rows, width = raw.shape
    heads = width // HD
    tok = rows // count
    each = tok // micro
    pack = rows // micro
    model_width = out_weight.shape[1]
    total_width = model_width
    scale = HD ** (-0.5)

    def kernel(
        raw_ref, values_ref, gain_ref, out_weight_ref, bias_ref, cos_ref, sin_ref, *refs
    ):
        parts = [ref[...] for ref in refs[:count]]
        context_ref, queries_ref, keys_ref, inv_ref = refs[count : count + 4]
        block_refs = refs[count + 4 :]
        inv_ref[...] = lax.rsqrt(aligned_total(parts, tok) / total_width + EPSILON)

        def one(m, carry):
            bias_v, cos_v, sin_v = bias_ref[m], cos_ref[m], sin_ref[m]
            inv = pick(inv_ref, m, each, tok, slice(None))
            own = pl.ds(pl.multiple_of(m * pack, pack), pack)
            for h in range(heads):
                at = slice(h * HD, (h + 1) * HD)
                q_raw = pick(raw_ref.at[0], m, each, tok, at)
                k_raw = pick(raw_ref.at[1], m, each, tok, at)
                q = turn(q_raw * inv[:, 0:1] * gain_ref[0:1, at], cos_v, sin_v).astype(BF)
                k = turn(k_raw * inv[:, 1:2] * gain_ref[1:2, at], cos_v, sin_v).astype(BF)
                queries_ref[own, at] = q
                keys_ref[own, at] = k
                scores = dot_t(q, k) * scale + bias_v
                weights = jnp.exp(scores - jnp.max(scores, axis=1, keepdims=True))
                probs = (weights / jnp.sum(weights, axis=1, keepdims=True)).astype(BF)
                context = dot(probs, pick(values_ref, m, each, tok, at)).astype(BF)
                place(context_ref, m, each, tok, at, context)
            return carry

        lax.fori_loop(0, micro, one, 0)
        write_blocks(dot(context_ref[...], out_weight_ref[...]), block_refs)

    return launch(
        order,
        kernel,
        [raw, values, qk_gain, out_weight, *tables, *squares],
        out_shape=[
            shape((rows, width), BF),
            shape((rows, width), BF),
            shape((rows, width), BF),
            shape((rows, 8), F32),
        ]
        + block_shapes(count, tok, model_width),
        in_specs=[VMEM] * (7 + count),
        out_specs=[VMEM] * (4 + count),
        cost_estimate=cost(
            4 * rows * pack * width + 2 * rows * width * model_width,
            2 * width * model_width + 14 * rows * width + 2 * rows * model_width,
            heads * rows * pack,
        ),
    )


def attend_back(order, d_attn_blocks, out_weight, queries, keys, values, raw, inv, tables, qk_gain):
    count = len(d_attn_blocks)
    micro = tables[0].shape[0]
    tok, model_width = d_attn_blocks[0].shape
    _, rows, width = raw.shape
    heads = width // HD
    each = tok // micro
    pack = rows // micro
    scale = HD ** (-0.5)

    def kernel(*refs):
        block_refs = refs[:count]
        (
            bias_ref,
            cos_ref,
            sin_ref,
            out_weight_ref,
            queries_ref,
            keys_ref,
            values_ref,
            raw_ref,
            inv_ref,
            gain_ref,
            d_attn_ref,
            d_norm_ref,
            d_values_ref,
            sums_ref,
            gain_sums_ref,
            d_context_ref,
            totals_ref,
        ) = refs[count:]
        join(block_refs, d_attn_ref)
        d_context_ref[...] = dot_t(d_attn_ref[...], out_weight_ref[...]).astype(BF)
        gain_sums_ref[...] = jnp.zeros((2, width), F32)

        def one(m, carry):
            bias_v, cos_v, sin_v = bias_ref[m], cos_ref[m], sin_ref[m]
            inv = pick(inv_ref, m, each, tok, slice(None))
            own = pl.ds(pl.multiple_of(m * pack, pack), pack)
            totals = [jnp.zeros((pack, HD), F32), jnp.zeros((pack, HD), F32)]
            for h in range(heads):
                at = slice(h * HD, (h + 1) * HD)
                q, k = queries_ref[own, at], keys_ref[own, at]
                v = pick(values_ref, m, each, tok, at)
                d_out = pick(d_context_ref, m, each, tok, at)
                scores = dot_t(q, k) * scale + bias_v
                weights = jnp.exp(scores - jnp.max(scores, axis=1, keepdims=True))
                probs = weights / jnp.sum(weights, axis=1, keepdims=True)
                d_probs = dot_t(d_out, v)
                delta = jnp.sum(d_probs * probs, axis=1, keepdims=True)
                d_scores = (probs * (d_probs - delta)).astype(BF)
                d_values = t_dot(probs.astype(BF), d_out).astype(BF)
                place(d_values_ref, m, each, tok, at, d_values)
                turned = (dot(d_scores, k) * scale, t_dot(d_scores, q) * scale)
                for n in range(2):
                    d_norm = turn_back(turned[n], cos_v, sin_v)
                    place(d_norm_ref.at[n], m, each, tok, at, d_norm)
                    field = pick(raw_ref.at[n], m, each, tok, at) * d_norm
                    totals[n] += field * gain_ref[n : n + 1, at]
                    gain_sums_ref[n : n + 1, at] += jnp.sum(
                        field * inv[:, n : n + 1], axis=0, keepdims=True
                    )
            for n in range(2):
                place(totals_ref.at[n], m, each, tok, slice(None), totals[n])
            return carry

        lax.fori_loop(0, micro, one, 0)
        for n in range(2):
            sums_ref[n : n + 1, :] = lane_sums(totals_ref[n])[:1]
        sums_ref[2:, :] = jnp.zeros((6, rows), F32)

    return launch(
        order,
        kernel,
        [*d_attn_blocks, *tables, out_weight, queries, keys, values, raw, inv, qk_gain],
        out_shape=[
            shape((rows, model_width), BF),
            shape((2, rows, width), F32),
            shape((rows, width), BF),
            shape((8, rows), F32),
            shape((2, width), F32),
        ],
        in_specs=[VMEM] * (10 + count),
        out_specs=[VMEM] * 5,
        scratch_shapes=[pltpu.VMEM((rows, width), BF), pltpu.VMEM((2, rows, HD), F32)],
        cost_estimate=cost(
            10 * rows * pack * width + 2 * rows * width * model_width,
            2 * width * model_width + 24 * rows * width + 2 * rows * model_width,
            heads * rows * pack,
        ),
    )


def project_back(order, d_norm, d_values, raw, inv, sums, qk_gain, qkv_weight):
    count = len(sums)
    _, rows, width = raw.shape
    tok = rows // count
    model_width = qkv_weight.shape[1]

    def kernel(d_norm_ref, d_values_ref, raw_ref, inv_ref, gain_ref, weight_ref, *refs):
        parts = refs[:count]
        d_projected_ref = refs[count]
        block_refs = refs[count + 1 : 2 * count + 1]
        total_ref = refs[2 * count + 1]
        step = pl.program_id(0)
        inv = inv_ref[...]

        @pl.when(step == 0)
        def _():
            d_projected_ref[...] = d_values_ref[...]

        @pl.when(step > 0)
        def _():
            shared = aligned_total([part[...] for part in parts], tok)
            first = step == 1
            r = jnp.where(first, inv[:, 0:1], inv[:, 1:2])
            s = jnp.where(first, shared[:, 0:1], shared[:, 1:2])
            gain = jnp.where(first, gain_ref[0:1, :], gain_ref[1:2, :])
            d_projected_ref[...] = (
                r * (d_norm_ref[...] * gain) - raw_ref[...] * (r * r * r * s / model_width)
            ).astype(BF)

        product = dot_t(d_projected_ref[...], weight_ref[...])

        total_ref[...] = jnp.where(step == 0, 0.0, total_ref[...]) + product

        @pl.when(step == 2)
        def _():
            write_blocks(total_ref[...], block_refs)

    def part_at(n):
        return lax.rem(n + 2, 3)

    field = pl.BlockSpec((None, rows, width), lambda n: (jnp.maximum(n - 1, 0), 0, 0))
    return launch(
        order,
        kernel,
        [d_norm, d_values, raw, inv, qk_gain, qkv_weight, *sums],
        out_shape=[shape((3, rows, width), BF)] + block_shapes(count, tok, model_width),
        grid=(3,),
        in_specs=[
            field,
            pl.BlockSpec((rows, width), lambda n: (0, 0)),
            field,
            pl.BlockSpec((rows, 8), lambda n: (0, 0)),
            pl.BlockSpec((2, width), lambda n: (0, 0)),
            pl.BlockSpec((None, model_width, width), lambda n: (part_at(n), 0, 0)),
        ]
        + [pl.BlockSpec((8, rows), lambda n: (0, 0))] * count,
        out_specs=[pl.BlockSpec((None, rows, width), lambda n: (part_at(n), 0, 0))]
        + [pl.BlockSpec((tok, model_width), lambda n: (0, 0))] * count,
        scratch_shapes=[pltpu.VMEM((rows, model_width), F32)],
        compiler_params=WHOLE,
        cost_estimate=cost(
            6 * rows * model_width * width, 6 * model_width * width + 22 * rows * width + 2 * rows * model_width
        ),
    )


def mlp_forward(order, hidden_blocks, gate_up_weight, down_weight):
    count = len(hidden_blocks)
    tok, model_width = hidden_blocks[0].shape
    rows = count * tok
    units = down_weight.shape[0]
    tile = min(512, units)
    last = units // tile - 1

    def kernel(*refs):
        gate_w_ref, up_w_ref, down_w_ref, gate_up_ref, swiglu_ref, hidden_ref = refs[
            count : count + 6
        ]
        block_refs = refs[count + 6 : 2 * count + 6]
        total_ref = refs[2 * count + 6]
        step = pl.program_id(0)

        @pl.when(step == 0)
        def _():
            join(refs[:count], hidden_ref)

        gate = dot(hidden_ref[...], gate_w_ref[...])
        up = dot(hidden_ref[...], up_w_ref[...])
        swiglu = (gate * jax.nn.sigmoid(gate) * up).astype(BF)
        gate_up_ref[0] = gate.astype(BF)
        gate_up_ref[1] = up.astype(BF)
        swiglu_ref[...] = swiglu
        product = dot(swiglu, down_w_ref[...])

        total_ref[...] = jnp.where(step == 0, 0.0, total_ref[...]) + product

        @pl.when(step == last)
        def _():
            write_blocks(total_ref[...], block_refs)

    field = pl.BlockSpec((rows, tile), lambda f: (0, f))
    return launch(
        order,
        kernel,
        [*hidden_blocks, gate_up_weight, gate_up_weight, down_weight],
        out_shape=[
            shape((2, rows, units), BF),
            shape((rows, units), BF),
            shape((rows, model_width), BF),
        ]
        + block_shapes(count, tok, model_width),
        grid=(units // tile,),
        in_specs=[pl.BlockSpec((tok, model_width), lambda f: (0, 0))] * count
        + [
            pl.BlockSpec((None, model_width, tile), lambda f: (0, 0, f)),
            pl.BlockSpec((None, model_width, tile), lambda f: (1, 0, f)),
            pl.BlockSpec((tile, model_width), lambda f: (f, 0)),
        ],
        out_specs=[pl.BlockSpec((2, rows, tile), lambda f: (0, 0, f)), field]
        + [pl.BlockSpec((rows, model_width), lambda f: (0, 0))]
        + [pl.BlockSpec((tok, model_width), lambda f: (0, 0))] * count,
        scratch_shapes=[pltpu.VMEM((rows, model_width), F32)],
        compiler_params=WHOLE,
        cost_estimate=cost(
            6 * rows * model_width * units,
            6 * model_width * units + 6 * rows * units + 8 * rows * model_width,
            rows * units,
        ),
    )


def unit_grads(gate, up, d_swiglu):
    sigmoid = jax.nn.sigmoid(gate)
    d_gate = d_swiglu * up * sigmoid * (1.0 + gate * (1.0 - sigmoid))
    return (d_gate.astype(BF), (d_swiglu * (gate * sigmoid)).astype(BF))


def mlp_back(order, d_mlp_blocks, gate_up, gate_up_weight, down_weight):
    count = len(d_mlp_blocks)
    tok, model_width = d_mlp_blocks[0].shape
    rows = count * tok
    units = down_weight.shape[0]
    tile = min(512, units)
    last = units // tile - 1

    def kernel(*refs):
        gate_up_ref, gate_w_ref, up_w_ref, down_w_ref, d_gate_up_ref, d_mlp_ref = refs[
            count : count + 6
        ]
        block_refs = refs[count + 6 : 2 * count + 6]
        total_ref = refs[2 * count + 6]
        step = pl.program_id(0)

        @pl.when(step == 0)
        def _():
            join(refs[:count], d_mlp_ref)

        d_swiglu = dot_t(d_mlp_ref[...], down_w_ref[...])
        d_gate, d_up = unit_grads(gate_up_ref[0].astype(F32), gate_up_ref[1].astype(F32), d_swiglu)
        d_gate_up_ref[0] = d_gate
        d_gate_up_ref[1] = d_up
        product = dot_t(d_gate, gate_w_ref[...]) + dot_t(d_up, up_w_ref[...])

        total_ref[...] = jnp.where(step == 0, 0.0, total_ref[...]) + product

        @pl.when(step == last)
        def _():
            write_blocks(total_ref[...], block_refs)

    field = pl.BlockSpec((2, rows, tile), lambda f: (0, 0, f))
    return launch(
        order,
        kernel,
        [*d_mlp_blocks, gate_up, gate_up_weight, gate_up_weight, down_weight],
        out_shape=[shape((2, rows, units), BF), shape((rows, model_width), BF)]
        + block_shapes(count, tok, model_width),
        grid=(units // tile,),
        in_specs=[pl.BlockSpec((tok, model_width), lambda f: (0, 0))] * count
        + [
            field,
            pl.BlockSpec((None, model_width, tile), lambda f: (0, 0, f)),
            pl.BlockSpec((None, model_width, tile), lambda f: (1, 0, f)),
            pl.BlockSpec((tile, model_width), lambda f: (f, 0)),
        ],
        out_specs=[field]
        + [pl.BlockSpec((rows, model_width), lambda f: (0, 0))]
        + [pl.BlockSpec((tok, model_width), lambda f: (0, 0))] * count,
        scratch_shapes=[pltpu.VMEM((rows, model_width), F32)],
        compiler_params=WHOLE,
        cost_estimate=cost(
            6 * rows * model_width * units,
            6 * model_width * units + 8 * rows * units + 8 * rows * model_width,
            rows * units,
        ),
    )


def mlp_units(order, hidden_blocks, d_mlp_blocks, gate_up_weight, down_weight):
    count = len(d_mlp_blocks)
    tok, model_width = d_mlp_blocks[0].shape
    rows = count * tok
    units = down_weight.shape[0]
    tile = min(256, units)

    def kernel(*refs):
        gate_w_ref, up_w_ref, down_w_ref = refs[2 * count : 2 * count + 3]
        d_gate_up_ref, swiglu_ref, d_mlp_ref, hidden_ref = refs[2 * count + 3 :]

        @pl.when(pl.program_id(0) == 0)
        def _():
            join(refs[:count], hidden_ref)
            join(refs[count : 2 * count], d_mlp_ref)

        gate = dot(hidden_ref[...], gate_w_ref[...])
        up = dot(hidden_ref[...], up_w_ref[...])
        d_gate, d_up = unit_grads(gate, up, dot_t(d_mlp_ref[...], down_w_ref[...]))
        swiglu_ref[...] = (gate * jax.nn.sigmoid(gate) * up).astype(BF)
        d_gate_up_ref[0] = d_gate
        d_gate_up_ref[1] = d_up

    return launch(
        order,
        kernel,
        [*hidden_blocks, *d_mlp_blocks, gate_up_weight, gate_up_weight, down_weight],
        out_shape=[
            shape((2, rows, units), BF),
            shape((rows, units), BF),
            shape((rows, model_width), BF),
            shape((rows, model_width), BF),
        ],
        grid=(units // tile,),
        in_specs=[pl.BlockSpec((tok, model_width), lambda f: (0, 0))] * (2 * count)
        + [
            pl.BlockSpec((None, model_width, tile), lambda f: (0, 0, f)),
            pl.BlockSpec((None, model_width, tile), lambda f: (1, 0, f)),
            pl.BlockSpec((tile, model_width), lambda f: (f, 0)),
        ],
        out_specs=[
            pl.BlockSpec((2, rows, tile), lambda f: (0, 0, f)),
            pl.BlockSpec((rows, tile), lambda f: (0, f)),
            pl.BlockSpec((rows, model_width), lambda f: (0, 0)),
            pl.BlockSpec((rows, model_width), lambda f: (0, 0)),
        ],
        compiler_params=WHOLE,
        cost_estimate=cost(
            6 * rows * model_width * units,
            6 * rows * model_width + 6 * model_width * units + 6 * rows * units,
            rows * units,
        ),
    )


def sum_parts(part_refs):
    total = part_refs[0][...].astype(F32)
    for part_ref in part_refs[1:]:
        total += part_ref[...].astype(F32)
    return total


def norm_back(field, gain, upstream):
    width = field.shape[1]
    inv = lax.rsqrt(jnp.sum(field * field, axis=1, keepdims=True) / width + EPSILON)
    weighted = upstream * gain
    shared = jnp.sum(field * weighted, axis=1, keepdims=True)
    gain_sum = jnp.sum(upstream * field * inv, axis=0, keepdims=True)
    return (inv * weighted - field * (inv * inv * inv * shared / width), gain_sum)


def by_rows(order, kernel, parts, rows, gains, outs, sums, work):
    tok, width = rows[0].shape
    block = min(32, tok)
    cut = pl.BlockSpec((block, width), lambda i: (i, 0))
    return launch(
        order,
        kernel,
        [*parts, *rows, gains],
        in_specs=[cut] * (len(parts) + len(rows)) + [pl.BlockSpec(gains.shape, lambda i: (0, 0))],
        out_shape=[shape((tok, width), kind) for kind in outs] + [shape((1, width), F32)] * sums,
        grid=(tok // block,),
        out_specs=[cut] * len(outs) + [pl.BlockSpec((1, width), lambda i: (0, 0))] * sums,
        compiler_params=WHOLE,
        cost_estimate=cost(work * tok * width, 24 * tok * width),
    )


def add_rows(sum_ref, value):
    @pl.when(pl.program_id(0) == 0)
    def _():
        sum_ref[...] = value

    @pl.when(pl.program_id(0) > 0)
    def _():
        sum_ref[...] += value


def after_attention(order, parts, x_rows, post_gain):
    count = len(parts)

    def kernel(*refs):
        x_ref, gain_ref, attn_ref, hidden_ref, rounded_ref = refs[count:]
        attn = sum_parts(refs[:count])
        inv = lax.rsqrt(jnp.sum(attn * attn, axis=1, keepdims=True) / attn.shape[1] + EPSILON)
        hidden = x_ref[...].astype(F32) + attn * inv * gain_ref[0:1, :]
        attn_ref[...] = attn
        hidden_ref[...] = hidden
        rounded_ref[...] = hidden.astype(BF)

    return by_rows(order, kernel, parts, [x_rows], post_gain, [F32, F32, BF], 0, 8)


def after_mlp(order, parts, hidden, grad_rows, post_gain):
    count = len(parts)

    def kernel(*refs):
        hidden_ref, grad_ref, gain_ref, out_ref, d_mlp_ref, gain_sum_ref = refs[count:]
        mlp = sum_parts(refs[:count])
        gain = gain_ref[1:2, :]
        inv = lax.rsqrt(jnp.sum(mlp * mlp, axis=1, keepdims=True) / mlp.shape[1] + EPSILON)
        out_ref[...] = hidden_ref[...] + mlp * inv * gain
        d_mlp, gain_sum = norm_back(mlp, gain, grad_ref[...].astype(F32))
        d_mlp_ref[...] = d_mlp.astype(BF)
        add_rows(gain_sum_ref, gain_sum)

    return by_rows(order, kernel, parts, [hidden, grad_rows], post_gain, [F32, BF], 1, 16)


def before_attention(order, parts, grad_rows, attn, post_gain):
    count = len(parts)

    def kernel(*refs):
        grad_ref, attn_ref, gain_ref, d_hidden_ref, d_attn_ref, gain_sum_ref = refs[count:]
        d_hidden = grad_ref[...].astype(F32) + sum_parts(refs[:count])
        d_hidden_ref[...] = d_hidden
        d_attn, gain_sum = norm_back(attn_ref[...], gain_ref[0:1, :], d_hidden)
        d_attn_ref[...] = d_attn.astype(BF)
        add_rows(gain_sum_ref, gain_sum)

    return by_rows(order, kernel, parts, [grad_rows, attn], post_gain, [F32, BF], 1, 16)


def send_order(top):
    def halves(codes, bit):
        if len(codes) == 1:
            return codes
        return halves([c for c in codes if c & bit], 2 * bit) + halves(
            [c for c in codes if not c & bit], 2 * bit
        )

    stages = []
    bit = 1
    while bit < top:
        stages.append((bit, [bit + c for c in halves(list(range(0, top, 2 * bit)), 2 * bit)]))
        bit *= 2
    return stages


def grad_rows_of(order, splits, sets):
    codes = [code for split in splits for code in split]
    blocks = len(codes)
    replicas = lax.axis_size("replica")
    picks = lax.axis_index("replica") ^ jnp.array(codes, jnp.int32)
    block = sets[0][0].shape[1] // replicas
    planes, _, units = sets[0][1].shape
    tile = min(512, units)
    tiles = units // tile
    width = planes * units
    depth = sum(rows for _, _, _, rows in sets)
    count = len(sets)
    kinds = [BF] * (len(splits) - 1) + [F32]

    def kernel(picks_ref, *refs):
        left_refs = refs[: count * blocks]
        right_refs = refs[count * blocks : count * blocks + count]
        out_refs = refs[count * blocks + count : count * blocks + count + len(splits)]
        turned_ref, right_ref = refs[count * blocks + count + len(splits) :]

        @pl.when(pl.program_id(0) == 0)
        def _():
            at = 0
            for k, (_, _, _, rows) in enumerate(sets):
                for b in range(blocks):
                    turned_ref[pl.ds(b * block, block), pl.ds(at, rows)] = left_refs[k * blocks + b][
                        ...
                    ].T
                at += rows

        at = 0
        for k, (_, _, _, rows) in enumerate(sets):
            right_ref[pl.ds(at, rows), :] = right_refs[k][...]
            at += rows
        first = 0
        for split, out_ref in zip(splits, out_refs):
            rows = len(split) * block
            out_ref[...] = dot(turned_ref[pl.ds(first, rows), :], right_ref[...]).astype(out_ref.dtype)
            first += rows

    in_specs = [
        pl.BlockSpec((rows, block), lambda f, picks_ref, group=group, b=b: (group, picks_ref[b]))
        for _, _, group, rows in sets
        for b in range(blocks)
    ] + [
        pl.BlockSpec(
            (None, rows, tile),
            lambda f, picks_ref, group=group: (lax.div(f, tiles), group, lax.rem(f, tiles)),
        )
        for _, _, group, rows in sets
    ]
    return launch(
        order,
        kernel,
        [picks]
        + [left for left, _, _, _ in sets for _ in range(blocks)]
        + [right for _, right, _, _ in sets],
        in_specs,
        lambda specs: pltpu.PrefetchScalarGridSpec(
            num_scalar_prefetch=1,
            grid=(planes * tiles,),
            in_specs=specs,
            out_specs=[
                pl.BlockSpec((len(split) * block, tile), lambda f, picks_ref: (0, f))
                for split in splits
            ],
            scratch_shapes=[
                pltpu.VMEM((blocks * block, depth), BF),
                pltpu.VMEM((depth, tile), BF),
            ],
        ),
        out_shape=[shape((len(split) * block, width), kind) for split, kind in zip(splits, kinds)],
        compiler_params=WHOLE,
        cost_estimate=cost(
            2 * depth * blocks * block * width,
            2 * depth * (blocks * block + width) + 2 * blocks * block * width,
        ),
    )


def add_parts(order, own, adds, column, width):
    rows = own.shape[0]
    tile = min(2048, width)
    tiles = width // tile

    def kernel(own_ref, *refs):
        refs[-1][...] = sum_parts([own_ref, *refs[:-1]]).astype(BF)

    return launch(
        order,
        kernel,
        [own] + [array for array, _, _ in adds],
        in_specs=[
            pl.BlockSpec((rows, tile), lambda f, group=group, at=at: (group, at * tiles + f))
            for group, at in [(0, column)] + [(group, at) for _, group, at in adds]
        ],
        out_shape=shape((rows, width), BF),
        grid=(tiles,),
        out_specs=pl.BlockSpec((rows, tile), lambda f: (0, f)),
        compiler_params=WHOLE,
        cost_estimate=cost(rows * width * len(adds), 2 * rows * width * (2 + len(adds))),
    )


class OwnersSum:
    def __init__(self, order, sets, top, pieces=1):
        self.stages = send_order(top)
        self.outs = grad_rows_of(order, [codes for _, codes in self.stages] + [[0]], sets)
        self.pieces = pieces
        self.at = 0
        self.received = [[] for _ in range(pieces)]
        bit, codes = self.stages[0]
        whole = exchange(self.outs[0], "replica", bit)
        for n in range(pieces):
            self.received[n].append((whole, [code ^ bit for code in codes], n))

    def adds(self, n, codes):
        return [
            (array, held.index(codes[0]) // len(codes), column)
            for array, held, column in self.received[n]
        ]

    def latest(self, n=0):
        return self.received[n][-1][0]

    def step(self, order):
        self.at += 1
        for n in range(self.pieces):
            self.send(order, n)

    def send(self, order, n):
        bit, codes = self.stages[self.at]
        own = self.outs[self.at]
        sent = add_parts(order, own, self.adds(n, codes), n, own.shape[1] // self.pieces)
        self.received[n].append((exchange(sent, "replica", bit), [code ^ bit for code in codes], 0))

    def finish(self, order, planes, turned):
        kept = self.outs[-1]
        rows, width = kept.shape
        units = width // planes
        span = width // self.pieces
        tile = min(512 if turned else 1024, units)
        tiles = units // tile
        grid = planes * tiles
        count = grid // self.pieces
        adds = [
            (array, group, column * count if array.shape[1] == width else -1, n)
            for n in range(self.pieces)
            for array, group, column in self.adds(n, [0])
        ]
        each = len(adds) // self.pieces

        def kernel(kept_ref, *refs):
            out_ref = refs[-1]
            for n in range(self.pieces):

                @pl.when(lax.div(pl.program_id(0), count) == n)
                def _():
                    total = kept_ref[...]
                    for add_ref in refs[n * each : (n + 1) * each]:
                        total += add_ref[...].astype(F32)
                    out_ref[...] = total.T if turned else total

        def add_spec(group, whole, n):
            def at(f):
                own = jnp.clip(f - n * count, 0, count - 1)
                return (group, own + n * count if whole else own)

            return pl.BlockSpec((rows, tile), at)

        if turned:
            out_shape = shape((units, rows), F32)
            out_spec = pl.BlockSpec((tile, rows), lambda f: (f, 0))
        else:
            out_shape = shape((planes, rows, units), F32)
            out_spec = pl.BlockSpec(
                (None, rows, tile), lambda f: (lax.div(f, tiles), 0, lax.rem(f, tiles))
            )
        return launch(
            order,
            kernel,
            [kept] + [array for array, _, _, _ in adds],
            in_specs=[pl.BlockSpec((rows, tile), lambda f: (0, f))]
            + [add_spec(group, first >= 0, n) for _, group, first, n in adds],
            out_shape=out_shape,
            grid=(grid,),
            out_specs=out_spec,
            compiler_params=WHOLE,
            cost_estimate=cost(rows * width * len(adds), rows * width * (8 + 2 * each)),
        )


def true_rows(tok_dev):
    size = lax.axis_size("fsdp")
    block = jnp.arange(size, dtype=jnp.int32) ^ lax.axis_index("fsdp")
    return (block[:, None] * tok_dev + jnp.arange(tok_dev, dtype=jnp.int32)[None, :]).reshape(-1)


def tree_tables(parent_row, length_row, places):
    segments = parent_row.shape[0]
    labels = jnp.arange(segments, dtype=jnp.int32)
    before = labels[:, None] >= labels[None, :]
    ends = jnp.sum(jnp.where(before, length_row[None, :], 0), axis=1)
    starts = ends - length_row
    segment_of = jnp.sum((places[:, None] >= ends[None, :]).astype(jnp.int32), axis=1)
    member = segment_of[:, None] == labels[None, :]
    reach = ((labels[:, None] == labels[None, :]) | (parent_row[:, None] == labels[None, :])).astype(F32)
    steps = 1
    while steps < segments - 1:
        reach = (jnp.dot(reach, reach) > 0.5).astype(F32)
        steps *= 2
    ancestry = reach > 0.5
    above = jnp.sum(jnp.where(ancestry, length_row[None, :], 0), axis=1) - length_row
    moved = jnp.sum(jnp.where(member, (above - starts)[None, :], 0), axis=1)
    position = (places + moved).astype(F32)
    member_f = member.astype(F32)
    near = jnp.dot(jnp.dot(member_f, reach), member_f.T) > 0.5
    visible = near & (places[None, :] <= places[:, None])
    freq = ROPE_BASE ** (-jnp.arange(0, HD, 2, dtype=F32) / HD)
    angle = position[:, None] * freq[None, :]
    cos_half, sin_half = jnp.cos(angle), jnp.sin(angle)
    return (
        jnp.where(visible, 0.0, -1e30).astype(F32),
        jnp.concatenate([cos_half, cos_half], axis=1),
        jnp.concatenate([-sin_half, sin_half], axis=1),
    )


def on_device(
    tokens,
    cotangent,
    parents,
    lengths,
    qkv_weight,
    out_weight,
    gate_up_weight,
    down_weight,
    qk_gain,
    post_gain,
):
    micro, tok_dev, model_width = tokens.shape
    local_width = qkv_weight.shape[2]
    size = lax.axis_size("fsdp")
    replicas = lax.axis_size("replica")
    tok = micro * tok_dev
    rows = tok * size
    far = replicas // 2
    places = true_rows(tok_dev)
    x_rows = tokens.reshape(tok, model_width)
    grad_rows = cotangent.reshape(tok, model_width)
    order = Order()
    x_blocks = gather_blocks(x_rows)
    tables = jax.vmap(tree_tables, in_axes=(0, 0, None))(parents[:, 0], lengths[:, 0], places)
    half = size // 2
    begun = project(order, x_blocks[:half], qkv_weight, 0, 2, [])
    order.clear()
    raw, values, squares, x_full = project(order, x_blocks[half:], qkv_weight, 1, 2, begun)
    context, queries, keys, inv, *attn_blocks = attend(
        order, raw, values, gather_blocks(squares), tables, qk_gain, out_weight
    )
    attn, hidden, hidden_b = after_attention(order, swap_blocks(attn_blocks), x_rows, post_gain)
    hidden_blocks = gather_blocks(hidden_b)
    far_hidden_blocks = gather_blocks(exchange(hidden_b, "replica", far))
    gate_up, swiglu, hidden_full, *mlp_blocks = mlp_forward(
        order, hidden_blocks, gate_up_weight, down_weight
    )
    order.extend(far_hidden_blocks[1:])
    mlp_blocks = gate(order, mlp_blocks)
    out_rows, d_mlp, mlp_gain_sum = after_mlp(
        order, swap_blocks(mlp_blocks), hidden, grad_rows, post_gain
    )
    d_mlp_blocks = gather_blocks(d_mlp)
    far_d_mlp_blocks = gather_blocks(exchange(d_mlp, "replica", far))
    d_gate_up, d_mlp_full, *d_hidden_blocks = mlp_back(
        order, d_mlp_blocks, gate_up, gate_up_weight, down_weight
    )
    d_hidden_parts = swap_blocks(d_hidden_blocks)
    fence(order, far_d_mlp_blocks[1:])
    far_d_gate_up, far_swiglu, far_d_mlp, far_hidden = mlp_units(
        order, far_hidden_blocks, far_d_mlp_blocks, gate_up_weight, down_weight
    )
    gate_up_sum = OwnersSum(
        order, [(hidden_full, d_gate_up, 0, rows), (far_hidden, far_d_gate_up, 0, rows)], far, 2
    )
    order.pace = 1000000
    d_hidden, d_attn, attn_gain_sum = before_attention(
        order, d_hidden_parts, grad_rows, attn, post_gain
    )
    d_attn_blocks = gather_blocks(d_attn)
    order.pace = 0.001
    gate_up_sum.at += 1
    gate_up_sum.send(order, 0)
    order.pace = 100
    down_sum = OwnersSum(
        order, [(d_mlp_full, swiglu[None], 0, rows), (far_d_mlp, far_swiglu[None], 0, rows)], far
    )
    order.pace = 0.001
    gate_up_sum.send(order, 1)
    order.pace = 100
    d_attn_full, d_norm, d_values, sums, qk_gain_sums = attend_back(
        order, d_attn_blocks, out_weight, queries, keys, values, raw, inv, tables, qk_gain
    )
    order.pace = 0.001
    sums_parts = gather_blocks(sums)
    down_sum.step(order)
    order.append(gate_up_sum.latest(0))
    d_projected, *input_blocks = project_back(
        order, d_norm, d_values, raw, inv, sums_parts, qk_gain, qkv_weight
    )
    input_parts = swap_blocks(input_blocks)
    [gain_rows] = gate(order, [jnp.concatenate([attn_gain_sum, mlp_gain_sum], axis=0)])
    me = lax.axis_index("fsdp")
    split = gain_rows.reshape(2, size, local_width)
    post_rows = lax.dynamic_index_in_dim(split, me, 1, keepdims=False)
    for flip in range(1, size):
        sent = lax.dynamic_index_in_dim(split, me ^ flip, 1, keepdims=False)
        post_rows = post_rows + exchange(sent, "fsdp", flip)
    gains = jnp.concatenate([qk_gain_sums, post_rows], axis=0)
    gains = gains + exchange(gains, "replica", 1)
    order.append(gate_up_sum.latest(1))
    qkv_sum = OwnersSum(order, [(x_full, d_projected, 0, rows)], replicas, 3)
    out_sum = OwnersSum(order, [(d_attn_full, context[None], 0, rows)], replicas)
    fence(order, [down_sum.latest(), gains])
    qkv_sum.step(order)
    out_sum.step(order)
    order.extend(input_parts[1:])
    [gains] = gate(order, [gains])
    flip = 2
    while flip < far:
        gains = gains + exchange(gains, "replica", flip)
        flip *= 2
    gate_up_grad = gate_up_sum.finish(order, 2, False)
    qkv_sum.at += 1
    qkv_sum.send(order, 0)
    down_grad = down_sum.finish(order, 1, True)
    qkv_sum.send(order, 1)
    order.append(qkv_sum.latest(0))
    qkv_sum.send(order, 2)
    order.append(qkv_sum.latest(1))
    order.append(gains)
    out_sum.step(order)
    qkv_grad = qkv_sum.finish(order, 3, False)
    out_grad = out_sum.finish(order, 1, True)
    [far_gains] = gate(order, [exchange(gains, "replica", far)])
    gains = gains + far_gains
    input_grad = d_hidden + sum(part.astype(F32) for part in input_parts)
    return (
        out_rows.reshape(micro, tok_dev, model_width),
        input_grad.reshape(micro, tok_dev, model_width),
        qkv_grad,
        out_grad,
        gate_up_grad,
        down_grad,
        gains[:2],
        gains[2:],
    )


def solution(mesh):
    in_specs = (
        P(None, ("replica", "fsdp"), None),
        P(None, ("replica", "fsdp"), None),
        P(None, "replica", None),
        P(None, "replica", None),
        P(None, None, "fsdp"),
        P("fsdp", None),
        P(None, None, "fsdp"),
        P("fsdp", None),
        P(None, "fsdp"),
        P(),
    )
    out_specs = (
        P(None, ("replica", "fsdp"), None),
        P(None, ("replica", "fsdp"), None),
        P(None, "replica", "fsdp"),
        P("fsdp", "replica"),
        P(None, "replica", "fsdp"),
        P("fsdp", "replica"),
        P(None, "fsdp"),
        P(None, "fsdp"),
    )
    return jax.shard_map(
        on_device, mesh=mesh, in_specs=in_specs, out_specs=out_specs, check_vma=False
    )
```
